32 devices in a mesh: stream: 2 (over core), dp: 16 (over z, y, x).
Axes of the slice: x: 2, y: 2, z: 4, core: 2. Of those that a mesh axis runs over, the one named last changes fastest.
Arguments:
- layer_input: bfloat16 [2, 16384, 768], P('stream', 'dp'), may hold values from -6 to 6
- pair_group: int32 [256], P('dp'), may hold values from 0 to 108, as said below
- query_weight: bfloat16 [768, 768], replicated, may hold values from -0.21875 to 0.21875
- query_bias: float32 [768], replicated, may hold values from -4 to 4
- key_weight: bfloat16 [768, 768], replicated, may hold values from -0.21875 to 0.21875
- value_weight: bfloat16 [768, 768], replicated, may hold values from -0.21875 to 0.21875
- value_bias: float32 [768], replicated, may hold values from -4 to 4
- out_weight: bfloat16 [768, 768], replicated, may hold values from -1 to 1
- out_bias: float32 [768], replicated, may hold values from -4 to 4
- mixer_gain: float32 [768], replicated, may hold values from 0.1 to 1.9
- mixer_shift: float32 [768], replicated, may hold values from -4 to 4
- up_weight: bfloat16 [768, 3072], replicated, may hold values from -0.21875 to 0.21875
- up_bias: float32 [3072], replicated, may hold values from -4 to 4
- down_weight: bfloat16 [3072, 768], replicated, may hold values from -0.109375 to 0.109375
- down_bias: float32 [768], replicated, may hold values from -4 to 4
- final_gain: float32 [768], replicated, may hold values from 0.1 to 1.9
- final_shift: float32 [768], replicated, may hold values from -4 to 4
- upstream: bfloat16 [2, 16384, 768], P('stream', 'dp'), may hold values from -0.75 to 0.75
Outputs:
- layer_output: bfloat16 [2, 16384, 768], P('stream', 'dp')
- input_grad: float32 [2, 16384, 768], P('stream', 'dp')
- total_loss: float32 [2, 256], P('stream', 'dp')
- query_weight_grad: float32 [768, 768], replicated
- query_bias_grad: float32 [768], replicated
- key_weight_grad: float32 [768, 768], replicated
- value_weight_grad: float32 [768, 768], replicated
- value_bias_grad: float32 [768], replicated
- out_weight_grad: float32 [768, 768], replicated
- out_bias_grad: float32 [768], replicated
- mixer_gain_grad: float32 [768], replicated
- mixer_shift_grad: float32 [768], replicated
- up_weight_grad: float32 [768, 3072], replicated
- up_bias_grad: float32 [3072], replicated
- down_weight_grad: float32 [3072, 768], replicated
- down_bias_grad: float32 [768], replicated
- final_gain_grad: float32 [768], replicated
- final_shift_grad: float32 [768], replicated
The draws below stay inside these ranges and needn't reach their ends.
Inputs may be any that keep to these rules, and one draw needn't show every extreme that they name: `pair_group`: every one of the 109 ids names 2 or more pairs; the first and the last pair have the same id.
All inputs are finite; a program needn't handle non-finite values.
Results may differ from the reference program's by a relative error of at most 0.014.
Values may be sent and summed in bfloat16 or wider, within the bound.
No kernel may reach another device: no remote copies, remote signals or barrier semaphores. Data moves between devices by JAX's collectives and lax.ppermute only.
A program may use at most 256 MiB of HBM per device.

```python
import math
import jax
import jax.numpy as jnp
from jax import lax

D = 768
HEADS = 12
HD = 64
FF = 3072
SEQ_LEN = 64
GROUPS = 109
HALVES = 2
PAIRS = 256
ROWS = 16384


def draw_pair_group(key, part):
    first_key = jax.random.fold_in(key, 11)
    second_key = jax.random.fold_in(key, 12)
    third_key = jax.random.fold_in(key, 13)
    fourth_key = jax.random.fold_in(key, 14)
    spare = PAIRS - 2 * GROUPS
    left_draw = jax.random.randint(first_key, (spare,), 0, GROUPS)
    right_draw = jax.random.randint(second_key, (spare,), 0, GROUPS)
    skewed = left_draw * right_draw // GROUPS
    order = jax.random.permutation(third_key, GROUPS)
    base_ids = jnp.arange(2 * GROUPS, dtype=jnp.int32) // 2
    mapped = order[jnp.concatenate([base_ids, skewed.astype(jnp.int32)])].astype(jnp.int32)
    middle = mapped[2:][jax.random.permutation(fourth_key, PAIRS - 2)]
    return jnp.concatenate([mapped[0:1], middle, mapped[1:2]]).astype(jnp.int32)


def shard_levels(stream_key, extent, pieces, smallest, top_value):
    def one(position, parts):
        steps = jax.random.uniform(jax.random.fold_in(jax.random.fold_in(stream_key, 6), position), (parts,), jnp.float32, smallest / len(pieces), top_value / len(pieces))
        return jnp.repeat(jnp.exp(steps), extent[position] // parts).reshape((-1,) + (1,) * (len(extent) - position - 1))

    level = one(*pieces[0])
    for cut in pieces[1:]:
        level = level * one(*cut)
    return level


def noise(own_key, dims, scale, limit, split=(), held_as=jnp.bfloat16):
    drawn = jax.random.normal(own_key, dims, jnp.float32) * scale
    if len(split) > 0:
        drawn = shard_levels(own_key, dims, split, -0.22, 0.18) * drawn
    return jnp.clip(drawn, min=-limit, max=limit).astype(held_as)


def setup_inputs(seed: int = 0) -> dict:
    seeds = jax.random.split(jax.random.key(seed), 19)
    layer_input = noise(seeds[0], (HALVES, ROWS, D), 1.0, 6.0, ((0, 2), (1, 16)))
    pair_group = draw_pair_group(jax.random.fold_in(seeds[18], 71), 0)
    query_weight = noise(seeds[2], (D, D), D ** -0.5, 0.21875)
    query_bias = noise(seeds[3], (D,), 0.3, 4.0, (), jnp.float32)
    key_weight = noise(seeds[4], (D, D), D ** -0.5, 0.21875)
    value_weight = noise(seeds[5], (D, D), D ** -0.5, 0.21875)
    value_bias = noise(seeds[6], (D,), 0.3, 4.0, (), jnp.float32)
    out_weight = noise(seeds[7], (D, D), 32 ** -0.5, 1.0)
    out_bias = noise(seeds[8], (D,), 0.3, 4.0, (), jnp.float32)
    mixer_gain = jnp.clip(1.0 + 0.18 * jax.random.normal(seeds[9], (D,), jnp.float32), 0.1, 1.9)
    mixer_shift = noise(seeds[10], (D,), 0.3, 4.0, (), jnp.float32)
    up_weight = noise(seeds[11], (D, FF), D ** -0.5, 0.21875)
    up_bias = noise(seeds[12], (FF,), 0.3, 4.0, (), jnp.float32)
    down_weight = noise(seeds[13], (FF, D), FF ** -0.5, 0.109375)
    down_bias = noise(seeds[14], (D,), 0.3, 4.0, (), jnp.float32)
    final_gain = jnp.clip(1.0 + 0.18 * jax.random.normal(seeds[15], (D,), jnp.float32), 0.1, 1.9)
    final_shift = noise(seeds[16], (D,), 0.3, 4.0, (), jnp.float32)
    upstream = noise(seeds[17], (HALVES, ROWS, D), 0.05, 0.75, ((0, 2), (1, 16)))
    return {"layer_input": layer_input, "pair_group": pair_group, "query_weight": query_weight, "query_bias": query_bias, "key_weight": key_weight, "value_weight": value_weight, "value_bias": value_bias, "out_weight": out_weight, "out_bias": out_bias, "mixer_gain": mixer_gain, "mixer_shift": mixer_shift, "up_weight": up_weight, "up_bias": up_bias, "down_weight": down_weight, "down_bias": down_bias, "final_gain": final_gain, "final_shift": final_shift, "upstream": upstream}


@jax.custom_vjp
def low(v):
    return lax.optimization_barrier(v.astype(jnp.bfloat16)).astype(jnp.float32)

@jax.custom_vjp
def low_back(v):
    return v

def low_keep(v):
    return (low(v), None)

def low_pass(kept, grad):
    return (grad,)

def back_keep(v):
    return (v, None)

def back_low(kept, grad):
    return (low(grad),)
low.defvjp(low_keep, low_pass)
low_back.defvjp(back_keep, back_low)
MARGIN = 0.3
LOGIT_SCALE = 30.0
NORM_EPS = 1e-12
UNIT_EPS = 1e-06
highest = lax.Precision.HIGHEST

def matmul(left, right):
    return jnp.dot(left, right, precision=highest, preferred_element_type=jnp.float32)

def layer_norm(values, gain, shift):
    centred = values - lax.optimization_barrier(jnp.mean(values, axis=-1, keepdims=True))
    inv_std = lax.rsqrt(lax.optimization_barrier(jnp.mean(centred * centred, axis=-1, keepdims=True)) + NORM_EPS)
    return centred * inv_std * gain + shift

def encode(params, seq_block):
    query_weight, query_bias, key_weight, value_weight, value_bias, out_weight, out_bias, mixer_gain, mixer_shift, up_weight, up_bias, down_weight, down_bias, final_gain, final_shift = params
    seq_count = seq_block.shape[0]
    token_rows = seq_block.reshape(-1, D)
    query_rows = low_back(low(matmul(token_rows, query_weight) + query_bias))
    key_rows = low_back(low(matmul(token_rows, key_weight)))
    value_rows = low_back(low(matmul(token_rows, value_weight) + value_bias))
    query_heads = query_rows.reshape(seq_count, SEQ_LEN, HEADS, HD)
    key_heads = key_rows.reshape(seq_count, SEQ_LEN, HEADS, HD)
    value_heads = value_rows.reshape(seq_count, SEQ_LEN, HEADS, HD)
    scores = low_back(jnp.einsum('bqhd,bkhd->bhqk', query_heads, key_heads, precision=highest) / math.sqrt(HD))
    attn_probs = low(jax.nn.softmax(scores, axis=-1))
    context = low_back(low(jnp.einsum('bhqk,bkhd->bqhd', attn_probs, value_heads, precision=highest)))
    context = context.reshape(-1, D)
    attended = low_back(matmul(context, out_weight) + out_bias)
    normed_one = layer_norm(token_rows + attended, mixer_gain, mixer_shift)
    hidden_pre = low_back(matmul(low(normed_one), up_weight) + up_bias)
    activated = low(jax.nn.gelu(hidden_pre, approximate=False))
    branch = low_back(matmul(activated, down_weight) + down_bias)
    normed_two = layer_norm(normed_one + branch, final_gain, final_shift)
    return normed_two.reshape(seq_count, SEQ_LEN, D)

def side_loss(logits, same_group):
    log_total = jax.nn.logsumexp(logits, axis=1, where=same_group)
    return log_total - jnp.diagonal(logits)

def contrast(source_units, target_units, pair_group):
    sim_scores = LOGIT_SCALE * matmul(source_units, target_units.T)
    same_group = pair_group[:, None] == pair_group[None, :]
    group_range = jnp.arange(GROUPS).astype(jnp.int32)
    counts = lax.optimization_barrier(jnp.sum((pair_group[:, None] == group_range[None, :]).astype(jnp.float32), axis=0))
    row_weight = PAIRS / GROUPS / counts[pair_group]
    eye_mask = jnp.eye(PAIRS, dtype=jnp.float32)
    logits = sim_scores - LOGIT_SCALE * MARGIN * eye_mask
    forward_loss = side_loss(logits, same_group)
    backward_loss = side_loss(logits.T, same_group)
    return jnp.stack([row_weight * forward_loss, row_weight * backward_loss])

def objective(params, halves, upstream_f, pair_group):
    seqs = halves.reshape(HALVES * PAIRS, SEQ_LEN, D)
    block_seqs = math.gcd(HALVES * PAIRS, max(1, 4096 // SEQ_LEN))
    blocked = seqs.reshape(-1, block_seqs, SEQ_LEN, D)
    outputs = lax.map(jax.checkpoint(lambda seq_block: encode(params, seq_block)), blocked)
    outputs = outputs.reshape(HALVES, PAIRS, SEQ_LEN, D)
    lead_rows = outputs[:, :, 0, :]
    unit_rows = low(lead_rows * lax.rsqrt(lax.optimization_barrier(jnp.sum(lead_rows * lead_rows, axis=-1, keepdims=True)) + UNIT_EPS))
    loss_rows = contrast(unit_rows[0], unit_rows[1], pair_group)
    outputs = outputs.reshape(HALVES, ROWS, D)
    return (jnp.sum(outputs * upstream_f) + jnp.sum(loss_rows), (outputs, loss_rows))

def reference(layer_input, pair_group, query_weight, query_bias, key_weight, value_weight, value_bias, out_weight, out_bias, mixer_gain, mixer_shift, up_weight, up_bias, down_weight, down_bias, final_gain, final_shift, upstream):
    params = tuple((piece.astype(jnp.float32) for piece in (query_weight, query_bias, key_weight, value_weight, value_bias, out_weight, out_bias, mixer_gain, mixer_shift, up_weight, up_bias, down_weight, down_bias, final_gain, final_shift)))
    halves = layer_input.astype(jnp.float32)
    upstream_f = upstream.astype(jnp.float32)

    def scalar_fn(param_tuple, halves_in):
        return objective(param_tuple, halves_in, upstream_f, pair_group)
    total, pullback, aux = jax.vjp(scalar_fn, params, halves, has_aux=True)
    outputs, loss_rows = aux
    grad_params, grad_input = pullback(jnp.ones_like(total))
    return (outputs.astype(jnp.bfloat16), grad_input, loss_rows, grad_params[0], grad_params[1], grad_params[2], grad_params[3], grad_params[4], grad_params[5], grad_params[6], grad_params[7], grad_params[8], grad_params[9], grad_params[10], grad_params[11], grad_params[12], grad_params[13], grad_params[14])
```

```python
import math

import jax
import jax.numpy as jnp
from jax import lax
from jax.sharding import PartitionSpec as P

D = 768
HEADS = 12
HD = 64
GROUPS = 109


MARGIN = 0.3
LOGIT_SCALE = 30.0
NORM_EPS = 1e-12
UNIT_EPS = 1e-06
highest = lax.Precision.HIGHEST


def norm_forward(values, gain, shift):
    centred = values - jnp.mean(values, axis=-1, keepdims=True)
    inv_std = lax.rsqrt(jnp.mean(centred * centred, axis=-1, keepdims=True) + NORM_EPS)
    normed_hat = centred * inv_std
    return (normed_hat * gain + shift, normed_hat, inv_std)


def norm_backward(grad_out, normed_hat, inv_std, gain):
    grad_hat = grad_out * gain
    mean_grad = jnp.mean(grad_hat, axis=-1, keepdims=True)
    mean_cross = jnp.mean(grad_hat * normed_hat, axis=-1, keepdims=True)
    grad_in = inv_std * (grad_hat - mean_grad - normed_hat * mean_cross)
    return (grad_in, jnp.sum(grad_out * normed_hat, axis=0), jnp.sum(grad_out, axis=0))


def gelu_slope(values):
    normal_cdf = 0.5 * (1.0 + lax.erf(values * (1.0 / math.sqrt(2.0))))
    return normal_cdf + values * jnp.exp(-0.5 * values * values) * (1.0 / math.sqrt(2.0 * math.pi))


def to_heads(matrix, key_span):
    return matrix.reshape(-1, key_span, HEADS, HD)


def attend_scores(query_heads, key_heads, key_mask, factor):
    raw_scores = (
        jnp.einsum("bqhd,bkhd->bhqk", query_heads, key_heads, preferred_element_type=jnp.float32)
        * factor
    )
    return jnp.where(key_mask, raw_scores, -jnp.inf)


def outer_sum(left, right):
    return jnp.einsum("ri,rj->ij", left, right, preferred_element_type=jnp.float32)


def back_project(grad_rows, weight):
    return jnp.einsum("re,de->rd", grad_rows, weight, preferred_element_type=jnp.float32)


def chip_partner(bit_zero, bit_one):
    chips = lax.axis_size("dp")
    return [
        (half * chips + chip, half * chips + (chip ^ (bit_zero if half == 0 else bit_one)))
        for half in range(2)
        for chip in range(chips)
    ]


def core_partner():
    chips = lax.axis_size("dp")
    return [(half * chips + chip, (1 - half) * chips + chip) for half in range(2) for chip in range(chips)]


def swap(piece, pairs):
    return lax.ppermute(piece, ("stream", "dp"), pairs)


def add_low(left, right):
    return (left.astype(jnp.float32) + right.astype(jnp.float32)).astype(jnp.bfloat16)


def all_sum(blocks):
    half = lax.axis_index("stream")
    chip = lax.axis_index("dp")
    low, high = chip & 1, (chip >> 1) & 1
    first = jnp.where(half == 0, low, high)
    second = jnp.where(half == 0, high, low)
    steps = [(half, core_partner()), (first, chip_partner(1, 2)), (second, chip_partner(2, 1))]
    for mine, pairs in steps:
        take = lambda index: lax.dynamic_index_in_dim(blocks, index, 0, keepdims=False)
        blocks = add_low(take(mine), swap(take(1 - mine), pairs))
    bits = [1 << k for k in range(2, lax.axis_size("dp").bit_length() - 1)]
    for bit_zero, bit_one in zip(bits, bits[::-1], strict=True):
        blocks = add_low(blocks, swap(blocks, chip_partner(bit_zero, bit_one)))
    for mine, pairs in steps[::-1]:
        other = swap(blocks, pairs)
        blocks = jnp.where(mine == 0, jnp.stack([blocks, other]), jnp.stack([other, blocks]))
    return blocks


def gather_rows(rows):
    chips = lax.axis_size("dp")
    bit = 1
    while bit < chips:
        rows = jnp.concatenate([rows, swap(rows, chip_partner(bit, bit))])
        bit *= 2
    return rows, swap(rows, core_partner())


def feed_forward(normed_low, up_weight, up_bias, down_weight, down_bias):
    hidden_pre = jnp.dot(normed_low, up_weight, preferred_element_type=jnp.float32) + up_bias
    activated = jax.nn.gelu(hidden_pre, approximate=False).astype(jnp.bfloat16)
    branch = jnp.dot(activated, down_weight, preferred_element_type=jnp.float32) + down_bias
    return hidden_pre, activated, branch


def pair_loss(lead_rows, pair_group):
    seq_count = pair_group.shape[0]
    pairs_all = seq_count * lax.axis_size("dp")
    lead_inv = lax.rsqrt(jnp.sum(lead_rows * lead_rows, axis=-1, keepdims=True) + UNIT_EPS)
    unit_rows = (lead_rows * lead_inv).astype(jnp.bfloat16)
    ids = jnp.broadcast_to(pair_group.astype(jnp.bfloat16)[:, None], (seq_count, 128))
    own_side, other_side = gather_rows(jnp.concatenate([unit_rows, ids], axis=1))
    groups = own_side[:, D].astype(jnp.float32)
    same_group = groups[:, None] == groups[None, :]
    row_weight = pairs_all / GROUPS / jnp.sum(same_group.astype(jnp.float32), axis=1)
    sim_scores = LOGIT_SCALE * jnp.einsum(
        "id,jd->ij", own_side[:, :D], other_side[:, :D], preferred_element_type=jnp.float32
    )
    place = jnp.arange(pairs_all, dtype=jnp.int32)
    diagonal = (place[:, None] == place[None, :]).astype(jnp.float32)
    logits = sim_scores - LOGIT_SCALE * MARGIN * diagonal
    masked = jnp.where(same_group, logits, -jnp.inf)
    col_top = jnp.max(masked, axis=0, keepdims=True)
    col_lse = col_top + jnp.log(jnp.sum(jnp.exp(masked - col_top), axis=0, keepdims=True))
    own = masked[:seq_count]
    row_top = jnp.max(own, axis=1, keepdims=True)
    row_lse = row_top + jnp.log(jnp.sum(jnp.exp(own - row_top), axis=1, keepdims=True))
    own_diag = diagonal[:seq_count]
    own_logit = jnp.sum(logits[:seq_count] * own_diag, axis=1)
    loss_rows = (row_weight[:seq_count] * (row_lse[:, 0] - own_logit))[None]
    dsims = row_weight[:seq_count, None] * (jnp.exp(own - row_lse) - own_diag) + row_weight[
        None, :
    ] * (jnp.exp(own - col_lse) - own_diag)
    unit_grad = LOGIT_SCALE * jnp.dot(
        dsims, other_side[:, :D].astype(jnp.float32), precision=highest
    )
    cross = jnp.sum(lead_rows * unit_grad, axis=-1, keepdims=True)
    lead_grad = lead_inv * unit_grad - lead_inv * lead_inv * lead_inv * cross * lead_rows
    return loss_rows, lead_grad


def shards(
    layer_input,
    pair_group,
    query_weight,
    query_bias,
    key_weight,
    value_weight,
    value_bias,
    out_weight,
    out_bias,
    mixer_gain,
    mixer_shift,
    up_weight,
    up_bias,
    down_weight,
    down_bias,
    final_gain,
    final_shift,
    upstream,
):
    tokens = layer_input[0]
    token_count = tokens.shape[0]
    seq_count = pair_group.shape[0]
    seq_len = token_count // seq_count
    key_span = 2 * seq_len
    factor = 1.0 / math.sqrt(HD)
    place = jnp.arange(key_span) // seq_len
    key_mask = place[:, None] == place[None, :]
    queries = (
        jnp.dot(tokens, query_weight, preferred_element_type=jnp.float32) + query_bias
    ).astype(jnp.bfloat16)
    keys_all = jnp.dot(tokens, key_weight, preferred_element_type=jnp.float32).astype(jnp.bfloat16)
    values_all = (
        jnp.dot(tokens, value_weight, preferred_element_type=jnp.float32) + value_bias
    ).astype(jnp.bfloat16)
    query_heads = to_heads(queries, key_span)
    key_heads = to_heads(keys_all, key_span)
    value_heads = to_heads(values_all, key_span)
    scores = attend_scores(query_heads, key_heads, key_mask, factor)
    row_top = jnp.max(scores, axis=-1, keepdims=True)
    log_total = row_top + jnp.log(jnp.sum(jnp.exp(scores - row_top), axis=-1, keepdims=True))
    probs_low = jnp.exp(scores - log_total).astype(jnp.bfloat16)
    context = jnp.einsum(
        "bhqk,bkhd->bqhd", probs_low, value_heads, preferred_element_type=jnp.float32
    )
    context = context.astype(jnp.bfloat16).reshape(token_count, D)
    attended = jnp.dot(context, out_weight, preferred_element_type=jnp.float32) + out_bias
    normed, hat_one, inv_one = norm_forward(
        tokens.astype(jnp.float32) + attended, mixer_gain, mixer_shift
    )
    normed_low = normed.astype(jnp.bfloat16)
    lead_normed = normed.reshape(seq_count, seq_len, D)[:, 0, :]
    _, _, lead_branch = feed_forward(
        lead_normed.astype(jnp.bfloat16), up_weight, up_bias, down_weight, down_bias
    )
    lead_rows, _, _ = norm_forward(lead_normed + lead_branch, final_gain, final_shift)
    loss_rows, lead_grad = pair_loss(lead_rows, pair_group)
    hidden_pre, activated, branch = feed_forward(
        normed_low, up_weight, up_bias, down_weight, down_bias
    )
    final_rows, hat_two, inv_two = norm_forward(normed + branch, final_gain, final_shift)
    layer_output = final_rows.astype(jnp.bfloat16)[None]
    final_grad = upstream[0].astype(jnp.float32).reshape(seq_count, seq_len, D)
    final_grad = final_grad.at[:, 0, :].add(lead_grad).reshape(token_count, D)
    dresid_two, final_gain_grad, final_shift_grad = norm_backward(
        final_grad, hat_two, inv_two, final_gain
    )
    dbranch = dresid_two.astype(jnp.bfloat16)
    down_weight_grad = outer_sum(activated, dbranch)
    down_bias_grad = jnp.sum(dbranch, axis=0, dtype=jnp.float32)
    dpre = (back_project(dbranch, down_weight) * gelu_slope(hidden_pre)).astype(jnp.bfloat16)
    up_weight_grad = outer_sum(normed_low, dpre)
    up_bias_grad = jnp.sum(dpre, axis=0, dtype=jnp.float32)
    dnormed = dresid_two + back_project(dpre, up_weight)
    dresid_one, mixer_gain_grad, mixer_shift_grad = norm_backward(
        dnormed, hat_one, inv_one, mixer_gain
    )
    datt = dresid_one.astype(jnp.bfloat16)
    out_weight_grad = outer_sum(context, datt)
    out_bias_grad = jnp.sum(datt, axis=0, dtype=jnp.float32)
    dcontext = back_project(datt, out_weight).astype(jnp.bfloat16)
    dcontext_heads = to_heads(dcontext, key_span)
    again = attend_scores(query_heads, key_heads, key_mask, factor)
    probs_f = jnp.exp(again - log_total)
    dprobs = jnp.einsum(
        "bqhd,bkhd->bhqk", dcontext_heads, value_heads, preferred_element_type=jnp.float32
    )
    row_dot = jnp.sum(probs_f * dprobs, axis=-1, keepdims=True)
    dscores = (probs_f * (dprobs - row_dot)).astype(jnp.bfloat16)
    dqueries = (
        jnp.einsum("bhqk,bkhd->bqhd", dscores, key_heads, preferred_element_type=jnp.float32)
        * factor
    )
    dqueries = dqueries.astype(jnp.bfloat16).reshape(token_count, D)
    dkeys = (
        jnp.einsum("bhqk,bqhd->bkhd", dscores, query_heads, preferred_element_type=jnp.float32)
        * factor
    )
    dkeys = dkeys.astype(jnp.bfloat16).reshape(token_count, D)
    dvalues = (
        jnp.einsum(
            "bhqk,bqhd->bkhd",
            probs_f.astype(jnp.bfloat16),
            dcontext_heads,
            preferred_element_type=jnp.float32,
        )
        .astype(jnp.bfloat16)
        .reshape(token_count, D)
    )
    query_weight_grad = outer_sum(tokens, dqueries)
    query_bias_grad = jnp.sum(dqueries, axis=0, dtype=jnp.float32)
    key_weight_grad = outer_sum(tokens, dkeys)
    value_weight_grad = outer_sum(tokens, dvalues)
    value_bias_grad = jnp.sum(dvalues, axis=0, dtype=jnp.float32)
    input_grad = (
        dresid_one
        + back_project(dqueries, query_weight)
        + back_project(dkeys, key_weight)
        + back_project(dvalues, value_weight)
    )
    low = lambda piece: piece.astype(jnp.bfloat16)
    wide = down_bias.shape[0] * 4
    small = jnp.concatenate(
        [
            up_bias_grad,
            query_bias_grad,
            value_bias_grad,
            out_bias_grad,
            mixer_gain_grad,
            mixer_shift_grad,
            down_bias_grad,
            final_gain_grad,
            final_shift_grad,
        ]
    )
    small = jnp.pad(small, (0, 8 * wide - small.shape[0])).reshape(2, 2, 2, 1, wide)
    down_sum = all_sum(low(down_weight_grad).reshape(2, 2, 2, -1, D))
    up_sum = all_sum(low(up_weight_grad).reshape(2, 2, 2, -1, up_weight.shape[1]))
    square = jnp.concatenate(
        [low(query_weight_grad), low(key_weight_grad), low(value_weight_grad), low(out_weight_grad)], axis=1
    ).reshape(2, 2, 2, -1, wide)
    square_sum = all_sum(jnp.concatenate([square, low(small)], axis=3))
    full = jnp.float32
    down_out = down_sum.reshape(down_weight.shape).astype(full)
    up_out = up_sum.reshape(up_weight.shape).astype(full)
    squares = square_sum[:, :, :, :-1].reshape(D, wide).astype(full)
    smalls = square_sum[:, :, :, -1].reshape(-1).astype(full)
    hidden = up_bias.shape[0]
    vector = lambda k: smalls[hidden + k * D : hidden + (k + 1) * D]
    return (
        layer_output,
        input_grad[None],
        loss_rows,
        squares[:, :D],
        vector(0),
        squares[:, D : 2 * D],
        squares[:, 2 * D : 3 * D],
        vector(1),
        squares[:, 3 * D :],
        vector(2),
        vector(3),
        vector(4),
        up_out,
        smalls[:hidden],
        down_out,
        vector(5),
        vector(6),
        vector(7),
    )


def solution(mesh):
    return jax.shard_map(
        shards,
        mesh=mesh,
        in_specs=(
            P("stream", "dp", None),
            P("dp"),
            P(),
            P(),
            P(),
            P(),
            P(),
            P(),
            P(),
            P(),
            P(),
            P(),
            P(),
            P(),
            P(),
            P(),
            P(),
            P("stream", "dp", None),
        ),
        out_specs=(
            P("stream", "dp", None),
            P("stream", "dp", None),
            P("stream", "dp"),
            P(),
            P(),
            P(),
            P(),
            P(),
            P(),
            P(),
            P(),
            P(),
            P(),
            P(),
            P(),
            P(),
            P(),
            P(),
        ),
        check_vma=False,
    )
```

```python
import functools
import math

import jax
import jax.numpy as jnp
from jax import lax
from jax.experimental import pallas as pl
from jax.experimental.pallas import tpu as pltpu
from jax.sharding import PartitionSpec as P

D = 768
HEADS = 12
HD = 64
GROUPS = 109
HALF = D // 2
LANES = 128

MARGIN = 0.3
LOGIT_SCALE = 30.0
NORM_EPS = 1e-12
UNIT_EPS = 1e-06
highest = lax.Precision.HIGHEST
low = jnp.bfloat16
full = jnp.float32


def dot(left, right):
    return lax.dot_general(left, right, (((1,), (0,)), ((), ())), preferred_element_type=full)


def dot_t(left, right):
    return lax.dot_general(left, right, (((1,), (1,)), ((), ())), preferred_element_type=full)


def t_dot(left, right):
    return lax.dot_general(left, right, (((0,), (0,)), ((), ())), preferred_element_type=full)


def mean_of(values):
    return jnp.sum(values, axis=-1, keepdims=True) * (1.0 / D)


def norm_stats(values):
    centred = values - mean_of(values)
    inv_std = lax.rsqrt(mean_of(centred * centred) + NORM_EPS)
    return centred * inv_std, inv_std


def norm_back(grad_hat, normed_hat, inv_std):
    return inv_std * (grad_hat - mean_of(grad_hat) - normed_hat * mean_of(grad_hat * normed_hat))


def normal_cdf(values):
    bell = jnp.exp(-0.5 * values * values)
    step = 1.0 / (1.0 + (0.3275911 / math.sqrt(2.0)) * jnp.abs(values))
    tail = 0.5 * 1.061405429
    for factor in (-1.453152027, 1.421413741, -0.284496736, 0.254829592):
        tail = tail * step + 0.5 * factor
    tail = tail * step * bell
    return jnp.where(values >= 0.0, 1.0 - tail, tail), bell


def gelu_and_slope(values):
    cdf, bell = normal_cdf(values)
    return values * cdf, cdf + values * bell * (1.0 / math.sqrt(2.0 * math.pi))


def columns_sum(values):
    return jnp.sum(values, axis=0, keepdims=True)


def rows_spec(rows, columns, first=0):
    return pl.BlockSpec((rows, columns), lambda i, *_: (first + i, 0))


def fixed_spec(*shape):
    return pl.BlockSpec(shape, lambda *_: (0,) * len(shape))


def shape_of(*shape, dtype=low):
    return jax.ShapeDtypeStruct(shape, dtype)


def params(grid_dims, mib=56):
    return pltpu.CompilerParams(
        dimension_semantics=("arbitrary",) * grid_dims, vmem_limit_bytes=mib << 20
    )


def two_heads(block):
    lane = lax.broadcasted_iota(jnp.int32, block.shape, 1)
    zero = jnp.zeros_like(block)
    return jnp.concatenate([jnp.where(lane < HD, block, zero), jnp.where(lane < HD, zero, block)], axis=0)


def own_head(both):
    count = both.shape[0] // 2
    lane = lax.broadcasted_iota(jnp.int32, (count, both.shape[1]), 1)
    return jnp.where(lane < HD, both[:count], both[count:])


def cells_of(count, seq_len):
    return [
        (slice(start, start + seq_len), slice(first, first + 2 * HD))
        for first in range(0, D, 2 * HD)
        for start in range(0, count, seq_len)
    ]


def joined(pieces, count, seq_len):
    tall = count // seq_len
    columns = [jnp.concatenate(pieces[k : k + tall], axis=0) for k in range(0, len(pieces), tall)]
    return jnp.concatenate(columns, axis=1)


def attention_kernel(seq_len, x_ref, wq, wk, wv, wo, vecs, q_ref, k_ref, v_ref, p_ref, c_ref, nl_ref, hat_ref, inv_ref,
                     nll_ref, hatl_ref):
    x = x_ref[...]
    count = x.shape[0]
    q = (dot(x, wq[...]) + vecs[0:1, :]).astype(low)
    k = dot(x, wk[...]).astype(low)
    v = (dot(x, wv[...]) + vecs[1:2, :]).astype(low)
    q_ref[...], k_ref[...], v_ref[...] = q, k, v
    cells = cells_of(count, seq_len)
    factor = 1.0 / math.sqrt(HD)
    scores = [dot_t(k[cell], two_heads(q[cell])) * factor for cell in cells]
    probs = []
    for cell, score in zip(cells, scores, strict=True):
        terms = jnp.exp(score - jnp.max(score, axis=0, keepdims=True))
        probs.append((terms * (1.0 / columns_sum(terms))).astype(low))
        p_ref[cell] = probs[-1]
    pieces = [own_head(t_dot(prob, v[cell])).astype(low) for cell, prob in zip(cells, probs, strict=True)]
    context = joined(pieces, count, seq_len)
    c_ref[...] = context
    hat, inv_std = norm_stats(x.astype(full) + dot(context, wo[...]) + vecs[2:3, :])
    normed_low = (hat * vecs[3:4, :] + vecs[4:5, :]).astype(low)
    hat_ref[...] = hat
    inv_ref[...] = jnp.broadcast_to(inv_std, inv_ref.shape)
    nl_ref[...] = normed_low
    for s in range(count // seq_len):
        nll_ref[0, s : s + 1, :] = normed_low[s * seq_len : s * seq_len + 1, :].astype(full)
        hatl_ref[0, s : s + 1, :] = hat[s * seq_len : s * seq_len + 1, :]


def attention_forward(tokens, seq_len, wq, wk, wv, wo, vecs):
    count = tokens.shape[0]
    rows = 256
    steps, leads = count // rows, rows // seq_len
    row, mat = rows_spec(rows, D), fixed_spec(D, D)
    lead = pl.BlockSpec((1, leads, D), lambda i: (i, 0, 0))
    return pl.pallas_call(
        functools.partial(attention_kernel, seq_len),
        grid=(steps,),
        in_specs=[row, mat, mat, mat, mat, fixed_spec(8, D)],
        out_specs=[row] * 7 + [rows_spec(rows, LANES), lead, lead],
        out_shape=[shape_of(count, D)] * 6
        + [shape_of(count, D, dtype=full), shape_of(count, LANES, dtype=full)]
        + [shape_of(steps, leads, D, dtype=full)] * 2,
        compiler_params=params(1),
        name="attention_forward",
        cost_estimate=pl.CostEstimate(flops=8 * count * D * D, bytes_accessed=16 << 20, transcendentals=count * D),
    )(tokens, wq, wk, wv, wo, vecs)


def lead_kernel(nl_ref, hat_ref, uw, ub, dw, vecs, lead_ref, hat2_ref, inv2_ref, linv_ref, unit_ref, nl, acc):
    step = pl.program_id(0)

    @pl.when(step == 0)
    def _():
        hat = jnp.concatenate([hat_ref[k] for k in range(hat_ref.shape[0])], axis=0)
        nl[...] = jnp.concatenate([nl_ref[k] for k in range(nl_ref.shape[0])], axis=0).astype(low)
        acc[...] = hat * vecs[3:4, :] + vecs[4:5, :] + vecs[5:6, :]

    pre = dot(nl[...], uw[...]) + ub[...]
    acc[...] += dot(gelu_and_slope(pre)[0].astype(low), dw[...])

    @pl.when(step == pl.num_programs(0) - 1)
    def _():
        hat, inv_std = norm_stats(acc[...])
        lead = hat * vecs[6:7, :] + vecs[7:8, :]
        lead_inv = lax.rsqrt(jnp.sum(lead * lead, axis=-1, keepdims=True) + UNIT_EPS)
        lead_ref[...] = lead
        hat2_ref[...] = hat
        inv2_ref[...] = jnp.broadcast_to(inv_std, inv2_ref.shape)
        linv_ref[...] = jnp.broadcast_to(lead_inv, linv_ref.shape)
        unit_ref[...] = (lead * lead_inv).astype(low)


def lead_forward(nl, hat, uw, ub, dw, vecs):
    count = nl.shape[0] * nl.shape[1]
    hidden = uw.shape[1]
    row, lane = fixed_spec(count, D), fixed_spec(count, LANES)
    return pl.pallas_call(
        lead_kernel,
        grid=(hidden // D,),
        in_specs=[
            fixed_spec(*nl.shape), fixed_spec(*hat.shape),
            pl.BlockSpec((D, D), lambda j: (0, j)), pl.BlockSpec((1, D), lambda j: (0, j)),
            pl.BlockSpec((D, D), lambda j: (j, 0)), fixed_spec(8, D),
        ],
        out_specs=[row, row, lane, lane, row],
        out_shape=[shape_of(count, D, dtype=full)] * 2
        + [shape_of(count, LANES, dtype=full)] * 2 + [shape_of(count, D)],
        scratch_shapes=[pltpu.VMEM((count, D), low), pltpu.VMEM((count, D), full)],
        compiler_params=params(1),
        name="lead_forward",
        cost_estimate=pl.CostEstimate(flops=4 * count * D * hidden, bytes_accessed=10 << 20, transcendentals=0),
    )(nl, hat, uw, ub, dw, vecs)


def put_swapped(ref, value, bit, lead=()):
    for part in range(2):
        at = pl.multiple_of((bit if part == 0 else 1 - bit) * HALF, LANES)
        ref[lead + (slice(None), pl.ds(at, HALF))] = value[:, part * HALF : (part + 1) * HALF]


def ff_kernel(place, nl_ref, hat_ref, up_ref, uw, ub, dw, vecs, *rest):
    out_ref, act_ref, slope_ref, dr2_ref, sums_ref, acc = rest[-6:]
    step = pl.program_id(0)

    @pl.when(step == 0)
    def _():
        acc[...] = hat_ref[...] * vecs[3:4, :] + vecs[4:5, :] + vecs[5:6, :]

    value, slope = gelu_and_slope(dot(nl_ref[...], uw[...]) + ub[...])
    act = value.astype(low)
    slope_ref[...] = slope.astype(low)
    put_swapped(act_ref, act, place[8 + step])
    acc[...] += dot(act, dw[...])

    @pl.when(step == pl.num_programs(0) - 1)
    def _():
        hat, inv_std = norm_stats(acc[...])
        out_ref[...] = (hat * vecs[6:7, :] + vecs[7:8, :]).astype(low)
        grad = up_ref[...].astype(full)
        dr2_ref[...] = norm_back(grad * vecs[6:7, :], hat, inv_std)
        sums_ref[0, 0:1, :] = columns_sum(grad * hat)
        sums_ref[0, 1:2, :] = columns_sum(grad)


def ff_forward(place, part, parts, carried, nl, hat, upstream, uw, ub, dw, vecs):
    count = nl.shape[0]
    rows = count // parts
    hidden = uw.shape[1]
    row = pl.BlockSpec((rows, D), lambda j, *_: (part, 0))
    wide = pl.BlockSpec((rows, D), lambda j, place: (part, j))
    held = pl.BlockSpec((rows, D), lambda j, place: (part, place[j]))
    operands = [nl, hat, upstream, uw, ub, dw, vecs]
    in_specs = [
        row, row, row, pl.BlockSpec((D, D), lambda j, place: (0, j)), pl.BlockSpec((1, D), lambda j, place: (0, j)),
        pl.BlockSpec((D, D), lambda j, place: (j, 0)), fixed_spec(8, D),
    ]
    aliases = {}
    if carried is not None:
        aliases = {1 + len(operands) + k: k for k in range(len(carried))}
        operands += carried
        in_specs += [pl.BlockSpec(memory_space=pl.ANY)] * len(carried)
    return pl.pallas_call(
        ff_kernel,
        grid_spec=pltpu.PrefetchScalarGridSpec(
            num_scalar_prefetch=1,
            grid=(hidden // D,),
            in_specs=in_specs,
            out_specs=[row, held, wide, row, pl.BlockSpec((1, 8, D), lambda j, *_: (part, 0, 0))],
            scratch_shapes=[pltpu.VMEM((rows, D), full)],
        ),
        out_shape=[
            shape_of(count, D), shape_of(count, hidden), shape_of(count, hidden),
            shape_of(count, D, dtype=full), shape_of(parts, 8, D, dtype=full),
        ],
        input_output_aliases=aliases,
        compiler_params=params(1),
        name=f"ff_forward_{part}",
        cost_estimate=pl.CostEstimate(flops=4 * rows * D * hidden, bytes_accessed=12 << 20, transcendentals=rows * hidden),
    )(place, *operands)


def down_grad_kernel(seq_len, emit, *refs):
    if emit:
        dr2_ref, fix_ref, act_ref, out_ref, db_ref, sum_ref = refs

        @pl.when(pl.program_id(0) == 0)
        def _():
            total = jnp.zeros((1, D), full)
            for s in range(fix_ref.shape[0]):
                rows = slice(s * seq_len, (s + 1) * seq_len)
                block = dr2_ref[rows, :]
                first = lax.broadcasted_iota(jnp.int32, block.shape, 0) == 0
                block = (block + jnp.where(first, fix_ref[s : s + 1, :], 0.0)).astype(low)
                db_ref[rows, :] = block
                total += columns_sum(block.astype(full))
            sum_ref[...] = total
    else:
        db_ref, act_ref, out_ref = refs
    out_ref[0] = t_dot(act_ref[...], db_ref[...]).astype(low)


def down_grad_first(dr2, fix, act, seq_len, parts, first):
    count = dr2.shape[0]
    return pl.pallas_call(
        functools.partial(down_grad_kernel, seq_len, True),
        grid=(parts,),
        in_specs=[fixed_spec(count, D), fixed_spec(*fix.shape), pl.BlockSpec((count, D), lambda p: (0, first + p))],
        out_specs=[pl.BlockSpec((1, D, D), lambda p: (p, 0, 0)), fixed_spec(count, D), fixed_spec(1, D)],
        out_shape=[shape_of(parts, D, D), shape_of(count, D), shape_of(1, D, dtype=full)],
        compiler_params=params(1),
        name="down_grad_first",
        cost_estimate=pl.CostEstimate(flops=2 * parts * count * D * D, bytes_accessed=8 << 20, transcendentals=0),
    )(dr2, fix, act)


def column_grad_kernel(left_ref, right_ref, out_ref):
    out_ref[0] = t_dot(left_ref[...], right_ref[...]).astype(low)


def paired_grad(left, right, parts, first, wide_left, name):
    count = left.shape[0]
    moving = pl.BlockSpec((count, D), lambda p: (0, first + p))
    still = fixed_spec(count, D)
    return pl.pallas_call(
        column_grad_kernel,
        grid=(parts,),
        in_specs=[moving, still] if wide_left else [still, moving],
        out_specs=pl.BlockSpec((1, D, D), lambda p: (p, 0, 0)),
        out_shape=shape_of(parts, D, D),
        compiler_params=params(1),
        name=name,
        cost_estimate=pl.CostEstimate(flops=2 * parts * count * D * D, bytes_accessed=6 << 20, transcendentals=0),
    )(left, right)


def ff_back_kernel(seq_len, place, db_ref, dr2_ref, fix_ref, slope_ref, hat_ref, inv_ref, uw, dw, wo, vecs, *rest):
    dpre_ref, dr1_ref, datt_ref, dctx_ref, bsum_ref, sums_ref, acc = rest[-7:]
    step = pl.program_id(0)
    rows = db_ref.shape[0]

    @pl.when(step == 0)
    def _():
        for s in range(rows // seq_len):
            span = slice(s * seq_len, (s + 1) * seq_len)
            block = dr2_ref[span, :]
            first = lax.broadcasted_iota(jnp.int32, block.shape, 0) == 0
            acc[span, :] = block + jnp.where(first, fix_ref[0, s : s + 1, :], 0.0)

    dpre = (dot_t(db_ref[...], dw[...]) * slope_ref[...].astype(full)).astype(low)
    put_swapped(dpre_ref, dpre, place[8 + step])
    bsum_ref[0, 0:1, :] = columns_sum(dpre.astype(full))
    acc[...] += dot_t(dpre, uw[...])

    @pl.when(step == pl.num_programs(0) - 1)
    def _():
        grad, hat = acc[...], hat_ref[...]
        dr1 = norm_back(grad * vecs[3:4, :], hat, inv_ref[:, 0:1])
        dr1_ref[...] = dr1
        datt = dr1.astype(low)
        put_swapped(datt_ref, datt, place[8 + 3])
        sums_ref[0, 0:1, :] = columns_sum(grad * hat)
        sums_ref[0, 1:2, :] = columns_sum(grad)
        sums_ref[0, 2:3, :] = columns_sum(datt.astype(full))
        dctx_ref[...] = dot_t(datt, wo[...]).astype(low)


def ff_backward(place, seq_len, part, parts, carried, db, dr2, fix, slope, hat, inv, uw, dw, wo, vecs):
    count = db.shape[0]
    rows = count // parts
    hidden = uw.shape[1]
    row = pl.BlockSpec((rows, D), lambda j, *_: (part, 0))
    held = pl.BlockSpec((rows, D), lambda j, place: (part, place[j]))
    fix = fix.reshape(parts, -1, D)
    operands = [db, dr2, fix, slope, hat, inv, uw, dw, wo, vecs]
    in_specs = [
        row, row, pl.BlockSpec((1,) + fix.shape[1:], lambda j, *_: (part, 0, 0)),
        pl.BlockSpec((rows, D), lambda j, place: (part, j)),
        row, pl.BlockSpec((rows, LANES), lambda j, *_: (part, 0)),
        pl.BlockSpec((D, D), lambda j, place: (0, j)), pl.BlockSpec((D, D), lambda j, place: (j, 0)),
        fixed_spec(D, D), fixed_spec(8, D),
    ]
    aliases = {}
    if carried is not None:
        aliases = {1 + len(operands) + k: k for k in range(len(carried))}
        operands += carried
        in_specs += [pl.BlockSpec(memory_space=pl.ANY)] * len(carried)
    return pl.pallas_call(
        functools.partial(ff_back_kernel, seq_len),
        grid_spec=pltpu.PrefetchScalarGridSpec(
            num_scalar_prefetch=1,
            grid=(hidden // D,),
            in_specs=in_specs,
            out_specs=[
                held, row, row, row,
                pl.BlockSpec((1, 8, D), lambda j, *_: (part, 0, j)),
                pl.BlockSpec((1, 8, D), lambda j, *_: (part, 0, 0)),
            ],
            scratch_shapes=[pltpu.VMEM((rows, D), full)],
        ),
        out_shape=[
            shape_of(count, hidden), shape_of(count, D, dtype=full), shape_of(count, D), shape_of(count, D),
            shape_of(parts, 8, hidden, dtype=full), shape_of(parts, 8, D, dtype=full),
        ],
        input_output_aliases=aliases,
        compiler_params=params(1),
        name=f"ff_backward_{part}",
        cost_estimate=pl.CostEstimate(flops=4 * rows * D * hidden, bytes_accessed=12 << 20, transcendentals=0),
    )(place, *operands)


def attention_back_kernel(seq_len, place, q_ref, k_ref, v_ref, p_ref, dc_ref, dqkv_ref, plain_ref, sums_ref):
    q, k, v, probs, dctx = (ref[...] for ref in (q_ref, k_ref, v_ref, p_ref, dc_ref))
    count = q.shape[0]
    cells = cells_of(count, seq_len)
    factor = 1.0 / math.sqrt(HD)
    spread_dctx = [two_heads(dctx[cell]) for cell in cells]
    dprobs = [dot_t(v[cell], wide) for cell, wide in zip(cells, spread_dctx, strict=True)]
    dvals = [dot(probs[cell], wide).astype(low) for cell, wide in zip(cells, spread_dctx, strict=True)]
    dscores = []
    for cell, dprob in zip(cells, dprobs, strict=True):
        prob = probs[cell].astype(full)
        dscores.append((prob * (dprob - columns_sum(prob * dprob))).astype(low))
    dkeys = [(dot(ds, two_heads(q[cell])) * factor).astype(low) for cell, ds in zip(cells, dscores, strict=True)]
    dqueries = [(own_head(t_dot(ds, k[cell])) * factor).astype(low) for cell, ds in zip(cells, dscores, strict=True)]
    for rank, pieces in enumerate((dqueries, dkeys, dvals)):
        grad = joined(pieces, count, seq_len)
        plain_ref[rank] = grad
        put_swapped(dqkv_ref, grad, place[8 + rank], (rank,))
        if rank != 1:
            sums_ref[0, rank : rank + 1, :] = columns_sum(grad.astype(full))


def attention_backward(place, seq_len, q, k, v, probs, dctx):
    count = q.shape[0]
    rows = 256
    row = pl.BlockSpec((rows, D), lambda i, *_: (i, 0))
    three = pl.BlockSpec((3, rows, D), lambda i, *_: (0, i, 0))
    return pl.pallas_call(
        functools.partial(attention_back_kernel, seq_len),
        grid_spec=pltpu.PrefetchScalarGridSpec(
            num_scalar_prefetch=1,
            grid=(count // rows,),
            in_specs=[row] * 5,
            out_specs=[three, three, pl.BlockSpec((1, 8, D), lambda i, *_: (i, 0, 0))],
        ),
        out_shape=[shape_of(3, count, D), shape_of(3, count, D), shape_of(count // rows, 8, D, dtype=full)],
        compiler_params=params(1),
        name="attention_backward",
        cost_estimate=pl.CostEstimate(flops=20 * count * D * HD, bytes_accessed=16 << 20, transcendentals=0),
    )(place, q, k, v, probs, dctx)


def square_grad_kernel(first, place, x_ref, c_ref, dqkv_ref, datt_ref, small_ref, out_ref):
    which = place[4 + first + pl.program_id(0)]

    @pl.when(which < 3)
    def _():
        out_ref[0, :D, :] = t_dot(x_ref[...], dqkv_ref[0]).astype(low)

    @pl.when(which == 3)
    def _():
        out_ref[0, :D, :] = t_dot(c_ref[...], datt_ref[...]).astype(low)

    bit = place[8 + which]
    for part in range(2):
        at = pl.multiple_of((bit if part == 0 else 1 - bit) * HALF, LANES)
        out_ref[0, D:, pl.ds(at, HALF)] = small_ref[0, :, part * HALF : (part + 1) * HALF].astype(low)


def square_grad(place, tokens, context, dqkv, datt, small, parts, first):
    count = tokens.shape[0]
    still = fixed_spec(count, D)
    which = lambda p, place: place[4 + first + p]
    return pl.pallas_call(
        functools.partial(square_grad_kernel, first),
        grid_spec=pltpu.PrefetchScalarGridSpec(
            num_scalar_prefetch=1,
            grid=(parts,),
            in_specs=[
                still, still,
                pl.BlockSpec((1, count, D), lambda p, place: (jnp.minimum(which(p, place), 2), 0, 0)),
                still,
                pl.BlockSpec((1, 16, D), lambda p, place: (which(p, place), 0, 0)),
            ],
            out_specs=pl.BlockSpec((1, D + 16, D), lambda p, *_: (p, 0, 0)),
        ),
        out_shape=shape_of(parts, D + 16, D),
        compiler_params=params(1),
        name=f"square_grad_{first}",
        cost_estimate=pl.CostEstimate(flops=2 * parts * count * D * D, bytes_accessed=8 << 20, transcendentals=0),
    )(place, tokens, context, dqkv, datt, small)


def input_grad_kernel(dr1_ref, d_ref, wq, wk, wv, out_ref):
    out_ref[...] = (
        dr1_ref[...] + dot_t(d_ref[0], wq[...]) + dot_t(d_ref[1], wk[...]) + dot_t(d_ref[2], wv[...])
    )


def input_gradient(dr1, dqkv, wq, wk, wv):
    count = dr1.shape[0]
    rows = 256
    mat = fixed_spec(D, D)
    return pl.pallas_call(
        input_grad_kernel,
        grid=(count // rows,),
        in_specs=[rows_spec(rows, D), pl.BlockSpec((3, rows, D), lambda i: (0, i, 0)), mat, mat, mat],
        out_specs=rows_spec(rows, D),
        out_shape=shape_of(count, D, dtype=full),
        compiler_params=params(1),
        name="input_gradient",
        cost_estimate=pl.CostEstimate(flops=6 * count * D * D, bytes_accessed=14 << 20, transcendentals=0),
    )(dr1, dqkv, wq, wk, wv)


def spread_kernel(split_rows, first, place, own_ref, *rest):
    out_ref = rest[-1]
    mine = own_ref[0]
    bit = place[8 + place[4 + first + pl.program_id(0)]]
    for part in range(2):
        span = slice(part * HALF, (part + 1) * HALF)
        at = pl.multiple_of((bit if part == 0 else 1 - bit) * HALF, LANES)
        if split_rows:
            out_ref[pl.ds(at, HALF), :] = mine[span].astype(full)
        else:
            out_ref[:, pl.ds(at, HALF)] = mine[:, span].astype(full)


def spread(place, blocks, first, out, split_rows, name):
    parts = blocks.shape[0]
    total = (4 * D, D) if split_rows else (D, 4 * D)
    where = lambda p, place: place[4 + first + p]
    index = (lambda p, place: (where(p, place), 0)) if split_rows else (lambda p, place: (0, where(p, place)))
    operands = [blocks] if out is None else [blocks, out]
    return pl.pallas_call(
        functools.partial(spread_kernel, split_rows, first),
        grid_spec=pltpu.PrefetchScalarGridSpec(
            num_scalar_prefetch=1,
            grid=(parts,),
            in_specs=[pl.BlockSpec((1, D, D), lambda p, *_: (p, 0, 0))]
            + [pl.BlockSpec(memory_space=pl.ANY)] * (len(operands) - 1),
            out_specs=pl.BlockSpec((D, D), index),
        ),
        out_shape=shape_of(*total, dtype=full),
        input_output_aliases={} if out is None else {2: 0},
        compiler_params=params(1),
        name=name,
        cost_estimate=pl.CostEstimate(flops=0, bytes_accessed=6 * parts * D * D, transcendentals=0),
    )(place, *operands)


def places():
    half = lax.axis_index("stream")
    chip = lax.axis_index("dp")
    bits = (chip & 1, (chip >> 1) & 1)
    pick = lambda side, one, two: jnp.where(side == 0, one, two)
    block_at = [2 * half + pick(half, *bits), 2 * half + 1 - pick(half, *bits)]
    block_at += [2 * (1 - half) + pick(1 - half, *bits), 2 * (1 - half) + 1 - pick(1 - half, *bits)]
    place_of = [sum(jnp.where(block == k, rank, 0) for rank, block in enumerate(block_at)) for k in range(4)]
    swapped = [bits[1], bits[1], bits[0], bits[0]]
    return jnp.stack(place_of + block_at + swapped).astype(jnp.int32)


def chip_partner(bit_zero, bit_one):
    chips = lax.axis_size("dp")
    return [
        (half * chips + chip, half * chips + (chip ^ (bit_zero if half == 0 else bit_one)))
        for half in range(2)
        for chip in range(chips)
    ]


def core_partner():
    chips = lax.axis_size("dp")
    return [(half * chips + chip, (1 - half) * chips + chip) for half in range(2) for chip in range(chips)]


def swap(piece, pairs):
    return lax.ppermute(piece, ("stream", "dp"), pairs)


def add_low(left, right):
    return (left.astype(full) + right.astype(full)).astype(low)


def tie(value, after):
    return value if after is None else lax.optimization_barrier((value, after))[0]


def all_sum(sent, kept, axis):
    other = swap(sent, core_partner())
    after = yield sent
    kept = tie(kept, after)
    sent = add_low(kept[1], other[1])
    block = add_low(kept[0], other[0])
    other = swap(sent, chip_partner(1, 2))
    after = yield sent
    block = tie(block, after)
    split = lambda rows, start: lax.slice_in_dim(rows, start, start + HALF, axis=axis)
    sent = add_low(split(block, HALF), split(other, HALF))
    mine = add_low(split(block, 0), split(other, 0))
    other = swap(sent, chip_partner(2, 1))
    after = yield sent
    bits = [1 << k for k in range(2, lax.axis_size("dp").bit_length() - 1)]
    for rank, pair in enumerate(zip(bits, bits[::-1], strict=True)):
        mine = add_low(tie(mine, after), other)
        other = swap(mine, chip_partner(*pair))
        after = (yield mine) if rank in (0, len(bits) - 1) else None
    mine = add_low(tie(mine, after), other)
    other = swap(mine, chip_partner(2, 1))
    after = yield mine
    block = jnp.concatenate([tie(mine, after), other], axis=axis)
    other = swap(block, chip_partner(1, 2))
    after = yield block
    blocks = jnp.stack([tie(block, after), other])
    other = swap(blocks, core_partner())
    after = yield blocks
    yield tie(blocks, after), other


def gather_rows(rows):
    chips = lax.axis_size("dp")
    bit = 1
    after = None
    while bit < chips:
        others = [swap(rows, chip_partner(k * bit, k * bit)) for k in range(1, 4) if k * bit < chips]
        after = yield rows
        rows = jnp.concatenate([tie(rows, after)] + others)
        bit *= 4
    other = swap(rows, core_partner())
    yield rows
    yield rows, other


def pair_loss(lead_rows, lead_inv, own_side, other_side, seq_count):
    pairs_all = own_side.shape[0]
    groups = own_side[:, D].astype(full)
    same_group = groups[:, None] == groups[None, :]
    row_weight = pairs_all / GROUPS / jnp.sum(same_group.astype(full), axis=1)
    sim_scores = LOGIT_SCALE * jnp.einsum(
        "id,jd->ij", own_side[:, :D], other_side[:, :D], preferred_element_type=full
    )
    place = jnp.arange(pairs_all, dtype=jnp.int32)
    diagonal = (place[:, None] == place[None, :]).astype(full)
    logits = sim_scores - LOGIT_SCALE * MARGIN * diagonal
    masked = jnp.where(same_group, logits, -jnp.inf)
    col_top = jnp.max(masked, axis=0, keepdims=True)
    col_lse = col_top + jnp.log(jnp.sum(jnp.exp(masked - col_top), axis=0, keepdims=True))
    own = masked[:seq_count]
    row_top = jnp.max(own, axis=1, keepdims=True)
    row_lse = row_top + jnp.log(jnp.sum(jnp.exp(own - row_top), axis=1, keepdims=True))
    own_diag = diagonal[:seq_count]
    own_logit = jnp.sum(logits[:seq_count] * own_diag, axis=1)
    loss_rows = (row_weight[:seq_count] * (row_lse[:, 0] - own_logit))[None]
    dsims = row_weight[:seq_count, None] * (jnp.exp(own - row_lse) - own_diag) + row_weight[
        None, :
    ] * (jnp.exp(own - col_lse) - own_diag)
    unit_grad = LOGIT_SCALE * jnp.dot(dsims, other_side[:, :D].astype(full), precision=highest)
    cross = jnp.sum(lead_rows * unit_grad, axis=-1, keepdims=True)
    lead_grad = lead_inv * unit_grad - lead_inv * lead_inv * lead_inv * cross * lead_rows
    return loss_rows, lead_grad


def shards(
    layer_input, pair_group, query_weight, query_bias, key_weight, value_weight, value_bias,
    out_weight, out_bias, mixer_gain, mixer_shift, up_weight, up_bias, down_weight, down_bias,
    final_gain, final_shift, upstream,
):
    tokens = layer_input[0]
    count = tokens.shape[0]
    seq_count = pair_group.shape[0]
    seq_len = count // seq_count
    place = places()
    vecs = jnp.stack(
        [query_bias, value_bias, out_bias, mixer_gain, mixer_shift, down_bias, final_gain, final_shift]
    )
    ub = up_bias.reshape(1, -1)
    g2 = final_gain.reshape(1, -1)

    q, k, v, probs, context, nl, hat, inv, lead_nl, lead_hat = attention_forward(
        tokens, seq_len, query_weight, key_weight, value_weight, out_weight, vecs
    )
    lead, lead_hat, lead_inv2, lead_inv, units = lead_forward(lead_nl, lead_hat, up_weight, ub, down_weight, vecs)
    ids = jnp.broadcast_to(pair_group.astype(low)[:, None], (seq_count, LANES))
    hops = gather_rows(jnp.concatenate([units, ids], axis=1))
    sent = next(hops)
    parts = 2
    carried = None
    for part in range(parts):
        carried = ff_forward(
            place, part, parts, carried, tie(nl, sent), hat, upstream[0], up_weight, ub, down_weight, vecs
        )
        sent = hops.send(carried[3])
    while not isinstance(sent, tuple):
        sent = hops.send(None)
    own_side, other_side = sent
    layer_output, act, slope, dr2, final_sums = carried
    loss_rows, lead_grad = pair_loss(lead, lead_inv[:, :1], own_side, other_side, seq_count)
    fix = norm_back(lead_grad * g2, lead_hat, lead_inv2[:, :1])
    final_gain_grad = jnp.sum(final_sums[:, 0], axis=0) + jnp.sum(lead_grad * lead_hat, axis=0)
    final_shift_grad = jnp.sum(final_sums[:, 1], axis=0) + jnp.sum(lead_grad, axis=0)

    down_sent, dbranch, down_bias_grad = down_grad_first(dr2, fix, act, seq_len, 2, 2)
    down_kept = paired_grad(act, tie(dbranch, down_sent), 2, 0, True, "down_grad_second")
    down = all_sum(down_sent, down_kept, 0)
    next(down)
    sent = down.send(None)
    carried = None
    for part in range(2):
        carried = ff_backward(
            place, seq_len, part, 2, carried, tie(dbranch, sent), dr2, fix, slope, hat, inv,
            up_weight, down_weight, out_weight, vecs,
        )
        sent = down.send(carried[0])
    dpre, dr1, datt, dctx, up_bias_sums, mixer_sums = carried
    up_sent = paired_grad(tie(nl, sent), dpre, 2, 2, False, "up_grad_first")
    up_kept = paired_grad(nl, tie(dpre, up_sent), 2, 0, False, "up_grad_second")
    up = all_sum(up_sent, up_kept, 1)
    next(up)
    sent = up.send(None)
    sent = down.send(sent)
    dqkv, dqkv_plain, qkv_sums = attention_backward(place, seq_len, tie(q, sent), k, v, probs, dctx)
    sent = up.send(dqkv)
    mixer = jnp.sum(mixer_sums, axis=0)
    qkv_bias = jnp.sum(qkv_sums, axis=0)
    small = jnp.concatenate(
        [
            jnp.sum(up_bias_sums[:, 0], axis=0),
            qkv_bias[0], qkv_bias[2], mixer[2], mixer[0], mixer[1],
            down_bias_grad[0], final_gain_grad, final_shift_grad,
        ]
    ).reshape(-1, D)
    small = jnp.pad(small, ((0, 64 - small.shape[0]), (0, 0))).reshape(4, 16, D)
    square_sent = square_grad(place, tie(tokens, sent), context, dqkv, datt, small, 2, 2)
    sent = down.send(square_sent)
    square_kept = square_grad(place, tie(tokens, sent), context, dqkv, datt, small, 2, 0)
    square = all_sum(square_sent, square_kept, 1)
    next(square)
    sent = square.send(sent)
    sent = up.send(sent)
    sent = down.send(sent)
    input_grad = input_gradient(dr1, tie(dqkv_plain, sent), query_weight, key_weight, value_weight)
    sent = up.send(input_grad)
    sent = square.send(sent)
    sent = down.send(sent)
    down_out = spread(place, tie(sent, sent), 0, None, True, "down_spread_own")
    sent = square.send(down_out)
    sent = up.send(sent)
    down_own, down_other = down.send(sent)
    down_out = spread(place, down_other, 2, down_out, True, "down_spread_other")
    sent = square.send(down_out)
    sent = up.send(sent)
    sent = square.send(sent)
    up_own = up.send(sent)
    up_out = spread(place, up_own, 0, None, False, "up_spread_own")
    sent = square.send(up_out)
    up_own, up_other = up.send(sent)
    up_out = spread(place, up_other, 2, up_out, False, "up_spread_other")
    sent = square.send(up_out)
    square_own, square_other = square.send(None)
    squares, smalls = square_out(place, square_own, square_other)
    hidden = up_bias.shape[0]
    vector = lambda k: smalls[hidden + k * D : hidden + (k + 1) * D]
    return (
        layer_output[None], input_grad[None], loss_rows,
        squares[0], vector(0), squares[1], squares[2], vector(1), squares[3], vector(2),
        vector(3), vector(4), up_out, smalls[:hidden], down_out, vector(5), vector(6), vector(7),
    )


def square_out_kernel(place, own_ref, other_ref, q_ref, k_ref, v_ref, o_ref, small_ref):
    for rank in range(4):
        source = own_ref if rank < 2 else other_ref
        which = place[4 + rank]
        for target, ref in enumerate((q_ref, k_ref, v_ref, o_ref)):

            @pl.when(which == target)
            def _(ref=ref, source=source, rank=rank, target=target):
                for part in range(2):
                    bit = place[8 + target]
                    at = pl.multiple_of((bit if part == 0 else 1 - bit) * HALF, LANES)
                    lanes = slice(part * HALF, (part + 1) * HALF)
                    ref[:, pl.ds(at, HALF)] = source[rank % 2, :D, lanes].astype(full)
                    small_ref[target, :, pl.ds(at, HALF)] = source[rank % 2, D:, lanes].astype(full)


def square_out(place, own, other):
    spec = pl.BlockSpec(memory_space=pltpu.VMEM)
    *squares, small = pl.pallas_call(
        square_out_kernel,
        in_specs=[pl.BlockSpec(memory_space=pltpu.SMEM), spec, spec],
        out_specs=[spec] * 5,
        out_shape=[shape_of(D, D, dtype=full)] * 4 + [shape_of(4, 16, D, dtype=full)],
        compiler_params=pltpu.CompilerParams(vmem_limit_bytes=40 << 20),
        name="square_out",
    )(place, own, other)
    return squares, small.reshape(-1)


def solution(mesh):
    split = P("stream", "dp", None)
    return jax.shard_map(
        shards,
        mesh=mesh,
        in_specs=(split, P("dp")) + (P(),) * 15 + (split,),
        out_specs=(split, split, P("stream", "dp")) + (P(),) * 15,
        check_vma=False,
    )
```

```python
import functools
import math

import jax
import jax.numpy as jnp
from jax import lax
from jax.experimental import pallas as pl
from jax.experimental.pallas import tpu as pltpu
from jax.sharding import PartitionSpec as P

D = 768
HEADS = 12
HD = 64
GROUPS = 109
LANES = 128

MARGIN = 0.3
LOGIT_SCALE = 30.0
NORM_EPS = 1e-12
UNIT_EPS = 1e-06
highest = lax.Precision.HIGHEST
low = jnp.bfloat16
full = jnp.float32


def dot(left, right):
    return lax.dot_general(left, right, (((1,), (0,)), ((), ())), preferred_element_type=full)


def dot_t(left, right):
    return lax.dot_general(left, right, (((1,), (1,)), ((), ())), preferred_element_type=full)


def t_dot(left, right):
    return lax.dot_general(left, right, (((0,), (0,)), ((), ())), preferred_element_type=full)


def mean_of(values):
    return jnp.sum(values, axis=-1, keepdims=True) * (1.0 / D)


def norm_stats(values):
    centred = values - mean_of(values)
    inv_std = lax.rsqrt(mean_of(centred * centred) + NORM_EPS)
    return centred * inv_std, inv_std


def norm_back(grad_hat, normed_hat, inv_std):
    return inv_std * (grad_hat - mean_of(grad_hat) - normed_hat * mean_of(grad_hat * normed_hat))


def normal_cdf(values):
    bell = jnp.exp(-0.5 * values * values)
    step = 1.0 / (1.0 + (0.3275911 / math.sqrt(2.0)) * jnp.abs(values))
    tail = 0.5 * 1.061405429
    for factor in (-1.453152027, 1.421413741, -0.284496736, 0.254829592):
        tail = tail * step + 0.5 * factor
    tail = tail * step * bell
    return jnp.where(values >= 0.0, 1.0 - tail, tail), bell


def gelu_and_slope(values):
    cdf, bell = normal_cdf(values)
    return values * cdf, cdf + values * bell * (1.0 / math.sqrt(2.0 * math.pi))


def columns_sum(values):
    return jnp.sum(values, axis=0, keepdims=True)


def line(ref, first=0):
    return jnp.concatenate([ref[pl.ds(first + k, 1), :] for k in range(D // LANES)], axis=1)


def fixed_spec(*shape):
    return pl.BlockSpec(shape, lambda *_: (0,) * len(shape))


def vector_spec(count=D):
    return fixed_spec(count // LANES, LANES)


def shape_of(*shape, dtype=low):
    return jax.ShapeDtypeStruct(shape, dtype)


def far(*shape, dtype=low):
    return pltpu.HBM(shape, dtype)


def params(grid_dims, mib=20):
    return pltpu.CompilerParams(dimension_semantics=("arbitrary",) * grid_dims, vmem_limit_bytes=mib << 20)


def cost(micros):
    return pl.CostEstimate(flops=int(micros * 3.0 * 1.15e9), bytes_accessed=1000, transcendentals=0)


def two_heads(block):
    lane = lax.broadcasted_iota(jnp.int32, block.shape, 1)
    zero = jnp.zeros_like(block)
    return jnp.concatenate([jnp.where(lane < HD, block, zero), jnp.where(lane < HD, zero, block)], axis=0)


def own_head(both):
    count = both.shape[0] // 2
    lane = lax.broadcasted_iota(jnp.int32, (count, both.shape[1]), 1)
    return jnp.where(lane < HD, both[:count], both[count:])


def cells_of(count, seq_len):
    return [
        (slice(start, start + seq_len), slice(first, first + 2 * HD))
        for first in range(0, D, 2 * HD)
        for start in range(0, count, seq_len)
    ]


def joined(pieces, count, seq_len):
    tall = count // seq_len
    columns = [jnp.concatenate(pieces[k : k + tall], axis=0) for k in range(0, len(pieces), tall)]
    return jnp.concatenate(columns, axis=1)


def attention_kernel(seq_len, x_ref, wq, wk, wv, wo, bq, bv, bo, gain, shift,
                     q_ref, k_ref, v_ref, p_ref, c_ref, nl_ref, hat_ref, inv_ref, nll_ref, hatl_ref):
    x = x_ref[...]
    count = x.shape[0]
    q = (dot(x, wq[...]) + line(bq)).astype(low)
    k = dot(x, wk[...]).astype(low)
    v = (dot(x, wv[...]) + line(bv)).astype(low)
    q_ref[...], k_ref[...], v_ref[...] = q, k, v
    cells = cells_of(count, seq_len)
    factor = 1.0 / math.sqrt(HD)
    scores = [dot_t(k[cell], two_heads(q[cell])) * factor for cell in cells]
    probs = []
    for cell, score in zip(cells, scores, strict=True):
        terms = jnp.exp(score - jnp.max(score, axis=0, keepdims=True))
        probs.append((terms * (1.0 / columns_sum(terms))).astype(low))
        p_ref[cell] = probs[-1]
    pieces = [own_head(t_dot(prob, v[cell])).astype(low) for cell, prob in zip(cells, probs, strict=True)]
    context = joined(pieces, count, seq_len)
    c_ref[...] = context
    hat, inv_std = norm_stats(x.astype(full) + dot(context, wo[...]) + line(bo))
    normed_low = (hat * line(gain) + line(shift)).astype(low)
    hat_ref[...] = hat
    inv_ref[...] = jnp.broadcast_to(inv_std, inv_ref.shape)
    nl_ref[...] = normed_low
    for s in range(count // seq_len):
        nll_ref[0, s : s + 1, :] = normed_low[s * seq_len : s * seq_len + 1, :].astype(full)
        hatl_ref[0, s : s + 1, :] = hat[s * seq_len : s * seq_len + 1, :]


def attention_forward(tokens, seq_len, wq, wk, wv, wo, *vectors):
    count = tokens.shape[0]
    rows = 256
    steps, leads = count // rows, rows // seq_len
    row, mat = pl.BlockSpec((rows, D), lambda i: (i, 0)), fixed_spec(D, D)
    lead = pl.BlockSpec((1, leads, D), lambda i: (i, 0, 0))
    return pl.pallas_call(
        functools.partial(attention_kernel, seq_len),
        grid=(steps,),
        in_specs=[row, mat, mat, mat, mat] + [vector_spec()] * 5,
        out_specs=[row] * 7 + [pl.BlockSpec((rows, LANES), lambda i: (i, 0)), lead, lead],
        out_shape=[far(count, D)] * 5
        + [far(count, D), far(count, D, dtype=full), far(count, LANES, dtype=full)]
        + [shape_of(steps, leads, D, dtype=full)] * 2,
        compiler_params=params(1, 20),
        name="attention_forward",
        cost_estimate=cost(10),
    )(tokens, wq, wk, wv, wo, *vectors)


def lead_kernel(nl_ref, hat_ref, uw, ub, dw, gain1, shift1, db, gain2, shift2,
                lead_ref, hat2_ref, inv2_ref, linv_ref, unit_ref, nl, acc):
    step = pl.program_id(0)

    @pl.when(step == 0)
    def _():
        hat = jnp.concatenate([hat_ref[k] for k in range(hat_ref.shape[0])], axis=0)
        nl[...] = jnp.concatenate([nl_ref[k] for k in range(nl_ref.shape[0])], axis=0).astype(low)
        acc[...] = hat * line(gain1) + line(shift1) + line(db)

    pre = dot(nl[...], uw[...]) + line(ub, step * (D // LANES))
    acc[...] += dot(gelu_and_slope(pre)[0].astype(low), dw[...])

    @pl.when(step == pl.num_programs(0) - 1)
    def _():
        hat, inv_std = norm_stats(acc[...])
        lead = hat * line(gain2) + line(shift2)
        lead_inv = lax.rsqrt(jnp.sum(lead * lead, axis=-1, keepdims=True) + UNIT_EPS)
        lead_ref[...] = lead
        hat2_ref[...] = hat
        inv2_ref[...] = jnp.broadcast_to(inv_std, inv2_ref.shape)
        linv_ref[...] = jnp.broadcast_to(lead_inv, linv_ref.shape)
        unit_ref[...] = (lead * lead_inv).astype(low)


def lead_forward(nl, hat, uw, ub, dw, *vectors):
    count = nl.shape[0] * nl.shape[1]
    hidden = uw.shape[1]
    row, lane = fixed_spec(count, D), fixed_spec(count, LANES)
    return pl.pallas_call(
        lead_kernel,
        grid=(hidden // D,),
        in_specs=[
            fixed_spec(*nl.shape), fixed_spec(*hat.shape),
            pl.BlockSpec((D, D), lambda j: (0, j)), vector_spec(hidden), pl.BlockSpec((D, D), lambda j: (j, 0)),
        ] + [vector_spec()] * 5,
        out_specs=[row, row, lane, lane, row],
        out_shape=[shape_of(count, D, dtype=full)] * 2
        + [shape_of(count, LANES, dtype=full)] * 2 + [shape_of(count, D)],
        scratch_shapes=[pltpu.VMEM((count, D), low), pltpu.VMEM((count, D), full)],
        compiler_params=params(1),
        name="lead_forward",
        cost_estimate=cost(3),
    )(nl, hat, uw, ub, dw, *vectors)


def ff_kernel(part, seq_len, nl_ref, uw, ub, dw, gain1, shift1, db, gain2, shift2, hat_far, up_far, *rest):
    out_ref, act_ref, slope_ref, dr2_ref, low_ref, sums_ref, leads_ref, acc, hat_ref, up_ref, sems = rest[-11:]
    step = pl.program_id(0)
    rows = acc.shape[0]
    span = pl.ds(part * rows, rows)
    copies = [
        pltpu.make_async_copy(source.at[span, :], target, sems.at[k])
        for k, (source, target) in enumerate(((hat_far, hat_ref), (up_far, up_ref)))
    ]

    @pl.when(step == 0)
    def _():
        for copy in copies:
            copy.start()
        acc[...] = jnp.zeros_like(acc)

    value, slope = gelu_and_slope(dot(nl_ref[...], uw[...]) + line(ub, step * (D // LANES)))
    act = value.astype(low)
    slope_ref[...] = slope.astype(low)
    act_ref[...] = act
    acc[...] += dot(act, dw[...])

    @pl.when(step == pl.num_programs(0) - 1)
    def _():
        for copy in copies:
            copy.wait()
        normed = hat_ref[...] * line(gain1) + line(shift1)
        hat, inv_std = norm_stats(acc[...] + (normed + line(db)))
        gain = line(gain2)
        out_ref[...] = (hat * gain + line(shift2)).astype(low)
        grad = up_ref[...].astype(full)
        dr2 = norm_back(grad * gain, hat, inv_std)
        dr2_ref[...] = dr2
        branch = dr2.astype(low)
        low_ref[...] = branch
        sums_ref[0, 0:1, :] = columns_sum(grad * hat)
        sums_ref[0, 1:2, :] = columns_sum(grad)
        sums_ref[0, 2:3, :] = columns_sum(branch.astype(full))
        for s in range(rows // seq_len):
            leads_ref[0, s : s + 1, :] = dr2[s * seq_len : s * seq_len + 1, :]


def ff_forward(part, parts, carried, seq_len, nl, hat, upstream, uw, ub, dw, *vectors):
    count = nl.shape[0]
    rows = count // parts
    hidden = uw.shape[1]
    row = pl.BlockSpec((rows, D), lambda j: (part, 0))
    wide = pl.BlockSpec((rows, D), lambda j: (part, j))
    anywhere = pl.BlockSpec(memory_space=pl.ANY)
    operands = [in_far(nl), uw, ub, dw, *vectors, in_far(hat), upstream]
    in_specs = [row, pl.BlockSpec((D, D), lambda j: (0, j)), vector_spec(hidden), pl.BlockSpec((D, D), lambda j: (j, 0))]
    in_specs += [vector_spec()] * 5 + [anywhere] * 2
    aliases = {}
    if carried is not None:
        aliases = {len(operands) + k: k for k in range(len(carried))}
        operands += list(carried)
        in_specs += [anywhere] * len(carried)
    sums = lambda tall: pl.BlockSpec((1, tall, D), lambda j: (part, 0, 0))
    return pl.pallas_call(
        functools.partial(ff_kernel, part, seq_len),
        grid=(hidden // D,),
        in_specs=in_specs,
        out_specs=[row, wide, wide, row, row, sums(8), sums(rows // seq_len)],
        scratch_shapes=[
            pltpu.VMEM((rows, D), full), pltpu.VMEM((rows, D), full), pltpu.VMEM((rows, D), low),
            pltpu.SemaphoreType.DMA((2,)),
        ],
        out_shape=[
            far(count, D), far(count, hidden), far(count, hidden),
            far(count, D, dtype=full), far(count, D), shape_of(parts, 8, D, dtype=full),
            shape_of(parts, rows // seq_len, D, dtype=full),
        ],
        input_output_aliases=aliases,
        compiler_params=params(1, 20),
        name=f"ff_forward_{part}",
        cost_estimate=cost(13),
    )(*operands)


def loss_kernel(seq_count, own_ref, other_ref, lead_ref, hat_ref, inv_ref, linv_ref, gain2, loss_ref, fix_ref, sums_ref):
    count = own_ref.shape[0]
    own, other = own_ref[:, :D], other_ref[:, :D]
    columns = own_ref[:, D : D + 1].astype(full)
    rows = dot_t(jnp.ones((8, LANES), low), own_ref[:, D:])[0:1] * (1.0 / LANES)
    same = columns == rows
    place = [lax.broadcasted_iota(jnp.int32, (count, count), axis) for axis in range(2)]
    diagonal = (place[0] == place[1]).astype(full)
    logits = LOGIT_SCALE * dot_t(own, other) - LOGIT_SCALE * MARGIN * diagonal
    masked = jnp.where(same, logits, -jnp.inf)
    col_top = jnp.max(masked, axis=0, keepdims=True)
    col_lse = col_top + jnp.log(columns_sum(jnp.exp(masked - col_top)))
    mine = masked[:seq_count]
    row_top = jnp.max(mine, axis=1, keepdims=True)
    row_lse = row_top + jnp.log(jnp.sum(jnp.exp(mine - row_top), axis=1, keepdims=True))
    mine_diag = diagonal[:seq_count]
    own_logit = jnp.sum(logits[:seq_count] * mine_diag, axis=1, keepdims=True)
    found = same.astype(full)
    row_weight = (count / GROUPS) / jnp.sum(found[:seq_count], axis=1, keepdims=True)
    col_weight = (count / GROUPS) / columns_sum(found)
    loss_ref[...] = jnp.broadcast_to(row_weight * (row_lse - own_logit), loss_ref.shape)
    dsims = row_weight * (jnp.exp(mine - row_lse) - mine_diag) + col_weight * (jnp.exp(mine - col_lse) - mine_diag)
    high = dsims.astype(low)
    rest = (dsims - high.astype(full)).astype(low)
    unit_grad = LOGIT_SCALE * (dot(high, other) + dot(rest, other))
    lead, lead_inv, hat = lead_ref[...], linv_ref[:, 0:1], hat_ref[...]
    cross = jnp.sum(lead * unit_grad, axis=-1, keepdims=True)
    lead_grad = lead_inv * unit_grad - lead_inv * lead_inv * lead_inv * cross * lead
    fix_ref[...] = norm_back(lead_grad * line(gain2), hat, inv_ref[:, 0:1])
    sums_ref[0:1, :] = columns_sum(lead_grad * hat)
    sums_ref[1:2, :] = columns_sum(lead_grad)


def pair_loss(own_side, other_side, lead, lead_hat, inv2, lead_inv, gain):
    seq_count = lead.shape[0]
    if own_side.shape[0] <= 512:
        loss, fix, sums = pl.pallas_call(
            functools.partial(loss_kernel, seq_count),
            out_shape=[
                shape_of(seq_count, LANES, dtype=full), shape_of(seq_count, D, dtype=full), shape_of(8, D, dtype=full)
            ],
            compiler_params=params(0),
            name="pair_loss",
            cost_estimate=cost(4),
        )(own_side, other_side, lead, lead_hat, inv2, lead_inv, in_far(gain.reshape(-1, LANES)))
        return loss[:, 0][None], fix, sums
    pairs_all = own_side.shape[0]
    groups = own_side[:, D].astype(full)
    same_group = groups[:, None] == groups[None, :]
    row_weight = pairs_all / GROUPS / jnp.sum(same_group.astype(full), axis=1)
    sim_scores = LOGIT_SCALE * jnp.einsum("id,jd->ij", own_side[:, :D], other_side[:, :D], preferred_element_type=full)
    place = jnp.arange(pairs_all, dtype=jnp.int32)
    diagonal = (place[:, None] == place[None, :]).astype(full)
    logits = sim_scores - LOGIT_SCALE * MARGIN * diagonal
    masked = jnp.where(same_group, logits, -jnp.inf)
    col_top = jnp.max(masked, axis=0, keepdims=True)
    col_lse = col_top + jnp.log(jnp.sum(jnp.exp(masked - col_top), axis=0, keepdims=True))
    own = masked[:seq_count]
    row_top = jnp.max(own, axis=1, keepdims=True)
    row_lse = row_top + jnp.log(jnp.sum(jnp.exp(own - row_top), axis=1, keepdims=True))
    own_diag = diagonal[:seq_count]
    own_logit = jnp.sum(logits[:seq_count] * own_diag, axis=1)
    loss_rows = (row_weight[:seq_count] * (row_lse[:, 0] - own_logit))[None]
    dsims = row_weight[:seq_count, None] * (jnp.exp(own - row_lse) - own_diag)
    dsims += row_weight[None, :] * (jnp.exp(own - col_lse) - own_diag)
    unit_grad = LOGIT_SCALE * jnp.dot(dsims, other_side[:, :D].astype(full), precision=highest)
    lead_inv = lead_inv[:, :1]
    cross = jnp.sum(lead * unit_grad, axis=-1, keepdims=True)
    lead_grad = lead_inv * unit_grad - lead_inv * lead_inv * lead_inv * cross * lead
    sums = jnp.stack([jnp.sum(lead_grad * lead_hat, axis=0), jnp.sum(lead_grad, axis=0)])
    return loss_rows, norm_back(lead_grad * gain[None], lead_hat, inv2[:, :1]), sums


def down_grad_kernel(seq_len, fresh, place, *refs):
    step = pl.program_id(0)
    if fresh:
        old_ref, leads_ref, fix_ref, act_ref, *outs, db_ref, sum_ref = refs

        @pl.when(step == 0)
        def _():
            db_ref[...] = old_ref[...]
            fixed = (leads_ref[...] + fix_ref[...]).astype(low)
            sum_ref[...] = columns_sum(fixed.astype(full) - leads_ref[...].astype(low).astype(full))
            for s in range(fix_ref.shape[0]):
                block = old_ref[s * seq_len : s * seq_len + 16, :]
                first = lax.broadcasted_iota(jnp.int32, block.shape, 0) == 0
                block = jnp.where(first, fixed[s : s + 1, :].astype(full), block.astype(full))
                db_ref[s * seq_len : s * seq_len + 16, :] = block.astype(low)
    else:
        db_ref, act_ref, *outs = refs
    grad = t_dot(act_ref[...], db_ref[...]).astype(low)
    tall = grad.shape[0]
    for rank in range(4):

        @pl.when(step == rank)
        def _(rank=rank):
            outs[rank // 2][rank % 2 * tall : (rank % 2 + 1) * tall, :] = grad


def down_gradient(place, first, act, dbranch, leads=None, fix=None, seq_len=None):
    count, hidden = act.shape
    tall = hidden // 8
    fresh = fix is not None
    operands = [dbranch] + ([leads, fix] if fresh else []) + [in_far(act)]
    moving = pl.BlockSpec((count, tall), lambda p, place: (0, place[first + p]))
    in_specs = [fixed_spec(*operand.shape) for operand in operands[:-1]] + [moving]
    out_specs = [fixed_spec(2 * tall, D)] * 2
    out_shape = [shape_of(2 * tall, D)] * 2
    if fresh:
        out_specs += [fixed_spec(count, D), fixed_spec(1, D)]
        out_shape += [shape_of(count, D), shape_of(1, D, dtype=full)]
    return pl.pallas_call(
        functools.partial(down_grad_kernel, seq_len, fresh),
        grid_spec=pltpu.PrefetchScalarGridSpec(
            num_scalar_prefetch=1, grid=(4,), in_specs=in_specs, out_specs=out_specs
        ),
        out_shape=out_shape,
        compiler_params=params(1),
        name=f"down_grad_{first}",
        cost_estimate=cost(4),
    )(place, *operands)


def put_rows(place, grad_ref, outs, columns):
    tall = grad_ref.shape[0] // 8
    for rank in range(8):
        at = pl.multiple_of(place[rank] * tall, 16)
        outs[rank // 2][rank % 2 * tall : (rank % 2 + 1) * tall, columns] = grad_ref[pl.ds(at, tall), :]


def hidden_kernel(place, db_ref, slope_ref, dw, nl_ref, *rest):
    dpre_ref, sum_ref, *outs, scratch = rest[-7:]
    dpre = (dot_t(db_ref[...], dw[...]) * slope_ref[...].astype(full)).astype(low)
    dpre_ref[...] = dpre
    sum_ref[0:1, :] = columns_sum(dpre.astype(full))
    scratch[...] = t_dot(nl_ref[...], dpre).astype(low)
    put_rows(place, scratch, outs, slice(None))


def hidden_gradient(place, part, parts, carried, dbranch, slope, dw, nl):
    count, hidden = slope.shape
    steps = hidden // D // parts
    wide = pl.BlockSpec((count, D), lambda j, *_: (0, part * steps + j))
    pair = D // 4
    operands = [dbranch, in_far(slope), dw, in_far(nl)]
    in_specs = [
        fixed_spec(count, D), wide, pl.BlockSpec((D, D), lambda j, *_: (part * steps + j, 0)), fixed_spec(count, D)
    ]
    aliases = {2: 0}
    if carried is not None:
        operands[1] = in_far(carried[0])
        aliases |= {5 + k: 1 + k for k in range(5)}
        operands += list(carried[1:])
        in_specs += [pl.BlockSpec(memory_space=pl.ANY)] * 5
    out_specs = [wide] + [
        pl.BlockSpec((rows, D), lambda j, *_: (0, part * steps + j)) for rows in (8, pair, pair, pair, pair)
    ]
    return pl.pallas_call(
        hidden_kernel,
        grid_spec=pltpu.PrefetchScalarGridSpec(
            num_scalar_prefetch=1,
            grid=(steps,),
            in_specs=in_specs,
            out_specs=out_specs,
            scratch_shapes=[pltpu.VMEM((D, D), low)],
        ),
        out_shape=[far(count, hidden), shape_of(8, hidden, dtype=full)] + [shape_of(pair, hidden)] * 4,
        input_output_aliases=aliases,
        compiler_params=params(1, 18),
        name=f"hidden_gradient_{part}",
        cost_estimate=cost(8),
    )(place, *operands)


def norm_one_kernel(seq_len, dpre_ref, fix_ref, uw, wo, gain1, dr2_far, hat_far, inv_ref,
                    dr1_ref, datt_ref, dctx_ref, sums_ref, acc, dr2_ref, hat_ref, sems):
    step = pl.program_id(0)
    copies = [
        pltpu.make_async_copy(source, target, sems.at[k])
        for k, (source, target) in enumerate(((dr2_far, dr2_ref), (hat_far, hat_ref)))
    ]

    @pl.when(step == 0)
    def _():
        for copy in copies:
            copy.start()
        acc[...] = jnp.zeros_like(acc)

    acc[...] += dot_t(dpre_ref[...], uw[...])

    @pl.when(step == pl.num_programs(0) - 1)
    def _():
        for copy in copies:
            copy.wait()
        gain = line(gain1)
        totals = [jnp.zeros((1, D), full)] * 3
        for start in range(0, acc.shape[0], 256):
            rows = slice(start, start + 256)
            pieces = []
            for s in range(start // seq_len, (start + 256) // seq_len):
                block = dr2_ref[s * seq_len : (s + 1) * seq_len, :]
                first = lax.broadcasted_iota(jnp.int32, block.shape, 0) == 0
                pieces.append(block + jnp.where(first, fix_ref[s : s + 1, :], 0.0))
            grad, hat = acc[rows, :] + jnp.concatenate(pieces, axis=0), hat_ref[rows, :]
            dr1 = norm_back(grad * gain, hat, inv_ref[rows, 0:1])
            dr1_ref[rows, :] = dr1
            datt = dr1.astype(low)
            datt_ref[0, rows, :] = datt
            dctx_ref[rows, :] = dot_t(datt, wo[...]).astype(low)
            totals = [
                total + columns_sum(part) for total, part in zip(totals, (grad * hat, grad, datt.astype(full)), strict=True)
            ]
        for rank, total in enumerate(totals):
            sums_ref[rank : rank + 1, :] = total


def norm_one_backward(dpre, dr2, fix, seq_len, hat, inv, uw, wo, gain1):
    count, hidden = dpre.shape
    anywhere = pl.BlockSpec(memory_space=pl.ANY)
    return pl.pallas_call(
        functools.partial(norm_one_kernel, seq_len),
        grid=(hidden // D,),
        in_specs=[
            pl.BlockSpec((count, D), lambda j: (0, j)), fixed_spec(*fix.shape), pl.BlockSpec((D, D), lambda j: (0, j)),
            fixed_spec(D, D), vector_spec(), anywhere, anywhere, fixed_spec(count, LANES),
        ],
        out_specs=[fixed_spec(count, D), pl.BlockSpec((1, count, D), lambda j: (3, 0, 0)), fixed_spec(count, D), fixed_spec(8, D)],
        out_shape=[far(count, D, dtype=full), far(4, count, D), far(count, D), shape_of(8, D, dtype=full)],
        scratch_shapes=[pltpu.VMEM((count, D), full)] * 3 + [pltpu.SemaphoreType.DMA((2,))],
        compiler_params=params(1, 30),
        name="norm_one_backward",
        cost_estimate=cost(13),
    )(in_far(dpre), fix, uw, wo, gain1, in_far(dr2), in_far(hat), in_far(inv))


def attention_back_kernel(seq_len, q_ref, k_ref, v_ref, p_ref, dc_ref, stack_ref, d_ref, sums):
    q, k, v, probs, dctx = (ref[...] for ref in (q_ref, k_ref, v_ref, p_ref, dc_ref))
    count = q.shape[0]
    cells = cells_of(count, seq_len)
    factor = 1.0 / math.sqrt(HD)
    spread_dctx = [two_heads(dctx[cell]) for cell in cells]
    dprobs = [dot_t(v[cell], wide) for cell, wide in zip(cells, spread_dctx, strict=True)]
    dvals = [dot(probs[cell], wide).astype(low) for cell, wide in zip(cells, spread_dctx, strict=True)]
    dscores = []
    for cell, dprob in zip(cells, dprobs, strict=True):
        prob = probs[cell].astype(full)
        dscores.append((prob * (dprob - columns_sum(prob * dprob))).astype(low))
    dkeys = [(dot(ds, two_heads(q[cell])) * factor).astype(low) for cell, ds in zip(cells, dscores, strict=True)]
    dqueries = [(own_head(t_dot(ds, k[cell])) * factor).astype(low) for cell, ds in zip(cells, dscores, strict=True)]

    @pl.when(pl.program_id(0) == 0)
    def _():
        sums[...] = jnp.zeros_like(sums)

    for rank, pieces in enumerate((dqueries, dkeys, dvals)):
        grad = joined(pieces, count, seq_len)
        d_ref[rank] = grad
        sums[rank : rank + 1, :] += columns_sum(grad.astype(full))


def attention_backward(seq_len, q, k, v, probs, dctx, stack):
    count = q.shape[0]
    rows = 256
    row = pl.BlockSpec((rows, D), lambda i: (i, 0))
    return pl.pallas_call(
        functools.partial(attention_back_kernel, seq_len),
        grid=(count // rows,),
        in_specs=[row] * 5 + [pl.BlockSpec(memory_space=pl.ANY)],
        out_specs=[pl.BlockSpec((3, rows, D), lambda i: (0, i, 0)), fixed_spec(8, D)],
        out_shape=[far(4, count, D), shape_of(8, D, dtype=full)],
        input_output_aliases={5: 0},
        compiler_params=params(1, 14),
        name="attention_backward",
        cost_estimate=cost(8),
    )(*map(in_far, (q, k, v, probs, dctx, stack)))


def square_grad_kernel(place, c_ref, d_ref, x_far, small_ref, *rest):
    outs, x_ref, scratch, sem = rest[:4], rest[4], rest[5], rest[6]
    step = pl.program_id(0)
    copy = pltpu.make_async_copy(x_far, x_ref, sem)

    @pl.when(step == 0)
    def _():
        copy.start()
        scratch[...] = t_dot(c_ref[...], d_ref[0]).astype(low)
        tall = D // 8
        for rank in range(8):
            out_ref, first = outs[rank // 2], rank % 2 * tall
            out_ref[first : first + tall, 4 * D :] = jnp.zeros((tall, LANES), low)

            @pl.when(place[rank] == 0)
            def _(out_ref=out_ref, first=first):
                out_ref[first : first + small_ref.shape[0], 4 * D :] = small_ref[...].astype(low)

    @pl.when(step == 1)
    def _():
        copy.wait()

    @pl.when(step > 0)
    def _():
        scratch[...] = t_dot(x_ref[...], d_ref[0]).astype(low)

    put_rows(place, scratch, outs, pl.ds(pl.multiple_of((3 - step) * D, LANES), D))


def square_gradient(place, tokens, context, stack, small):
    count = tokens.shape[0]
    pair, columns = D // 4, 4 * D + LANES
    return pl.pallas_call(
        square_grad_kernel,
        grid_spec=pltpu.PrefetchScalarGridSpec(
            num_scalar_prefetch=1,
            grid=(4,),
            in_specs=[
                fixed_spec(count, D), pl.BlockSpec((1, count, D), lambda j, *_: (3 - j, 0, 0)),
                pl.BlockSpec(memory_space=pl.ANY), fixed_spec(*small.shape),
            ],
            out_specs=[fixed_spec(pair, columns)] * 4,
            scratch_shapes=[pltpu.VMEM((count, D), low), pltpu.VMEM((D, D), low), pltpu.SemaphoreType.DMA],
        ),
        out_shape=[shape_of(pair, columns)] * 4,
        compiler_params=params(1, 18),
        name="square_gradient",
        cost_estimate=cost(12),
    )(place, *map(in_far, (context, stack, tokens)), small)


def input_grad_kernel(dr1_ref, d_ref, wq, wk, wv, out_ref):
    out_ref[...] = dr1_ref[...] + dot_t(d_ref[0], wq[...]) + dot_t(d_ref[1], wk[...]) + dot_t(d_ref[2], wv[...])


def input_gradient(dr1, stack, wq, wk, wv):
    count = dr1.shape[0]
    rows = 256
    row, mat = pl.BlockSpec((rows, D), lambda i: (i, 0)), fixed_spec(D, D)
    return pl.pallas_call(
        input_grad_kernel,
        grid=(count // rows,),
        in_specs=[row, pl.BlockSpec((3, rows, D), lambda i: (0, i, 0))] + [mat] * 3,
        out_specs=row,
        out_shape=far(count, D, dtype=full),
        compiler_params=params(1),
        name="input_gradient",
        cost_estimate=cost(6),
    )(in_far(dr1), in_far(stack), wq, wk, wv)


def spread_kernel(widths, talls, first, place, *refs):
    smalls = refs[len(refs) - len(talls) :]
    outs = refs[len(refs) - len(talls) - len(widths) : len(refs) - len(talls)]
    tall = outs[0].shape[0]
    held = refs[0].shape[0] // tall
    if first and talls:

        @pl.when(pl.program_id(0) == 0)
        def _():
            for ref, old in zip(smalls, refs[4 // held : 4 // held + len(talls)], strict=True):
                ref[...] = old[...]

    for rank in range(4):

        @pl.when(pl.program_id(0) == rank)
        def _(rank=rank):
            source, rows = refs[rank // held], rank % held * tall
            at = 0
            for ref, width in zip(outs, widths, strict=True):
                ref[...] = source[rows : rows + tall, at : at + width].astype(full)
                at += width
            if talls:

                @pl.when(place[first + rank] == 0)
                def _():
                    top = rows
                    for ref in smalls:
                        ref[...] = source[top : top + ref.shape[0], at:].astype(full)
                        top += ref.shape[0]


def spread(place, first, pairs, widths, talls, carried, name):
    tall = sum(pair.shape[0] for pair in pairs) // 4
    carried = list(carried or [])
    small = [fixed_spec(rows, LANES) for rows in talls]
    in_specs = [fixed_spec(*pair.shape) for pair in pairs]
    operands = list(pairs)
    if carried:
        operands += carried[len(widths) :] + carried[: len(widths)]
        in_specs += small + [pl.BlockSpec(memory_space=pl.ANY)] * len(widths)
    return pl.pallas_call(
        functools.partial(spread_kernel, widths, talls, first),
        grid_spec=pltpu.PrefetchScalarGridSpec(
            num_scalar_prefetch=1,
            grid=(4,),
            in_specs=in_specs,
            out_specs=[pl.BlockSpec((tall, width), lambda p, place: (place[first + p], 0)) for width in widths] + small,
        ),
        out_shape=[far(8 * tall, width, dtype=full) for width in widths]
        + [shape_of(rows, LANES, dtype=full) for rows in talls],
        input_output_aliases={1 + len(operands) - len(widths) + k: k for k in range(len(widths))} if carried else {},
        compiler_params=params(1),
        name=f"{name}_spread_{first}",
        cost_estimate=cost(3),
    )(place, *operands)


def places():
    half = lax.axis_index("stream")
    chip = lax.axis_index("dp")
    bits = (chip & 1, (chip >> 1) & 1)
    table = []
    for side in (half, 1 - half):
        first = jnp.where(side == 0, bits[0], bits[1])
        second = jnp.where(side == 0, bits[1], bits[0])
        table += [4 * side + 2 * (first ^ (k >> 1)) + (second ^ (k & 1)) for k in range(4)]
    return jnp.stack(table).astype(jnp.int32)


def chip_partner(bit_zero, bit_one):
    chips = lax.axis_size("dp")
    return [
        (half * chips + chip, half * chips + (chip ^ (bit_zero if half == 0 else bit_one)))
        for half in range(2)
        for chip in range(chips)
    ]


def core_partner():
    chips = lax.axis_size("dp")
    return [(half * chips + chip, (1 - half) * chips + chip) for half in range(2) for chip in range(chips)]


def swap(piece, pairs):
    return lax.ppermute(piece, ("stream", "dp"), pairs)


def add_low(left, right):
    return (left.astype(full) + right.astype(full)).astype(low)


def tie(value, after):
    return value if after is None else lax.optimization_barrier((value, after))[0]


def all_sum(sent):
    others = [swap(pair, core_partner()) for pair in sent]
    kept = yield sent
    pair = add_low(kept[1], others[1])
    other = swap(pair, chip_partner(1, 2))
    mine = add_low(kept[0], others[0])
    after = yield pair
    tall = mine.shape[0] // 2
    mine = tie(mine, after)
    block = add_low(mine[tall:], other[tall:])
    mine = add_low(mine[:tall], other[:tall])
    other = swap(block, chip_partner(2, 1))
    after = yield block
    bits = [1 << k for k in range(2, lax.axis_size("dp").bit_length() - 1)]
    for rank, pair in enumerate(zip(bits, bits[::-1], strict=True)):
        mine = add_low(tie(mine, after), other)
        other = swap(mine, chip_partner(*pair))
        after = (yield mine) if rank in (0, len(bits) - 1) else None
    mine = add_low(tie(mine, after), other)
    other = swap(mine, chip_partner(2, 1))
    after = yield mine
    pair = jnp.concatenate([tie(mine, after), other])
    other = swap(pair, chip_partner(1, 2))
    after = yield pair
    pairs = [tie(pair, after), other]
    others = [swap(each, core_partner()) for each in pairs]
    yield pairs
    yield others


def gather_rows(rows):
    chips = lax.axis_size("dp")
    bit = 1
    after = None
    while bit < chips:
        others = [swap(rows, chip_partner(k * bit, k * bit)) for k in range(1, 4) if k * bit < chips]
        after = yield rows
        rows = jnp.concatenate([tie(rows, after)] + others)
        bit *= 4
    other = swap(rows, core_partner())
    yield rows
    yield rows, other


def in_far(array):
    return pltpu.with_memory_space_constraint(array, pltpu.HBM)


def shards(
    layer_input, pair_group, query_weight, query_bias, key_weight, value_weight, value_bias,
    out_weight, out_bias, mixer_gain, mixer_shift, up_weight, up_bias, down_weight, down_bias,
    final_gain, final_shift, upstream,
):
    count = layer_input.shape[1]
    seq_count = pair_group.shape[0]
    seq_len = count // seq_count
    hidden = up_bias.shape[0]
    tokens, upstream = in_far(layer_input[0]), in_far(upstream[0])
    wq, wk, wv, wo = map(in_far, (query_weight, key_weight, value_weight, out_weight))
    uw, dw = in_far(up_weight), in_far(down_weight)
    fold = lambda vector: in_far(vector.reshape(-1, LANES))
    bq, bv, bo, g1, s1 = map(fold, (query_bias, value_bias, out_bias, mixer_gain, mixer_shift))
    ub, db, g2, s2 = map(fold, (up_bias, down_bias, final_gain, final_shift))
    place = places()

    q, k, v, probs, context, nl, hat, inv, lead_nl, lead_hat = attention_forward(
        tokens, seq_len, wq, wk, wv, wo, bq, bv, bo, g1, s1
    )
    lead, lead_hat, lead_inv2, lead_inv, units = lead_forward(lead_nl, lead_hat, uw, ub, dw, g1, s1, db, g2, s2)
    ids = jnp.broadcast_to(pair_group.astype(low)[:, None], (seq_count, LANES))
    hops = gather_rows(jnp.concatenate([units, ids], axis=1))
    sent = next(hops)
    parts = 2
    carried = None
    for part in range(parts):
        carried = ff_forward(
            part, parts, carried, seq_len, tie(nl, sent), hat, upstream, uw, ub, dw, g1, s1, db, g2, s2
        )
        sent = hops.send(carried[5])
    while not isinstance(sent, tuple):
        sent = hops.send(None)
    layer_output, act, slope, dr2, dbranch, final_sums, dr2_leads = carried
    loss_rows, fix, lead_sums = pair_loss(*sent, lead, lead_hat, lead_inv2, lead_inv, final_gain)

    *down_sent, dbranch, down_sum = down_gradient(place, 4, act, dbranch, dr2_leads.reshape(-1, D), fix, seq_len)
    sent = down_sent
    talls = [hidden // LANES] + [D // LANES] * 8
    down = all_sum(down_sent)
    next(down)
    down_kept = down_gradient(place, 0, act, tie(dbranch, sent))
    sent = down_kept
    sent = down.send(tie(down_kept, sent))
    dpre, up_sums, *up_blocks = hidden_gradient(place, 0, 1, None, tie(dbranch, sent), slope, dw, nl)
    sent = dpre
    sent = down.send(sent)
    up = all_sum(up_blocks[2:])
    next(up)
    sent = (sent, up_blocks[2:])
    dr1, stack, dctx, mixer = norm_one_backward(tie(dpre, sent), dr2, fix, seq_len, hat, inv, uw, wo, g1)
    sent = dctx
    sent = up.send(tie(up_blocks[:2], sent))
    sent = down.send(sent)
    stack, qkv = attention_backward(seq_len, q, k, v, probs, tie(dctx, sent), stack)
    sent = stack
    final = jnp.sum(final_sums, axis=0)
    small = jnp.concatenate(
        [
            up_sums[0], mixer[2], mixer[0], mixer[1], final[2] + down_sum[0], final[0] + lead_sums[0],
            final[1] + lead_sums[1], qkv[0], qkv[2],
        ]
    ).reshape(-1, LANES)
    square_blocks = square_gradient(place, tokens, context, tie(stack, sent), small)
    sent = square_blocks[2]
    sent = down.send(sent)
    sent = up.send(sent)
    square = all_sum(square_blocks[2:])
    next(square)
    sent = (sent, square_blocks[2:])
    sent = square.send(tie(square_blocks[:2], sent))
    sent = up.send(sent)
    input_grad = input_gradient(tie(dr1, sent), stack, wq, wk, wv)
    sent = input_grad
    sent = down.send(sent)
    sent = square.send(sent)
    sent = up.send(sent)
    sent = down.send(sent)
    sent = square.send(sent)
    sent = up.send(sent)
    down_own = down.send(sent)
    sent = down_own
    sent = square.send(sent)
    sent = up.send(sent)
    down_out = spread(place, 0, tie(down_own, sent), [D], [], None, "down")
    sent = down_out
    sent = square.send(sent)
    up_own = up.send(sent)
    sent = up_own
    sent = square.send(sent)
    up_out = spread(place, 0, tie(up_own, sent), [hidden], [], None, "up")
    sent = up_out
    up_out = spread(place, 4, up.send(sent), [hidden], [], up_out, "up")
    sent = up_out
    down_out = spread(place, 4, down.send(sent), [D], [], down_out, "down")
    sent = down_out
    square_own = square.send(sent)
    sent = square_own
    squares = spread(place, 0, tie(square_own, sent), [D] * 4, talls, None, "square")
    sent = squares
    squares = spread(place, 4, square.send(sent), [D] * 4, talls, squares, "square")
    wq_grad, wk_grad, wv_grad, wo_grad, *smalls = squares
    up_b, out_b, gain_one, shift_one, down_b, gain_two, shift_two, query_b, value_b = (each.reshape(-1) for each in smalls)
    return (
        layer_output[None], input_grad[None], loss_rows,
        wq_grad, query_b, wk_grad, wv_grad, value_b, wo_grad, out_b,
        gain_one, shift_one, up_out[0], up_b, down_out[0], down_b, gain_two, shift_two,
    )


def solution(mesh):
    split = P("stream", "dp", None)
    return jax.shard_map(
        shards,
        mesh=mesh,
        in_specs=(split, P("dp")) + (P(),) * 15 + (split,),
        out_specs=(split, split, P("stream", "dp")) + (P(),) * 15,
        check_vma=False,
    )
```

```python
import functools
import math

import jax
import jax.numpy as jnp
from jax import lax
from jax.experimental import pallas as pl
from jax.experimental.pallas import tpu as pltpu
from jax.sharding import PartitionSpec as P

D = 768
HEADS = 12
HD = 64
GROUPS = 109
LANES = 128

MARGIN = 0.3
LOGIT_SCALE = 30.0
NORM_EPS = 1e-12
UNIT_EPS = 1e-06
highest = lax.Precision.HIGHEST
low = jnp.bfloat16
full = jnp.float32


def dot(left, right):
    return lax.dot_general(left, right, (((1,), (0,)), ((), ())), preferred_element_type=full)


def dot_t(left, right):
    return lax.dot_general(left, right, (((1,), (1,)), ((), ())), preferred_element_type=full)


def t_dot(left, right):
    return lax.dot_general(left, right, (((0,), (0,)), ((), ())), preferred_element_type=full)


def mean_of(values):
    return jnp.sum(values, axis=-1, keepdims=True) * (1.0 / D)


def norm_stats(values):
    centred = values - mean_of(values)
    inv_std = lax.rsqrt(mean_of(centred * centred) + NORM_EPS)
    return centred * inv_std, inv_std


def norm_back(grad_hat, normed_hat, inv_std):
    return inv_std * (grad_hat - mean_of(grad_hat) - normed_hat * mean_of(grad_hat * normed_hat))


def normal_cdf(values):
    bell = jnp.exp(-0.5 * values * values)
    step = 1.0 / (1.0 + (0.3275911 / math.sqrt(2.0)) * jnp.abs(values))
    tail = 0.5 * 1.061405429
    for factor in (-1.453152027, 1.421413741, -0.284496736, 0.254829592):
        tail = tail * step + 0.5 * factor
    tail = tail * step * bell
    return jnp.where(values >= 0.0, 1.0 - tail, tail), bell


def gelu_and_slope(values):
    cdf, bell = normal_cdf(values)
    return values * cdf, cdf + values * bell * (1.0 / math.sqrt(2.0 * math.pi))


def columns_sum(values):
    return jnp.sum(values, axis=0, keepdims=True)


def line(ref, first=0):
    return jnp.concatenate([ref[pl.ds(first + k, 1), :] for k in range(D // LANES)], axis=1)


def fixed_spec(*shape):
    return pl.BlockSpec(shape, lambda *_: (0,) * len(shape))


def vector_spec(count=D):
    return fixed_spec(count // LANES, LANES)


def shape_of(*shape, dtype=low):
    return jax.ShapeDtypeStruct(shape, dtype)


def far(*shape, dtype=low):
    return pltpu.HBM(shape, dtype)


def params(grid_dims, mib=20):
    return pltpu.CompilerParams(dimension_semantics=("arbitrary",) * grid_dims, vmem_limit_bytes=mib << 20)


def cost(micros):
    return pl.CostEstimate(flops=int(micros * 0.02 * 1.15e9), bytes_accessed=1000, transcendentals=0)


def two_heads(block):
    lane = lax.broadcasted_iota(jnp.int32, block.shape, 1)
    zero = jnp.zeros_like(block)
    return jnp.concatenate([jnp.where(lane < HD, block, zero), jnp.where(lane < HD, zero, block)], axis=0)


def own_head(both):
    count = both.shape[0] // 2
    lane = lax.broadcasted_iota(jnp.int32, (count, both.shape[1]), 1)
    return jnp.where(lane < HD, both[:count], both[count:])


def cells_of(count, seq_len):
    return [
        (slice(start, start + seq_len), slice(first, first + 2 * HD))
        for first in range(0, D, 2 * HD)
        for start in range(0, count, seq_len)
    ]


def joined(pieces, count, seq_len):
    tall = count // seq_len
    columns = [jnp.concatenate(pieces[k : k + tall], axis=0) for k in range(0, len(pieces), tall)]
    return jnp.concatenate(columns, axis=1)


def attention_kernel(seq_len, x_ref, wq, wk, wv, wo, bq, bv, bo, gain, shift,
                     q_ref, k_ref, v_ref, p_ref, c_ref, nl_ref, hat_ref, inv_ref, nll_ref, hatl_ref):
    x = x_ref[...]
    count = x.shape[0]
    q = (dot(x, wq[...]) + line(bq)).astype(low)
    k = dot(x, wk[...]).astype(low)
    v = (dot(x, wv[...]) + line(bv)).astype(low)
    q_ref[...], k_ref[...], v_ref[...] = q, k, v
    cells = cells_of(count, seq_len)
    factor = 1.0 / math.sqrt(HD)
    scores = [dot_t(k[cell], two_heads(q[cell])) * factor for cell in cells]
    probs = []
    for cell, score in zip(cells, scores, strict=True):
        terms = jnp.exp(score - jnp.max(score, axis=0, keepdims=True))
        probs.append((terms * (1.0 / columns_sum(terms))).astype(low))
        p_ref[cell] = probs[-1]
    pieces = [own_head(t_dot(prob, v[cell])).astype(low) for cell, prob in zip(cells, probs, strict=True)]
    context = joined(pieces, count, seq_len)
    c_ref[...] = context
    hat, inv_std = norm_stats(x.astype(full) + dot(context, wo[...]) + line(bo))
    normed_low = (hat * line(gain) + line(shift)).astype(low)
    hat_ref[...] = hat
    inv_ref[...] = jnp.broadcast_to(inv_std, inv_ref.shape)
    nl_ref[...] = normed_low
    for s in range(count // seq_len):
        nll_ref[0, s : s + 1, :] = normed_low[s * seq_len : s * seq_len + 1, :].astype(full)
        hatl_ref[0, s : s + 1, :] = hat[s * seq_len : s * seq_len + 1, :]


def attention_forward(tokens, seq_len, wq, wk, wv, wo, *vectors):
    count = tokens.shape[0]
    rows = 256
    steps, leads = count // rows, rows // seq_len
    row, mat = pl.BlockSpec((rows, D), lambda i: (i, 0)), fixed_spec(D, D)
    lead = pl.BlockSpec((1, leads, D), lambda i: (i, 0, 0))
    return pl.pallas_call(
        functools.partial(attention_kernel, seq_len),
        grid=(steps,),
        in_specs=[row, mat, mat, mat, mat] + [vector_spec()] * 5,
        out_specs=[row] * 7 + [pl.BlockSpec((rows, LANES), lambda i: (i, 0)), lead, lead],
        out_shape=[far(count, D)] * 5
        + [far(count, D), far(count, D, dtype=full), far(count, LANES, dtype=full)]
        + [shape_of(steps, leads, D, dtype=full)] * 2,
        compiler_params=params(1, 20),
        name="attention_forward",
        cost_estimate=cost(10),
    )(tokens, wq, wk, wv, wo, *vectors)


def lead_kernel(nl_ref, hat_ref, uw, ub, dw, gain1, shift1, db, gain2, shift2,
                lead_ref, hat2_ref, inv2_ref, linv_ref, unit_ref, nl, acc):
    step = pl.program_id(0)

    @pl.when(step == 0)
    def _():
        hat = jnp.concatenate([hat_ref[k] for k in range(hat_ref.shape[0])], axis=0)
        nl[...] = jnp.concatenate([nl_ref[k] for k in range(nl_ref.shape[0])], axis=0).astype(low)
        acc[...] = hat * line(gain1) + line(shift1) + line(db)

    pre = dot(nl[...], uw[...]) + line(ub, step * (D // LANES))
    acc[...] += dot(gelu_and_slope(pre)[0].astype(low), dw[...])

    @pl.when(step == pl.num_programs(0) - 1)
    def _():
        hat, inv_std = norm_stats(acc[...])
        lead = hat * line(gain2) + line(shift2)
        lead_inv = lax.rsqrt(jnp.sum(lead * lead, axis=-1, keepdims=True) + UNIT_EPS)
        lead_ref[...] = lead
        hat2_ref[...] = hat
        inv2_ref[...] = jnp.broadcast_to(inv_std, inv2_ref.shape)
        linv_ref[...] = jnp.broadcast_to(lead_inv, linv_ref.shape)
        unit_ref[...] = (lead * lead_inv).astype(low)


def lead_forward(nl, hat, uw, ub, dw, *vectors):
    count = nl.shape[0] * nl.shape[1]
    hidden = uw.shape[1]
    row, lane = fixed_spec(count, D), fixed_spec(count, LANES)
    return pl.pallas_call(
        lead_kernel,
        grid=(hidden // D,),
        in_specs=[
            fixed_spec(*nl.shape), fixed_spec(*hat.shape),
            pl.BlockSpec((D, D), lambda j: (0, j)), vector_spec(hidden), pl.BlockSpec((D, D), lambda j: (j, 0)),
        ] + [vector_spec()] * 5,
        out_specs=[row, row, lane, lane, row],
        out_shape=[shape_of(count, D, dtype=full)] * 2
        + [shape_of(count, LANES, dtype=full)] * 2 + [shape_of(count, D)],
        scratch_shapes=[pltpu.VMEM((count, D), low), pltpu.VMEM((count, D), full)],
        compiler_params=params(1),
        name="lead_forward",
        cost_estimate=cost(3),
    )(nl, hat, uw, ub, dw, *vectors)


def ff_kernel(part, seq_len, nl_ref, uw, ub, dw, gain1, shift1, db, gain2, shift2, hat_far, up_far, *rest):
    out_ref, act_ref, slope_ref, low_ref, sums_ref, leads_ref, acc, hat_ref, up_ref, sems = rest[-10:]
    step = pl.program_id(0)
    rows = acc.shape[0]
    span = pl.ds(part * rows, rows)
    copies = [
        pltpu.make_async_copy(source.at[span, :], target, sems.at[k])
        for k, (source, target) in enumerate(((hat_far, hat_ref), (up_far, up_ref)))
    ]

    @pl.when(step == 0)
    def _():
        for copy in copies:
            copy.start()
        acc[...] = jnp.zeros_like(acc)

    value, slope = gelu_and_slope(dot(nl_ref[...], uw[...]) + line(ub, step * (D // LANES)))
    act = value.astype(low)
    slope_ref[...] = slope.astype(low)
    act_ref[...] = act
    acc[...] += dot(act, dw[...])

    @pl.when(step == pl.num_programs(0) - 1)
    def _():
        for copy in copies:
            copy.wait()
        normed = hat_ref[...] * line(gain1) + line(shift1)
        hat, inv_std = norm_stats(acc[...] + (normed + line(db)))
        gain = line(gain2)
        out_ref[...] = (hat * gain + line(shift2)).astype(low)
        grad = up_ref[...].astype(full)
        dr2 = norm_back(grad * gain, hat, inv_std)
        branch = dr2.astype(low)
        low_ref[...] = branch
        sums_ref[0, 0:1, :] = columns_sum(grad * hat)
        sums_ref[0, 1:2, :] = columns_sum(grad)
        sums_ref[0, 2:3, :] = columns_sum(branch.astype(full))
        for s in range(rows // seq_len):
            leads_ref[0, s : s + 1, :] = dr2[s * seq_len : s * seq_len + 1, :]


def ff_forward(part, parts, carried, seq_len, nl, hat, upstream, uw, ub, dw, *vectors):
    count = nl.shape[0]
    rows = count // parts
    hidden = uw.shape[1]
    row = pl.BlockSpec((rows, D), lambda j: (part, 0))
    wide = pl.BlockSpec((rows, D), lambda j: (part, j))
    anywhere = pl.BlockSpec(memory_space=pl.ANY)
    operands = [in_far(nl), uw, ub, dw, *vectors, in_far(hat), upstream]
    in_specs = [row, pl.BlockSpec((D, D), lambda j: (0, j)), vector_spec(hidden), pl.BlockSpec((D, D), lambda j: (j, 0))]
    in_specs += [vector_spec()] * 5 + [anywhere] * 2
    aliases = {}
    if carried is not None:
        aliases = {len(operands) + k: k for k in range(len(carried))}
        operands += list(carried)
        in_specs += [anywhere] * len(carried)
    sums = lambda tall: pl.BlockSpec((1, tall, D), lambda j: (part, 0, 0))
    return pl.pallas_call(
        functools.partial(ff_kernel, part, seq_len),
        grid=(hidden // D,),
        in_specs=in_specs,
        out_specs=[row, wide, wide, row, sums(8), sums(rows // seq_len)],
        scratch_shapes=[
            pltpu.VMEM((rows, D), full), pltpu.VMEM((rows, D), full), pltpu.VMEM((rows, D), low),
            pltpu.SemaphoreType.DMA((2,)),
        ],
        out_shape=[
            far(count, D), far(count, hidden), far(count, hidden),
            far(count, D), shape_of(parts, 8, D, dtype=full),
            shape_of(parts, rows // seq_len, D, dtype=full),
        ],
        input_output_aliases=aliases,
        compiler_params=params(1, 20),
        name=f"ff_forward_{part}",
        cost_estimate=cost(13),
    )(*operands)


def loss_kernel(seq_count, own_ref, other_ref, lead_ref, hat_ref, inv_ref, linv_ref, gain2, loss_ref, fix_ref, sums_ref):
    count = own_ref.shape[0]
    own, other = own_ref[:, :D], other_ref[:, :D]
    columns = own_ref[:, D : D + 1].astype(full)
    rows = dot_t(jnp.ones((8, LANES), low), own_ref[:, D:])[0:1] * (1.0 / LANES)
    same = columns == rows
    place = [lax.broadcasted_iota(jnp.int32, (count, count), axis) for axis in range(2)]
    diagonal = (place[0] == place[1]).astype(full)
    logits = LOGIT_SCALE * dot_t(own, other) - LOGIT_SCALE * MARGIN * diagonal
    masked = jnp.where(same, logits, -jnp.inf)
    col_top = jnp.max(masked, axis=0, keepdims=True)
    col_lse = col_top + jnp.log(columns_sum(jnp.exp(masked - col_top)))
    mine = masked[:seq_count]
    row_top = jnp.max(mine, axis=1, keepdims=True)
    row_lse = row_top + jnp.log(jnp.sum(jnp.exp(mine - row_top), axis=1, keepdims=True))
    mine_diag = diagonal[:seq_count]
    own_logit = jnp.sum(logits[:seq_count] * mine_diag, axis=1, keepdims=True)
    found = same.astype(full)
    row_weight = (count / GROUPS) / jnp.sum(found[:seq_count], axis=1, keepdims=True)
    col_weight = (count / GROUPS) / columns_sum(found)
    loss_ref[...] = jnp.broadcast_to(row_weight * (row_lse - own_logit), loss_ref.shape)
    dsims = row_weight * (jnp.exp(mine - row_lse) - mine_diag) + col_weight * (jnp.exp(mine - col_lse) - mine_diag)
    high = dsims.astype(low)
    rest = (dsims - high.astype(full)).astype(low)
    unit_grad = LOGIT_SCALE * (dot(high, other) + dot(rest, other))
    lead, lead_inv, hat = lead_ref[...], linv_ref[:, 0:1], hat_ref[...]
    cross = jnp.sum(lead * unit_grad, axis=-1, keepdims=True)
    lead_grad = lead_inv * unit_grad - lead_inv * lead_inv * lead_inv * cross * lead
    fix_ref[...] = norm_back(lead_grad * line(gain2), hat, inv_ref[:, 0:1])
    sums_ref[0:1, :] = columns_sum(lead_grad * hat)
    sums_ref[1:2, :] = columns_sum(lead_grad)


def pair_loss(own_side, other_side, lead, lead_hat, inv2, lead_inv, gain):
    seq_count = lead.shape[0]
    if own_side.shape[0] <= 512:
        loss, fix, sums = pl.pallas_call(
            functools.partial(loss_kernel, seq_count),
            out_shape=[
                shape_of(seq_count, LANES, dtype=full), shape_of(seq_count, D, dtype=full), shape_of(8, D, dtype=full)
            ],
            compiler_params=params(0),
            name="pair_loss",
            cost_estimate=cost(4),
        )(own_side, other_side, lead, lead_hat, inv2, lead_inv, in_far(gain.reshape(-1, LANES)))
        return loss[:, 0][None], fix, sums
    pairs_all = own_side.shape[0]
    groups = own_side[:, D].astype(full)
    same_group = groups[:, None] == groups[None, :]
    row_weight = pairs_all / GROUPS / jnp.sum(same_group.astype(full), axis=1)
    sim_scores = LOGIT_SCALE * jnp.einsum("id,jd->ij", own_side[:, :D], other_side[:, :D], preferred_element_type=full)
    place = jnp.arange(pairs_all, dtype=jnp.int32)
    diagonal = (place[:, None] == place[None, :]).astype(full)
    logits = sim_scores - LOGIT_SCALE * MARGIN * diagonal
    masked = jnp.where(same_group, logits, -jnp.inf)
    col_top = jnp.max(masked, axis=0, keepdims=True)
    col_lse = col_top + jnp.log(jnp.sum(jnp.exp(masked - col_top), axis=0, keepdims=True))
    own = masked[:seq_count]
    row_top = jnp.max(own, axis=1, keepdims=True)
    row_lse = row_top + jnp.log(jnp.sum(jnp.exp(own - row_top), axis=1, keepdims=True))
    own_diag = diagonal[:seq_count]
    own_logit = jnp.sum(logits[:seq_count] * own_diag, axis=1)
    loss_rows = (row_weight[:seq_count] * (row_lse[:, 0] - own_logit))[None]
    dsims = row_weight[:seq_count, None] * (jnp.exp(own - row_lse) - own_diag)
    dsims += row_weight[None, :] * (jnp.exp(own - col_lse) - own_diag)
    unit_grad = LOGIT_SCALE * jnp.dot(dsims, other_side[:, :D].astype(full), precision=highest)
    lead_inv = lead_inv[:, :1]
    cross = jnp.sum(lead * unit_grad, axis=-1, keepdims=True)
    lead_grad = lead_inv * unit_grad - lead_inv * lead_inv * lead_inv * cross * lead
    sums = jnp.stack([jnp.sum(lead_grad * lead_hat, axis=0), jnp.sum(lead_grad, axis=0)])
    return loss_rows, norm_back(lead_grad * gain[None], lead_hat, inv2[:, :1]), sums


def down_grad_kernel(seq_len, fresh, place, *refs):
    step = pl.program_id(0)
    if fresh:
        old_ref, leads_ref, fix_ref, act_ref, *outs, db_ref, sum_ref = refs

        @pl.when(step == 0)
        def _():
            db_ref[...] = old_ref[...]
            fixed = (leads_ref[...] + fix_ref[...]).astype(low)
            sum_ref[...] = columns_sum(fixed.astype(full) - leads_ref[...].astype(low).astype(full))
            for s in range(fix_ref.shape[0]):
                block = old_ref[s * seq_len : s * seq_len + 16, :]
                first = lax.broadcasted_iota(jnp.int32, block.shape, 0) == 0
                block = jnp.where(first, fixed[s : s + 1, :].astype(full), block.astype(full))
                db_ref[s * seq_len : s * seq_len + 16, :] = block.astype(low)
    else:
        db_ref, act_ref, *outs = refs
    grad = t_dot(act_ref[...], db_ref[...]).astype(low)
    tall = grad.shape[0]
    for rank in range(4):

        @pl.when(step == rank)
        def _(rank=rank):
            outs[rank // 2][rank % 2 * tall : (rank % 2 + 1) * tall, :] = grad


def down_gradient(place, first, act, dbranch, leads=None, fix=None, seq_len=None):
    count, hidden = act.shape
    tall = hidden // 8
    fresh = fix is not None
    operands = [in_far(dbranch)] + ([leads, fix] if fresh else []) + [in_far(act)]
    moving = pl.BlockSpec((count, tall), lambda p, place: (0, place[first + p]))
    in_specs = [fixed_spec(*operand.shape) for operand in operands[:-1]] + [moving]
    out_specs = [fixed_spec(2 * tall, D)] * 2
    out_shape = [shape_of(2 * tall, D)] * 2
    if fresh:
        out_specs += [fixed_spec(count, D), fixed_spec(1, D)]
        out_shape += [far(count, D), shape_of(1, D, dtype=full)]
    return pl.pallas_call(
        functools.partial(down_grad_kernel, seq_len, fresh),
        grid_spec=pltpu.PrefetchScalarGridSpec(
            num_scalar_prefetch=1, grid=(4,), in_specs=in_specs, out_specs=out_specs
        ),
        out_shape=out_shape,
        compiler_params=params(1),
        name=f"down_grad_{first}",
        cost_estimate=cost(4),
    )(place, *operands)


def put_rows(place, grad_ref, outs, columns):
    tall = grad_ref.shape[0] // 8
    for rank in range(8):
        at = pl.multiple_of(place[rank] * tall, 16)
        outs[rank // 2][rank % 2 * tall : (rank % 2 + 1) * tall, columns] = grad_ref[pl.ds(at, tall), :]


def hidden_kernel(place, db_ref, slope_ref, dw, nl_ref, dpre_ref, sum_ref, *rest):
    *outs, scratch = rest
    dpre = (dot_t(db_ref[...], dw[...]) * slope_ref[...].astype(full)).astype(low)
    dpre_ref[...] = dpre
    sum_ref[0:1, :] = columns_sum(dpre.astype(full))
    scratch[...] = t_dot(nl_ref[...], dpre).astype(low)
    put_rows(place, scratch, outs, slice(None))


def hidden_gradient(place, dbranch, slope, dw, nl):
    count, hidden = slope.shape
    wide = pl.BlockSpec((count, D), lambda j, *_: (0, j))
    pair = D // 4
    return pl.pallas_call(
        hidden_kernel,
        grid_spec=pltpu.PrefetchScalarGridSpec(
            num_scalar_prefetch=1,
            grid=(hidden // D,),
            in_specs=[fixed_spec(count, D), wide, pl.BlockSpec((D, D), lambda j, *_: (j, 0)), fixed_spec(count, D)],
            out_specs=[wide] + [pl.BlockSpec((rows, D), lambda j, *_: (0, j)) for rows in (8, pair, pair, pair, pair)],
            scratch_shapes=[pltpu.VMEM((D, D), low)],
        ),
        out_shape=[far(count, hidden), shape_of(8, hidden, dtype=full)] + [shape_of(pair, hidden)] * 4,
        input_output_aliases={2: 0},
        compiler_params=params(1, 18),
        name="hidden_gradient",
        cost_estimate=cost(15),
    )(place, in_far(dbranch), in_far(slope), dw, in_far(nl))


def norm_one_kernel(dpre_ref, uw, gain1, wo_far, branch_far, hat_far, inv_far,
                    datt_ref, dctx_ref, sums_ref, acc, wo, branch_ref, hat_ref, inv_ref, sems):
    step = pl.program_id(0)
    copies = [
        pltpu.make_async_copy(source, target, sems.at[k])
        for k, (source, target) in enumerate(((wo_far, wo), (branch_far, branch_ref), (hat_far, hat_ref), (inv_far, inv_ref)))
    ]

    @pl.when(step == 0)
    def _():
        for copy in copies:
            copy.start()
        acc[...] = jnp.zeros_like(acc)

    acc[...] += dot_t(dpre_ref[...], uw[...])

    @pl.when(step == pl.num_programs(0) - 1)
    def _():
        for copy in copies:
            copy.wait()
        gain = line(gain1)
        totals = [jnp.zeros((1, D), full)] * 3
        for start in range(0, acc.shape[0], 256):
            rows = slice(start, start + 256)
            grad, hat = acc[rows, :] + branch_ref[rows, :].astype(full), hat_ref[rows, :]
            dr1 = norm_back(grad * gain, hat, inv_ref[rows, 0:1])
            datt = dr1.astype(low)
            datt_ref[0, rows, :] = datt
            dctx_ref[rows, :] = dot_t(datt, wo[...]).astype(low)
            totals = [
                total + columns_sum(part) for total, part in zip(totals, (grad * hat, grad, datt.astype(full)), strict=True)
            ]
        for rank, total in enumerate(totals):
            sums_ref[rank : rank + 1, :] = total


def norm_one_backward(dpre, dbranch, hat, inv, uw, wo, gain1):
    count, hidden = dpre.shape
    anywhere = pl.BlockSpec(memory_space=pl.ANY)
    return pl.pallas_call(
        norm_one_kernel,
        grid=(hidden // D,),
        in_specs=[
            pl.BlockSpec((count, D), lambda j: (0, j)), pl.BlockSpec((D, D), lambda j: (0, j)), vector_spec(), anywhere, anywhere, anywhere, anywhere,
        ],
        out_specs=[pl.BlockSpec((1, count, D), lambda j: (3, 0, 0)), fixed_spec(count, D), fixed_spec(8, D)],
        out_shape=[far(4, count, D), far(count, D), shape_of(8, D, dtype=full)],
        scratch_shapes=[
            pltpu.VMEM((count, D), full), pltpu.VMEM((D, D), low), pltpu.VMEM((count, D), low),
            pltpu.VMEM((count, D), full), pltpu.VMEM((count, LANES), full), pltpu.SemaphoreType.DMA((4,)),
        ],
        compiler_params=params(1, 24),
        name="norm_one_backward",
        cost_estimate=cost(13),
    )(in_far(dpre), uw, gain1, wo, in_far(dbranch), in_far(hat), in_far(inv))


def attention_back_kernel(seq_len, q_ref, k_ref, v_ref, p_ref, dc_ref, stack_ref, d_ref, sums):
    q, k, v, probs, dctx = (ref[...] for ref in (q_ref, k_ref, v_ref, p_ref, dc_ref))
    count = q.shape[0]
    cells = cells_of(count, seq_len)
    factor = 1.0 / math.sqrt(HD)
    spread_dctx = [two_heads(dctx[cell]) for cell in cells]
    dprobs = [dot_t(v[cell], wide) for cell, wide in zip(cells, spread_dctx, strict=True)]
    dvals = [dot(probs[cell], wide).astype(low) for cell, wide in zip(cells, spread_dctx, strict=True)]
    dscores = []
    for cell, dprob in zip(cells, dprobs, strict=True):
        prob = probs[cell].astype(full)
        dscores.append((prob * (dprob - columns_sum(prob * dprob))).astype(low))
    dkeys = [(dot(ds, two_heads(q[cell])) * factor).astype(low) for cell, ds in zip(cells, dscores, strict=True)]
    dqueries = [(own_head(t_dot(ds, k[cell])) * factor).astype(low) for cell, ds in zip(cells, dscores, strict=True)]

    @pl.when(pl.program_id(0) == 0)
    def _():
        sums[...] = jnp.zeros_like(sums)

    for rank, pieces in enumerate((dqueries, dkeys, dvals)):
        grad = joined(pieces, count, seq_len)
        d_ref[rank] = grad
        sums[rank : rank + 1, :] += columns_sum(grad.astype(full))


def attention_backward(seq_len, q, k, v, probs, dctx, stack):
    count = q.shape[0]
    rows = 256
    row = pl.BlockSpec((rows, D), lambda i: (i, 0))
    return pl.pallas_call(
        functools.partial(attention_back_kernel, seq_len),
        grid=(count // rows,),
        in_specs=[row] * 5 + [pl.BlockSpec(memory_space=pl.ANY)],
        out_specs=[pl.BlockSpec((3, rows, D), lambda i: (0, i, 0)), fixed_spec(8, D)],
        out_shape=[far(4, count, D), shape_of(8, D, dtype=full)],
        input_output_aliases={5: 0},
        compiler_params=params(1, 14),
        name="attention_backward",
        cost_estimate=cost(8),
    )(*map(in_far, (q, k, v, probs, dctx, stack)))


def square_grad_kernel(late, place, left_ref, d_ref, *rest):
    step = pl.program_id(0)
    if late:
        far_ref, *outs, scratch, late_ref, sem = rest
        copy = pltpu.make_async_copy(far_ref, late_ref, sem)

        @pl.when(step == 0)
        def _():
            copy.start()
            scratch[...] = t_dot(left_ref[...], d_ref[0]).astype(low)

        @pl.when(step == 1)
        def _():
            copy.wait()
            scratch[...] = t_dot(late_ref[...], d_ref[0]).astype(low)
    else:
        small_ref, *outs, scratch = rest
        scratch[...] = t_dot(left_ref[...], d_ref[0]).astype(low)

        @pl.when(step == 0)
        def _():
            tall = D // 8
            for rank in range(8):
                out_ref, first = outs[rank // 2], rank % 2 * tall
                out_ref[first : first + tall, 2 * D :] = jnp.zeros((tall, LANES), low)

                @pl.when(place[rank] == 0)
                def _(out_ref=out_ref, first=first):
                    out_ref[first : first + small_ref.shape[0], 2 * D :] = small_ref[...].astype(low)

    put_rows(place, scratch, outs, pl.ds(pl.multiple_of(step * D, LANES), D))


def square_gradient(place, lefts, stack, slots, small, name):
    count = lefts[0].shape[0]
    late = len(lefts) == 2
    pair, columns = D // 4, 2 * D + (0 if late else LANES)
    scratch = [pltpu.VMEM((D, D), low)]
    if late:
        scratch += [pltpu.VMEM((count, D), low), pltpu.SemaphoreType.DMA]
    return pl.pallas_call(
        functools.partial(square_grad_kernel, late),
        grid_spec=pltpu.PrefetchScalarGridSpec(
            num_scalar_prefetch=1,
            grid=(2,),
            in_specs=[
                fixed_spec(count, D),
                pl.BlockSpec((1, count, D), lambda j, *_: (slots[0] + j * (slots[1] - slots[0]), 0, 0)),
                pl.BlockSpec(memory_space=pl.ANY) if late else fixed_spec(*small.shape),
            ],
            out_specs=[fixed_spec(pair, columns)] * 4,
            scratch_shapes=scratch,
        ),
        out_shape=[shape_of(pair, columns)] * 4,
        compiler_params=params(1, 18),
        name=name,
        cost_estimate=cost(6),
    )(place, in_far(lefts[0]), in_far(stack), in_far(lefts[1]) if late else small)


def input_grad_kernel(d_ref, wq, wk, wv, out_ref):
    out_ref[...] = (
        d_ref[3].astype(full) + dot_t(d_ref[0], wq[...]) + dot_t(d_ref[1], wk[...]) + dot_t(d_ref[2], wv[...])
    )


def input_gradient(stack, wq, wk, wv):
    count = stack.shape[1]
    rows = 256
    mat = fixed_spec(D, D)
    return pl.pallas_call(
        input_grad_kernel,
        grid=(count // rows,),
        in_specs=[pl.BlockSpec((4, rows, D), lambda i: (0, i, 0))] + [mat] * 3,
        out_specs=pl.BlockSpec((rows, D), lambda i: (i, 0)),
        out_shape=far(count, D, dtype=full),
        compiler_params=params(1),
        name="input_gradient",
        cost_estimate=cost(6),
    )(in_far(stack), wq, wk, wv)


def spread_kernel(widths, talls, first, place, *refs):
    smalls = refs[len(refs) - len(talls) :]
    outs = refs[len(refs) - len(talls) - len(widths) : len(refs) - len(talls)]
    tall = outs[0].shape[0]
    held = refs[0].shape[0] // tall
    if first and talls:

        @pl.when(pl.program_id(0) == 0)
        def _():
            for ref, old in zip(smalls, refs[4 // held : 4 // held + len(talls)], strict=True):
                ref[...] = old[...]

    for rank in range(4):

        @pl.when(pl.program_id(0) == rank)
        def _(rank=rank):
            source, rows = refs[rank // held], rank % held * tall
            at = 0
            for ref, width in zip(outs, widths, strict=True):
                ref[...] = source[rows : rows + tall, at : at + width].astype(full)
                at += width
            if talls:

                @pl.when(place[first + rank] == 0)
                def _():
                    top = rows
                    for ref in smalls:
                        ref[...] = source[top : top + ref.shape[0], at:].astype(full)
                        top += ref.shape[0]


def spread(place, first, pairs, widths, talls, carried, name):
    tall = sum(pair.shape[0] for pair in pairs) // 4
    carried = list(carried or [])
    small = [fixed_spec(rows, LANES) for rows in talls]
    in_specs = [fixed_spec(*pair.shape) for pair in pairs]
    operands = list(pairs)
    if carried:
        operands += carried[len(widths) :] + carried[: len(widths)]
        in_specs += small + [pl.BlockSpec(memory_space=pl.ANY)] * len(widths)
    return pl.pallas_call(
        functools.partial(spread_kernel, widths, talls, first),
        grid_spec=pltpu.PrefetchScalarGridSpec(
            num_scalar_prefetch=1,
            grid=(4,),
            in_specs=in_specs,
            out_specs=[pl.BlockSpec((tall, width), lambda p, place: (place[first + p], 0)) for width in widths] + small,
        ),
        out_shape=[far(8 * tall, width, dtype=full) for width in widths]
        + [shape_of(rows, LANES, dtype=full) for rows in talls],
        input_output_aliases={1 + len(operands) - len(widths) + k: k for k in range(len(widths))} if carried else {},
        compiler_params=params(1),
        name=f"{name}_spread_{first}",
        cost_estimate=cost(3),
    )(place, *operands)


def places():
    half = lax.axis_index("stream")
    chip = lax.axis_index("dp")
    bits = (chip & 1, (chip >> 1) & 1)
    table = []
    for side in (half, 1 - half):
        first = jnp.where(side == 0, bits[0], bits[1])
        second = jnp.where(side == 0, bits[1], bits[0])
        table += [4 * side + 2 * (first ^ (k >> 1)) + (second ^ (k & 1)) for k in range(4)]
    return jnp.stack(table).astype(jnp.int32)


def chip_partner(bit_zero, bit_one):
    chips = lax.axis_size("dp")
    return [
        (half * chips + chip, half * chips + (chip ^ (bit_zero if half == 0 else bit_one)))
        for half in range(2)
        for chip in range(chips)
    ]


def core_partner():
    chips = lax.axis_size("dp")
    return [(half * chips + chip, (1 - half) * chips + chip) for half in range(2) for chip in range(chips)]


def swap(piece, pairs):
    return lax.ppermute(piece, ("stream", "dp"), pairs)


def add_low(left, right):
    return (left.astype(full) + right.astype(full)).astype(low)


def tie(value, after):
    return value if after is None else lax.optimization_barrier((value, after))[0]


def all_sum(sent):
    others = [swap(pair, core_partner()) for pair in sent]
    kept = yield sent
    pair = add_low(kept[1], others[1])
    other = swap(pair, chip_partner(1, 2))
    mine = add_low(kept[0], others[0])
    after = yield pair
    tall = mine.shape[0] // 2
    mine = tie(mine, after)
    block = add_low(mine[tall:], other[tall:])
    mine = add_low(mine[:tall], other[:tall])
    other = swap(block, chip_partner(2, 1))
    after = yield block
    bits = [1 << k for k in range(2, lax.axis_size("dp").bit_length() - 1)]
    for rank, pair in enumerate(zip(bits, bits[::-1], strict=True)):
        mine = add_low(tie(mine, after), other)
        other = swap(mine, chip_partner(*pair))
        after = (yield mine) if rank in (0, len(bits) - 1) else None
    mine = add_low(tie(mine, after), other)
    other = swap(mine, chip_partner(2, 1))
    after = yield mine
    pair = jnp.concatenate([tie(mine, after), other])
    other = swap(pair, chip_partner(1, 2))
    after = yield pair
    pairs = [tie(pair, after), other]
    others = [swap(each, core_partner()) for each in pairs]
    yield pairs
    yield others


def gather_rows(rows):
    chips = lax.axis_size("dp")
    bit = 1
    after = None
    while bit < chips:
        others = [swap(rows, chip_partner(k * bit, k * bit)) for k in range(1, 4) if k * bit < chips]
        after = yield rows
        rows = jnp.concatenate([tie(rows, after)] + others)
        bit *= 4
    other = swap(rows, core_partner())
    yield rows
    yield rows, other


def in_far(array):
    return pltpu.with_memory_space_constraint(array, pltpu.HBM)


def shards(
    layer_input, pair_group, query_weight, query_bias, key_weight, value_weight, value_bias,
    out_weight, out_bias, mixer_gain, mixer_shift, up_weight, up_bias, down_weight, down_bias,
    final_gain, final_shift, upstream,
):
    count = layer_input.shape[1]
    seq_count = pair_group.shape[0]
    seq_len = count // seq_count
    hidden = up_bias.shape[0]
    tokens, upstream = in_far(layer_input[0]), in_far(upstream[0])
    wq, wk, wv, wo = map(in_far, (query_weight, key_weight, value_weight, out_weight))
    uw, dw = in_far(up_weight), in_far(down_weight)
    fold = lambda vector: in_far(vector.reshape(-1, LANES))
    bq, bv, bo, g1, s1 = map(fold, (query_bias, value_bias, out_bias, mixer_gain, mixer_shift))
    ub, db, g2, s2 = map(fold, (up_bias, down_bias, final_gain, final_shift))
    place = places()

    q, k, v, probs, context, nl, hat, inv, lead_nl, lead_hat = attention_forward(
        tokens, seq_len, wq, wk, wv, wo, bq, bv, bo, g1, s1
    )
    lead, lead_hat, lead_inv2, lead_inv, units = lead_forward(lead_nl, lead_hat, uw, ub, dw, g1, s1, db, g2, s2)
    ids = jnp.broadcast_to(pair_group.astype(low)[:, None], (seq_count, LANES))
    hops = gather_rows(jnp.concatenate([units, ids], axis=1))
    sent = next(hops)
    parts = 2
    carried = None
    for part in range(parts):
        carried = ff_forward(
            part, parts, carried, seq_len, tie(nl, sent), hat, upstream, uw, ub, dw, g1, s1, db, g2, s2
        )
        sent = hops.send(carried[4])
    while not isinstance(sent, tuple):
        sent = hops.send(None)
    layer_output, act, slope, dbranch, final_sums, dr2_leads = carried
    loss_rows, fix, lead_sums = pair_loss(*sent, lead, lead_hat, lead_inv2, lead_inv, final_gain)

    *down_blocks, dbranch, down_sum = down_gradient(place, 4, act, dbranch, dr2_leads.reshape(-1, D), fix, seq_len)
    sent = down_blocks
    talls = [hidden // LANES] + [D // LANES] * 8
    down = all_sum(down_blocks)
    next(down)
    sent = (sent, down_blocks)
    down_kept = down_gradient(place, 0, act, tie(dbranch, sent))
    sent = down_kept
    sent = down.send(tie(down_kept, sent))
    dpre, up_sums, *up_blocks = hidden_gradient(place, tie(dbranch, sent), slope, dw, nl)
    sent = dpre
    sent = down.send(sent)
    up = all_sum(up_blocks[2:])
    next(up)
    sent = (sent, up_blocks[2:])
    stack, dctx, mixer = norm_one_backward(tie(dpre, sent), dbranch, hat, inv, uw, wo, g1)
    sent = dctx
    sent = down.send(sent)
    sent = up.send(tie(up_blocks[:2], sent))
    stack, qkv = attention_backward(seq_len, q, k, v, probs, tie(dctx, sent), stack)
    sent = stack
    value_blocks = square_gradient(place, [context, tokens], tie(stack, sent), (3, 2), None, "value_gradient")
    sent = value_blocks[2]
    sent = down.send(sent)
    value = all_sum(value_blocks[2:])
    next(value)
    sent = (sent, value_blocks[2:])
    sent = up.send(sent)
    final = jnp.sum(final_sums, axis=0)
    small = jnp.concatenate(
        [
            up_sums[0], mixer[2], mixer[0], mixer[1], final[2] + down_sum[0], final[0] + lead_sums[0],
            final[1] + lead_sums[1], qkv[0], qkv[2],
        ]
    ).reshape(-1, LANES)
    query_blocks = square_gradient(place, [tokens], tie(stack, sent), (0, 1), small, "query_gradient")
    sent = query_blocks[2]
    sent = value.send(tie(value_blocks[:2], sent))
    sent = up.send(sent)
    query = all_sum(query_blocks[2:])
    next(query)
    sent = (sent, query_blocks[2:])
    sent = down.send(sent)
    sent = query.send(tie(query_blocks[:2], sent))
    sent = value.send(sent)
    sent = up.send(sent)
    sent = down.send(sent)
    input_grad = input_gradient(tie(stack, sent), wq, wk, wv)
    sent = input_grad
    sent = value.send(sent)
    sent = query.send(sent)
    sent = up.send(sent)
    down_own = down.send(sent)
    sent = down_own
    sent = value.send(sent)
    down_out = spread(place, 0, tie(down_own, sent), [D], [], None, "down")
    sent = down_out
    sent = query.send(sent)
    sent = up.send(sent)
    sent = query.send(sent)
    sent = value.send(sent)
    sent = query.send(sent)
    down_out = spread(place, 4, down.send(sent), [D], [], down_out, "down")
    sent = down_out
    up_own = up.send(sent)
    sent = up_own
    sent = value.send(sent)
    up_out = spread(place, 0, tie(up_own, sent), [hidden], [], None, "up")
    sent = up_out
    sent = query.send(sent)
    up_out = spread(place, 4, up.send(sent), [hidden], [], up_out, "up")
    sent = up_out
    value_own = value.send(sent)
    sent = value_own
    value_out = spread(place, 0, tie(value_own, sent), [D] * 2, [], None, "value")
    sent = value_out
    value_out = spread(place, 4, value.send(sent), [D] * 2, [], value_out, "value")
    sent = value_out
    query_own = query.send(sent)
    sent = query_own
    query_out = spread(place, 0, tie(query_own, sent), [D] * 2, talls, None, "query")
    sent = query_out
    query_out = spread(place, 4, query.send(sent), [D] * 2, talls, query_out, "query")
    sent = query_out
    wq_grad, wk_grad, *smalls = query_out
    up_b, out_b, gain_one, shift_one, down_b, gain_two, shift_two, query_b, value_b = (each.reshape(-1) for each in smalls)
    return (
        layer_output[None], input_grad[None], loss_rows,
        wq_grad, query_b, wk_grad, value_out[1], value_b, value_out[0], out_b,
        gain_one, shift_one, up_out[0], up_b, down_out[0], down_b, gain_two, shift_two,
    )


def solution(mesh):
    split = P("stream", "dp", None)
    return jax.shard_map(
        shards,
        mesh=mesh,
        in_specs=(split, P("dp")) + (P(),) * 15 + (split,),
        out_specs=(split, split, P("stream", "dp")) + (P(),) * 15,
        check_vma=False,
    )
```

```python
import functools
import math

import jax
import jax.numpy as jnp
from jax import lax
from jax.experimental import pallas as pl
from jax.experimental.pallas import tpu as pltpu
from jax.sharding import PartitionSpec as P

D = 768
HEADS = 12
HD = 64
GROUPS = 109
LANES = 128

MARGIN = 0.3
LOGIT_SCALE = 30.0
NORM_EPS = 1e-12
UNIT_EPS = 1e-06
highest = lax.Precision.HIGHEST
low = jnp.bfloat16
full = jnp.float32


def dot(left, right):
    return lax.dot_general(left, right, (((1,), (0,)), ((), ())), preferred_element_type=full)


def dot_t(left, right):
    return lax.dot_general(left, right, (((1,), (1,)), ((), ())), preferred_element_type=full)


def t_dot(left, right):
    return lax.dot_general(left, right, (((0,), (0,)), ((), ())), preferred_element_type=full)


def mean_of(values):
    return jnp.sum(values, axis=-1, keepdims=True) * (1.0 / D)


def norm_stats(values):
    centred = values - mean_of(values)
    inv_std = lax.rsqrt(mean_of(centred * centred) + NORM_EPS)
    return centred * inv_std, inv_std


def norm_back(grad_hat, normed_hat, inv_std):
    return inv_std * (grad_hat - mean_of(grad_hat) - normed_hat * mean_of(grad_hat * normed_hat))


def normal_cdf(values):
    bell = jnp.exp(-0.5 * values * values)
    step = 1.0 / (1.0 + (0.3275911 / math.sqrt(2.0)) * jnp.abs(values))
    tail = 0.5 * 1.061405429
    for factor in (-1.453152027, 1.421413741, -0.284496736, 0.254829592):
        tail = tail * step + 0.5 * factor
    tail = tail * step * bell
    return jnp.where(values >= 0.0, 1.0 - tail, tail), bell


def gelu_and_slope(values):
    cdf, bell = normal_cdf(values)
    return values * cdf, cdf + values * bell * (1.0 / math.sqrt(2.0 * math.pi))


def columns_sum(values):
    return jnp.sum(values, axis=0, keepdims=True)


def line(ref, first=0):
    return jnp.concatenate([ref[pl.ds(first + k, 1), :] for k in range(D // LANES)], axis=1)


def fixed_spec(*shape):
    return pl.BlockSpec(shape, lambda *_: (0,) * len(shape))


def vector_spec(count=D):
    return fixed_spec(count // LANES, LANES)


def shape_of(*shape, dtype=low):
    return jax.ShapeDtypeStruct(shape, dtype)


def far(*shape, dtype=low):
    return pltpu.HBM(shape, dtype)


def near(*shape, dtype=low):
    return pltpu.VMEM(shape, dtype)


def params(grid_dims, mib=20):
    return pltpu.CompilerParams(dimension_semantics=("arbitrary",) * grid_dims, vmem_limit_bytes=mib << 20)


def cost(micros):
    return pl.CostEstimate(flops=int(micros * 0.02 * 1.15e9), bytes_accessed=1000, transcendentals=0)


def two_heads(block):
    lane = lax.broadcasted_iota(jnp.int32, block.shape, 1)
    zero = jnp.zeros_like(block)
    return jnp.concatenate([jnp.where(lane < HD, block, zero), jnp.where(lane < HD, zero, block)], axis=0)


def own_head(both):
    count = both.shape[0] // 2
    lane = lax.broadcasted_iota(jnp.int32, (count, both.shape[1]), 1)
    return jnp.where(lane < HD, both[:count], both[count:])


def cells_of(count, seq_len):
    return [
        (slice(start, start + seq_len), slice(first, first + 2 * HD))
        for first in range(0, D, 2 * HD)
        for start in range(0, count, seq_len)
    ]


def joined(pieces, count, seq_len):
    tall = count // seq_len
    columns = [jnp.concatenate(pieces[k : k + tall], axis=0) for k in range(0, len(pieces), tall)]
    return jnp.concatenate(columns, axis=1)


def attention_kernel(seq_len, x_ref, wq, wk, wv, wo, bq, bv, bo, gain, shift,
                     q_ref, k_ref, v_ref, p_ref, c_ref, nl_ref, hat_ref, inv_ref, nll_ref, hatl_ref):
    x = x_ref[...]
    count = x.shape[0]
    q = (dot(x, wq[...]) + line(bq)).astype(low)
    k = dot(x, wk[...]).astype(low)
    v = (dot(x, wv[...]) + line(bv)).astype(low)
    q_ref[...], k_ref[...], v_ref[...] = q, k, v
    cells = cells_of(count, seq_len)
    factor = 1.0 / math.sqrt(HD)
    scores = [dot_t(k[cell], two_heads(q[cell])) * factor for cell in cells]
    probs = []
    for cell, score in zip(cells, scores, strict=True):
        terms = jnp.exp(score - jnp.max(score, axis=0, keepdims=True))
        probs.append((terms * (1.0 / columns_sum(terms))).astype(low))
        p_ref[cell] = probs[-1]
    pieces = [own_head(t_dot(prob, v[cell])).astype(low) for cell, prob in zip(cells, probs, strict=True)]
    context = joined(pieces, count, seq_len)
    c_ref[...] = context
    hat, inv_std = norm_stats(x.astype(full) + dot(context, wo[...]) + line(bo))
    normed_low = (hat * line(gain) + line(shift)).astype(low)
    hat_ref[...] = hat
    inv_ref[...] = jnp.broadcast_to(inv_std, inv_ref.shape)
    nl_ref[...] = normed_low
    for s in range(count // seq_len):
        nll_ref[0, s : s + 1, :] = normed_low[s * seq_len : s * seq_len + 1, :].astype(full)
        hatl_ref[0, s : s + 1, :] = hat[s * seq_len : s * seq_len + 1, :]


def attention_forward(tokens, seq_len, wq, wk, wv, wo, *vectors):
    count = tokens.shape[0]
    rows = 256
    steps, leads = count // rows, rows // seq_len
    row, mat = pl.BlockSpec((rows, D), lambda i: (i, 0)), fixed_spec(D, D)
    lead = pl.BlockSpec((1, leads, D), lambda i: (i, 0, 0))
    return pl.pallas_call(
        functools.partial(attention_kernel, seq_len),
        grid=(steps,),
        in_specs=[row, mat, mat, mat, mat] + [vector_spec()] * 5,
        out_specs=[row] * 7 + [pl.BlockSpec((rows, LANES), lambda i: (i, 0)), lead, lead],
        out_shape=[far(count, D)] * 5
        + [far(count, D), far(count, D, dtype=full), far(count, LANES, dtype=full)]
        + [shape_of(steps, leads, D, dtype=full)] * 2,
        compiler_params=params(1, 20),
        name="attention_forward",
        cost_estimate=cost(10),
    )(tokens, wq, wk, wv, wo, *vectors)


def lead_kernel(nl_ref, hat_ref, uw, ub, dw, gain1, shift1, db, gain2, shift2,
                lead_ref, hat2_ref, inv2_ref, linv_ref, unit_ref, nl, acc):
    step = pl.program_id(0)

    @pl.when(step == 0)
    def _():
        hat = jnp.concatenate([hat_ref[k] for k in range(hat_ref.shape[0])], axis=0)
        nl[...] = jnp.concatenate([nl_ref[k] for k in range(nl_ref.shape[0])], axis=0).astype(low)
        acc[...] = hat * line(gain1) + line(shift1) + line(db)

    pre = dot(nl[...], uw[...]) + line(ub, step * (D // LANES))
    acc[...] += dot(gelu_and_slope(pre)[0].astype(low), dw[...])

    @pl.when(step == pl.num_programs(0) - 1)
    def _():
        hat, inv_std = norm_stats(acc[...])
        lead = hat * line(gain2) + line(shift2)
        lead_inv = lax.rsqrt(jnp.sum(lead * lead, axis=-1, keepdims=True) + UNIT_EPS)
        lead_ref[...] = lead
        hat2_ref[...] = hat
        inv2_ref[...] = jnp.broadcast_to(inv_std, inv2_ref.shape)
        linv_ref[...] = jnp.broadcast_to(lead_inv, linv_ref.shape)
        unit_ref[...] = (lead * lead_inv).astype(low)


def lead_forward(nl, hat, uw, ub, dw, *vectors):
    count = nl.shape[0] * nl.shape[1]
    hidden = uw.shape[1]
    row, lane = fixed_spec(count, D), fixed_spec(count, LANES)
    return pl.pallas_call(
        lead_kernel,
        grid=(hidden // D,),
        in_specs=[
            fixed_spec(*nl.shape), fixed_spec(*hat.shape),
            pl.BlockSpec((D, D), lambda j: (0, j)), vector_spec(hidden), pl.BlockSpec((D, D), lambda j: (j, 0)),
        ] + [vector_spec()] * 5,
        out_specs=[row, row, lane, lane, row],
        out_shape=[shape_of(count, D, dtype=full)] * 2
        + [shape_of(count, LANES, dtype=full)] * 2 + [shape_of(count, D)],
        scratch_shapes=[pltpu.VMEM((count, D), low), pltpu.VMEM((count, D), full)],
        compiler_params=params(1),
        name="lead_forward",
        cost_estimate=cost(3),
    )(nl, hat, uw, ub, dw, *vectors)


def ff_kernel(part, seq_len, nl_ref, uw, ub, dw, gain1, shift1, db, gain2, shift2, hat_far, up_far, *rest):
    out_ref, act_ref, slope_ref, low_ref, sums_ref, leads_ref, acc, hat_ref, up_ref, sems = rest[-10:]
    step = pl.program_id(0)
    rows = acc.shape[0]
    span = pl.ds(part * rows, rows)
    copies = [
        pltpu.make_async_copy(source.at[span, :], target, sems.at[k])
        for k, (source, target) in enumerate(((hat_far, hat_ref), (up_far, up_ref)))
    ]

    @pl.when(step == 0)
    def _():
        for copy in copies:
            copy.start()
        acc[...] = jnp.zeros_like(acc)

    value, slope = gelu_and_slope(dot(nl_ref[...], uw[...]) + line(ub, step * (D // LANES)))
    act = value.astype(low)
    slope_ref[...] = slope.astype(low)
    act_ref[...] = act
    acc[...] += dot(act, dw[...])

    @pl.when(step == pl.num_programs(0) - 1)
    def _():
        for copy in copies:
            copy.wait()
        normed = hat_ref[...] * line(gain1) + line(shift1)
        hat, inv_std = norm_stats(acc[...] + (normed + line(db)))
        gain = line(gain2)
        out_ref[...] = (hat * gain + line(shift2)).astype(low)
        grad = up_ref[...].astype(full)
        dr2 = norm_back(grad * gain, hat, inv_std)
        branch = dr2.astype(low)
        low_ref[...] = branch
        sums_ref[0, 0:1, :] = columns_sum(grad * hat)
        sums_ref[0, 1:2, :] = columns_sum(grad)
        sums_ref[0, 2:3, :] = columns_sum(branch.astype(full))
        for s in range(rows // seq_len):
            leads_ref[0, s : s + 1, :] = dr2[s * seq_len : s * seq_len + 1, :]


def ff_forward(part, parts, carried, seq_len, nl, hat, upstream, uw, ub, dw, *vectors):
    count = nl.shape[0]
    rows = count // parts
    hidden = uw.shape[1]
    row = pl.BlockSpec((rows, D), lambda j: (part, 0))
    wide = pl.BlockSpec((rows, D), lambda j: (part, j))
    anywhere = pl.BlockSpec(memory_space=pl.ANY)
    operands = [in_far(nl), uw, ub, dw, *vectors, in_far(hat), upstream]
    in_specs = [row, pl.BlockSpec((D, D), lambda j: (0, j)), vector_spec(hidden), pl.BlockSpec((D, D), lambda j: (j, 0))]
    in_specs += [vector_spec()] * 5 + [anywhere] * 2
    aliases = {}
    if carried is not None:
        aliases = {len(operands) + k: k for k in range(len(carried))}
        operands += list(carried)
        in_specs += [anywhere] * len(carried)
    sums = lambda tall: pl.BlockSpec((1, tall, D), lambda j: (part, 0, 0))
    return pl.pallas_call(
        functools.partial(ff_kernel, part, seq_len),
        grid=(hidden // D,),
        in_specs=in_specs,
        out_specs=[row, wide, wide, row, sums(8), sums(rows // seq_len)],
        scratch_shapes=[
            pltpu.VMEM((rows, D), full), pltpu.VMEM((rows, D), full), pltpu.VMEM((rows, D), low),
            pltpu.SemaphoreType.DMA((2,)),
        ],
        out_shape=[
            far(count, D), far(count, hidden), far(count, hidden),
            far(count, D), shape_of(parts, 8, D, dtype=full),
            shape_of(parts, rows // seq_len, D, dtype=full),
        ],
        input_output_aliases=aliases,
        compiler_params=params(1, 20),
        name=f"ff_forward_{part}",
        cost_estimate=cost(13),
    )(*operands)


def loss_kernel(seq_count, own_ref, other_ref, lead_ref, hat_ref, inv_ref, linv_ref, gain2, loss_ref, fix_ref, sums_ref):
    count = own_ref.shape[0]
    own, other = own_ref[:, :D], other_ref[:, :D]
    columns = own_ref[:, D : D + 1].astype(full)
    rows = dot_t(jnp.ones((8, LANES), low), own_ref[:, D:])[0:1] * (1.0 / LANES)
    same = columns == rows
    place = [lax.broadcasted_iota(jnp.int32, (count, count), axis) for axis in range(2)]
    diagonal = (place[0] == place[1]).astype(full)
    logits = LOGIT_SCALE * dot_t(own, other) - LOGIT_SCALE * MARGIN * diagonal
    masked = jnp.where(same, logits, -jnp.inf)
    col_top = jnp.max(masked, axis=0, keepdims=True)
    col_lse = col_top + jnp.log(columns_sum(jnp.exp(masked - col_top)))
    mine = masked[:seq_count]
    row_top = jnp.max(mine, axis=1, keepdims=True)
    row_lse = row_top + jnp.log(jnp.sum(jnp.exp(mine - row_top), axis=1, keepdims=True))
    mine_diag = diagonal[:seq_count]
    own_logit = jnp.sum(logits[:seq_count] * mine_diag, axis=1, keepdims=True)
    found = same.astype(full)
    row_weight = (count / GROUPS) / jnp.sum(found[:seq_count], axis=1, keepdims=True)
    col_weight = (count / GROUPS) / columns_sum(found)
    loss_ref[...] = jnp.broadcast_to(row_weight * (row_lse - own_logit), loss_ref.shape)
    dsims = row_weight * (jnp.exp(mine - row_lse) - mine_diag) + col_weight * (jnp.exp(mine - col_lse) - mine_diag)
    high = dsims.astype(low)
    rest = (dsims - high.astype(full)).astype(low)
    unit_grad = LOGIT_SCALE * (dot(high, other) + dot(rest, other))
    lead, lead_inv, hat = lead_ref[...], linv_ref[:, 0:1], hat_ref[...]
    cross = jnp.sum(lead * unit_grad, axis=-1, keepdims=True)
    lead_grad = lead_inv * unit_grad - lead_inv * lead_inv * lead_inv * cross * lead
    fix_ref[...] = norm_back(lead_grad * line(gain2), hat, inv_ref[:, 0:1])
    sums_ref[0:1, :] = columns_sum(lead_grad * hat)
    sums_ref[1:2, :] = columns_sum(lead_grad)


def pair_loss(own_side, other_side, lead, lead_hat, inv2, lead_inv, gain):
    seq_count = lead.shape[0]
    if own_side.shape[0] <= 512:
        loss, fix, sums = pl.pallas_call(
            functools.partial(loss_kernel, seq_count),
            out_shape=[
                shape_of(seq_count, LANES, dtype=full), shape_of(seq_count, D, dtype=full), shape_of(8, D, dtype=full)
            ],
            compiler_params=params(0),
            name="pair_loss",
            cost_estimate=cost(4),
        )(own_side, other_side, lead, lead_hat, inv2, lead_inv, in_far(gain.reshape(-1, LANES)))
        return loss[:, 0][None], fix, sums
    pairs_all = own_side.shape[0]
    groups = own_side[:, D].astype(full)
    same_group = groups[:, None] == groups[None, :]
    row_weight = pairs_all / GROUPS / jnp.sum(same_group.astype(full), axis=1)
    sim_scores = LOGIT_SCALE * jnp.einsum("id,jd->ij", own_side[:, :D], other_side[:, :D], preferred_element_type=full)
    place = jnp.arange(pairs_all, dtype=jnp.int32)
    diagonal = (place[:, None] == place[None, :]).astype(full)
    logits = sim_scores - LOGIT_SCALE * MARGIN * diagonal
    masked = jnp.where(same_group, logits, -jnp.inf)
    col_top = jnp.max(masked, axis=0, keepdims=True)
    col_lse = col_top + jnp.log(jnp.sum(jnp.exp(masked - col_top), axis=0, keepdims=True))
    own = masked[:seq_count]
    row_top = jnp.max(own, axis=1, keepdims=True)
    row_lse = row_top + jnp.log(jnp.sum(jnp.exp(own - row_top), axis=1, keepdims=True))
    own_diag = diagonal[:seq_count]
    own_logit = jnp.sum(logits[:seq_count] * own_diag, axis=1)
    loss_rows = (row_weight[:seq_count] * (row_lse[:, 0] - own_logit))[None]
    dsims = row_weight[:seq_count, None] * (jnp.exp(own - row_lse) - own_diag)
    dsims += row_weight[None, :] * (jnp.exp(own - col_lse) - own_diag)
    unit_grad = LOGIT_SCALE * jnp.dot(dsims, other_side[:, :D].astype(full), precision=highest)
    lead_inv = lead_inv[:, :1]
    cross = jnp.sum(lead * unit_grad, axis=-1, keepdims=True)
    lead_grad = lead_inv * unit_grad - lead_inv * lead_inv * lead_inv * cross * lead
    sums = jnp.stack([jnp.sum(lead_grad * lead_hat, axis=0), jnp.sum(lead_grad, axis=0)])
    return loss_rows, norm_back(lead_grad * gain[None], lead_hat, inv2[:, :1]), sums


def down_grad_kernel(seq_len, fresh, place, *refs):
    step = pl.program_id(0)
    if fresh:
        old_ref, leads_ref, fix_ref, act_ref, *outs, db_ref, sum_ref = refs

        @pl.when(step == 0)
        def _():
            db_ref[...] = old_ref[...]
            fixed = (leads_ref[...] + fix_ref[...]).astype(low)
            sum_ref[...] = columns_sum(fixed.astype(full) - leads_ref[...].astype(low).astype(full))
            for s in range(fix_ref.shape[0]):
                block = old_ref[s * seq_len : s * seq_len + 16, :]
                first = lax.broadcasted_iota(jnp.int32, block.shape, 0) == 0
                block = jnp.where(first, fixed[s : s + 1, :].astype(full), block.astype(full))
                db_ref[s * seq_len : s * seq_len + 16, :] = block.astype(low)
    else:
        db_ref, act_ref, *outs = refs
    grad = t_dot(act_ref[...], db_ref[...]).astype(low)
    tall = grad.shape[0]
    for rank in range(4):

        @pl.when(step == rank)
        def _(rank=rank):
            outs[rank // 2][rank % 2 * tall : (rank % 2 + 1) * tall, :] = grad


def down_gradient(place, first, act, dbranch, leads=None, fix=None, seq_len=None):
    count, hidden = act.shape
    tall = hidden // 8
    fresh = fix is not None
    operands = [dbranch] + ([leads, fix] if fresh else []) + [in_far(act)]
    moving = pl.BlockSpec((count, tall), lambda p, place: (0, place[first + p]))
    in_specs = [fixed_spec(*operand.shape) for operand in operands[:-1]] + [moving]
    out_specs = [fixed_spec(2 * tall, D)] * 2
    out_shape = [pltpu.VMEM((2 * tall, D), low)] * 2
    if fresh:
        out_specs += [fixed_spec(count, D), fixed_spec(1, D)]
        out_shape += [shape_of(count, D), shape_of(1, D, dtype=full)]
    return pl.pallas_call(
        functools.partial(down_grad_kernel, seq_len, fresh),
        grid_spec=pltpu.PrefetchScalarGridSpec(
            num_scalar_prefetch=1, grid=(4,), in_specs=in_specs, out_specs=out_specs
        ),
        out_shape=out_shape,
        compiler_params=params(1),
        name=f"down_grad_{first}",
        cost_estimate=cost(4),
    )(place, *operands)


def put_rows(place, grad_ref, outs, columns):
    tall = grad_ref.shape[0] // 8
    for rank in range(8):
        at = pl.multiple_of(place[rank] * tall, 16)
        outs[rank // 2][rank % 2 * tall : (rank % 2 + 1) * tall, columns] = grad_ref[pl.ds(at, tall), :]


def hidden_kernel(place, db_ref, slope_ref, dw, nl_ref, dpre_ref, sum_ref, *rest):
    *outs, scratch = rest
    dpre = (dot_t(db_ref[...], dw[...]) * slope_ref[...].astype(full)).astype(low)
    dpre_ref[...] = dpre
    sum_ref[0:1, :] = columns_sum(dpre.astype(full))
    scratch[...] = t_dot(nl_ref[...], dpre).astype(low)
    put_rows(place, scratch, outs, slice(None))


def hidden_gradient(place, dbranch, slope, dw, nl):
    count, hidden = slope.shape
    wide = pl.BlockSpec((count, D), lambda j, *_: (0, j))
    pair = D // 4
    return pl.pallas_call(
        hidden_kernel,
        grid_spec=pltpu.PrefetchScalarGridSpec(
            num_scalar_prefetch=1,
            grid=(hidden // D,),
            in_specs=[fixed_spec(count, D), wide, pl.BlockSpec((D, D), lambda j, *_: (j, 0)), fixed_spec(count, D)],
            out_specs=[wide] + [pl.BlockSpec((rows, D), lambda j, *_: (0, j)) for rows in (8, pair, pair, pair, pair)],
            scratch_shapes=[pltpu.VMEM((D, D), low)],
        ),
        out_shape=[far(count, hidden), shape_of(8, hidden, dtype=full)] + [shape_of(pair, hidden)] * 4,
        input_output_aliases={2: 0},
        compiler_params=params(1, 18),
        name="hidden_gradient",
        cost_estimate=cost(15),
    )(place, dbranch, in_far(slope), dw, in_far(nl))


def norm_one_kernel(dpre_ref, uw, gain1, wo_far, branch_far, hat_far, inv_far,
                    datt_ref, dctx_ref, sums_ref, acc, wo, branch_ref, hat_ref, inv_ref, sems):
    step = pl.program_id(0)
    copies = [
        pltpu.make_async_copy(source, target, sems.at[k])
        for k, (source, target) in enumerate(((wo_far, wo), (branch_far, branch_ref), (hat_far, hat_ref), (inv_far, inv_ref)))
    ]

    @pl.when(step == 0)
    def _():
        for copy in copies:
            copy.start()
        acc[...] = jnp.zeros_like(acc)

    acc[...] += dot_t(dpre_ref[...], uw[...])

    @pl.when(step == pl.num_programs(0) - 1)
    def _():
        for copy in copies:
            copy.wait()
        gain = line(gain1)
        totals = [jnp.zeros((1, D), full)] * 3
        for start in range(0, acc.shape[0], 256):
            rows = slice(start, start + 256)
            grad, hat = acc[rows, :] + branch_ref[rows, :].astype(full), hat_ref[rows, :]
            dr1 = norm_back(grad * gain, hat, inv_ref[rows, 0:1])
            datt = dr1.astype(low)
            datt_ref[0, rows, :] = datt
            dctx_ref[rows, :] = dot_t(datt, wo[...]).astype(low)
            totals = [
                total + columns_sum(part) for total, part in zip(totals, (grad * hat, grad, datt.astype(full)), strict=True)
            ]
        for rank, total in enumerate(totals):
            sums_ref[rank : rank + 1, :] = total


def norm_one_backward(dpre, dbranch, hat, inv, uw, wo, gain1):
    count, hidden = dpre.shape
    anywhere = pl.BlockSpec(memory_space=pl.ANY)
    return pl.pallas_call(
        norm_one_kernel,
        grid=(hidden // D,),
        in_specs=[
            pl.BlockSpec((count, D), lambda j: (0, j)), pl.BlockSpec((D, D), lambda j: (0, j)), vector_spec(), anywhere, anywhere, anywhere, anywhere,
        ],
        out_specs=[pl.BlockSpec((1, count, D), lambda j: (3, 0, 0)), fixed_spec(count, D), fixed_spec(8, D)],
        out_shape=[near(4, count, D), near(count, D), shape_of(8, D, dtype=full)],
        scratch_shapes=[
            pltpu.VMEM((count, D), full), pltpu.VMEM((D, D), low), pltpu.VMEM((count, D), low),
            pltpu.VMEM((count, D), full), pltpu.VMEM((count, LANES), full), pltpu.SemaphoreType.DMA((4,)),
        ],
        compiler_params=params(1, 24),
        name="norm_one_backward",
        cost_estimate=cost(13),
    )(in_far(dpre), uw, gain1, wo, dbranch, in_far(hat), in_far(inv))


def attention_back_kernel(seq_len, q_ref, k_ref, v_ref, p_ref, dc_ref, stack_ref, d_ref, sums):
    q, k, v, probs, dctx = (ref[...] for ref in (q_ref, k_ref, v_ref, p_ref, dc_ref))
    count = q.shape[0]
    cells = cells_of(count, seq_len)
    factor = 1.0 / math.sqrt(HD)
    spread_dctx = [two_heads(dctx[cell]) for cell in cells]
    dprobs = [dot_t(v[cell], wide) for cell, wide in zip(cells, spread_dctx, strict=True)]
    dvals = [dot(probs[cell], wide).astype(low) for cell, wide in zip(cells, spread_dctx, strict=True)]
    dscores = []
    for cell, dprob in zip(cells, dprobs, strict=True):
        prob = probs[cell].astype(full)
        dscores.append((prob * (dprob - columns_sum(prob * dprob))).astype(low))
    dkeys = [(dot(ds, two_heads(q[cell])) * factor).astype(low) for cell, ds in zip(cells, dscores, strict=True)]
    dqueries = [(own_head(t_dot(ds, k[cell])) * factor).astype(low) for cell, ds in zip(cells, dscores, strict=True)]

    @pl.when(pl.program_id(0) == 0)
    def _():
        sums[...] = jnp.zeros_like(sums)

    for rank, pieces in enumerate((dqueries, dkeys, dvals)):
        grad = joined(pieces, count, seq_len)
        d_ref[rank] = grad
        sums[rank : rank + 1, :] += columns_sum(grad.astype(full))


def attention_backward(seq_len, q, k, v, probs, dctx, stack):
    count = q.shape[0]
    rows = 256
    row = pl.BlockSpec((rows, D), lambda i: (i, 0))
    return pl.pallas_call(
        functools.partial(attention_back_kernel, seq_len),
        grid=(count // rows,),
        in_specs=[row] * 5 + [pl.BlockSpec(memory_space=pl.ANY)],
        out_specs=[pl.BlockSpec((3, rows, D), lambda i: (0, i, 0)), fixed_spec(8, D)],
        out_shape=[near(4, count, D), shape_of(8, D, dtype=full)],
        input_output_aliases={5: 0},
        compiler_params=params(1, 14),
        name="attention_backward",
        cost_estimate=cost(8),
    )(*map(in_near, (q, k, v, probs, dctx, stack)))


def square_grad_kernel(late, place, left_ref, d_ref, *rest):
    step = pl.program_id(0)
    if late:
        far_ref, *outs, scratch, late_ref, sem = rest
        copy = pltpu.make_async_copy(far_ref, late_ref, sem)

        @pl.when(step == 0)
        def _():
            copy.start()
            scratch[...] = t_dot(left_ref[...], d_ref[0]).astype(low)

        @pl.when(step == 1)
        def _():
            copy.wait()
            scratch[...] = t_dot(late_ref[...], d_ref[0]).astype(low)
    else:
        small_ref, *outs, scratch = rest
        scratch[...] = t_dot(left_ref[...], d_ref[0]).astype(low)

        @pl.when(step == 0)
        def _():
            tall = D // 8
            for rank in range(8):
                out_ref, first = outs[rank // 2], rank % 2 * tall
                out_ref[first : first + tall, 2 * D :] = jnp.zeros((tall, LANES), low)

                @pl.when(place[rank] == 0)
                def _(out_ref=out_ref, first=first):
                    out_ref[first : first + small_ref.shape[0], 2 * D :] = small_ref[...].astype(low)

    put_rows(place, scratch, outs, pl.ds(pl.multiple_of(step * D, LANES), D))


def square_gradient(place, lefts, stack, slots, small, name):
    count = lefts[0].shape[0]
    late = len(lefts) == 2
    pair, columns = D // 4, 2 * D + (0 if late else LANES)
    scratch = [pltpu.VMEM((D, D), low)]
    if late:
        scratch += [pltpu.VMEM((count, D), low), pltpu.SemaphoreType.DMA]
    return pl.pallas_call(
        functools.partial(square_grad_kernel, late),
        grid_spec=pltpu.PrefetchScalarGridSpec(
            num_scalar_prefetch=1,
            grid=(2,),
            in_specs=[
                fixed_spec(count, D),
                pl.BlockSpec((1, count, D), lambda j, *_: (slots[0] + j * (slots[1] - slots[0]), 0, 0)),
                pl.BlockSpec(memory_space=pl.ANY) if late else fixed_spec(*small.shape),
            ],
            out_specs=[fixed_spec(pair, columns)] * 4,
            scratch_shapes=scratch,
        ),
        out_shape=[shape_of(pair, columns)] * 4,
        compiler_params=params(1, 18),
        name=name,
        cost_estimate=cost(6),
    )(place, in_far(lefts[0]), in_near(stack), in_far(lefts[1]) if late else small)


def input_grad_kernel(d_ref, wq, wk, wv, out_ref):
    out_ref[...] = (
        d_ref[3].astype(full) + dot_t(d_ref[0], wq[...]) + dot_t(d_ref[1], wk[...]) + dot_t(d_ref[2], wv[...])
    )


def input_gradient(stack, wq, wk, wv):
    count = stack.shape[1]
    rows = 256
    mat = fixed_spec(D, D)
    return pl.pallas_call(
        input_grad_kernel,
        grid=(count // rows,),
        in_specs=[pl.BlockSpec((4, rows, D), lambda i: (0, i, 0))] + [mat] * 3,
        out_specs=pl.BlockSpec((rows, D), lambda i: (i, 0)),
        out_shape=far(count, D, dtype=full),
        compiler_params=params(1),
        name="input_gradient",
        cost_estimate=cost(6),
    )(in_near(stack), wq, wk, wv)


def spread_kernel(widths, talls, first, place, *refs):
    smalls = refs[len(refs) - len(talls) :]
    outs = refs[len(refs) - len(talls) - len(widths) : len(refs) - len(talls)]
    tall = outs[0].shape[0]
    held = refs[0].shape[0] // tall
    if first and talls:

        @pl.when(pl.program_id(0) == 0)
        def _():
            for ref, old in zip(smalls, refs[4 // held : 4 // held + len(talls)], strict=True):
                ref[...] = old[...]

    for rank in range(4):

        @pl.when(pl.program_id(0) == rank)
        def _(rank=rank):
            source, rows = refs[rank // held], rank % held * tall
            at = 0
            for ref, width in zip(outs, widths, strict=True):
                ref[...] = source[rows : rows + tall, at : at + width].astype(full)
                at += width
            if talls:

                @pl.when(place[first + rank] == 0)
                def _():
                    top = rows
                    for ref in smalls:
                        ref[...] = source[top : top + ref.shape[0], at:].astype(full)
                        top += ref.shape[0]


def spread(place, first, pairs, widths, talls, carried, name):
    tall = sum(pair.shape[0] for pair in pairs) // 4
    carried = list(carried or [])
    small = [fixed_spec(rows, LANES) for rows in talls]
    in_specs = [fixed_spec(*pair.shape) for pair in pairs]
    operands = list(pairs)
    if carried:
        operands += carried[len(widths) :] + carried[: len(widths)]
        in_specs += small + [pl.BlockSpec(memory_space=pl.ANY)] * len(widths)
    return pl.pallas_call(
        functools.partial(spread_kernel, widths, talls, first),
        grid_spec=pltpu.PrefetchScalarGridSpec(
            num_scalar_prefetch=1,
            grid=(4,),
            in_specs=in_specs,
            out_specs=[pl.BlockSpec((tall, width), lambda p, place: (place[first + p], 0)) for width in widths] + small,
        ),
        out_shape=[far(8 * tall, width, dtype=full) for width in widths]
        + [shape_of(rows, LANES, dtype=full) for rows in talls],
        input_output_aliases={1 + len(operands) - len(widths) + k: k for k in range(len(widths))} if carried else {},
        compiler_params=params(1),
        name=f"{name}_spread_{first}",
        cost_estimate=cost(3),
    )(place, *operands)


def places():
    half = lax.axis_index("stream")
    chip = lax.axis_index("dp")
    bits = (chip & 1, (chip >> 1) & 1)
    table = []
    for side in (half, 1 - half):
        first = jnp.where(side == 0, bits[0], bits[1])
        second = jnp.where(side == 0, bits[1], bits[0])
        table += [4 * side + 2 * (first ^ (k >> 1)) + (second ^ (k & 1)) for k in range(4)]
    return jnp.stack(table).astype(jnp.int32)


def chip_partner(bit_zero, bit_one):
    chips = lax.axis_size("dp")
    return [
        (half * chips + chip, half * chips + (chip ^ (bit_zero if half == 0 else bit_one)))
        for half in range(2)
        for chip in range(chips)
    ]


def core_partner():
    chips = lax.axis_size("dp")
    return [(half * chips + chip, (1 - half) * chips + chip) for half in range(2) for chip in range(chips)]


def swap(piece, pairs):
    return lax.ppermute(piece, ("stream", "dp"), pairs)


def add_low(left, right):
    return (left.astype(full) + right.astype(full)).astype(low)


def tie(value, after):
    return value if after is None else lax.optimization_barrier((value, after))[0]


def all_sum(sent):
    others = [swap(pair, core_partner()) for pair in sent]
    kept = yield sent
    pair = add_low(kept[1], others[1])
    other = swap(pair, chip_partner(1, 2))
    mine = add_low(kept[0], others[0])
    after = yield pair, mine
    tall = mine.shape[0] // 2
    mine = tie(mine, after)
    block = add_low(mine[tall:], other[tall:])
    mine = add_low(mine[:tall], other[:tall])
    other = swap(block, chip_partner(2, 1))
    after = yield block, mine
    bits = [1 << k for k in range(2, lax.axis_size("dp").bit_length() - 1)]
    for rank, pair in enumerate(zip(bits, bits[::-1], strict=True)):
        mine = add_low(tie(mine, after), other)
        other = swap(mine, chip_partner(*pair))
        after = (yield mine) if rank in (0, len(bits) - 1) else None
    mine = add_low(tie(mine, after), other)
    other = swap(mine, chip_partner(2, 1))
    after = yield mine
    pair = jnp.concatenate([tie(mine, after), other])
    other = swap(pair, chip_partner(1, 2))
    after = yield pair
    pairs = [tie(pair, after), other]
    others = [swap(each, core_partner()) for each in pairs]
    yield pairs
    yield others


def gather_rows(rows):
    chips = lax.axis_size("dp")
    bit = 1
    after = None
    while bit < chips:
        others = [swap(rows, chip_partner(k * bit, k * bit)) for k in range(1, 4) if k * bit < chips]
        after = yield rows
        rows = jnp.concatenate([tie(rows, after)] + others)
        bit *= 4
    other = swap(rows, core_partner())
    yield rows
    yield rows, other


def in_far(array):
    return pltpu.with_memory_space_constraint(array, pltpu.HBM)


def in_near(array):
    return pltpu.with_memory_space_constraint(array, pltpu.VMEM)


def shards(
    layer_input, pair_group, query_weight, query_bias, key_weight, value_weight, value_bias,
    out_weight, out_bias, mixer_gain, mixer_shift, up_weight, up_bias, down_weight, down_bias,
    final_gain, final_shift, upstream,
):
    count = layer_input.shape[1]
    seq_count = pair_group.shape[0]
    seq_len = count // seq_count
    hidden = up_bias.shape[0]
    tokens, upstream = in_far(layer_input[0]), in_far(upstream[0])
    wq, wk, wv, wo = map(in_far, (query_weight, key_weight, value_weight, out_weight))
    uw, dw = in_far(up_weight), in_far(down_weight)
    fold = lambda vector: in_far(vector.reshape(-1, LANES))
    bq, bv, bo, g1, s1 = map(fold, (query_bias, value_bias, out_bias, mixer_gain, mixer_shift))
    ub, db, g2, s2 = map(fold, (up_bias, down_bias, final_gain, final_shift))
    place = places()

    q, k, v, probs, context, nl, hat, inv, lead_nl, lead_hat = attention_forward(
        tokens, seq_len, wq, wk, wv, wo, bq, bv, bo, g1, s1
    )
    lead, lead_hat, lead_inv2, lead_inv, units = lead_forward(lead_nl, lead_hat, uw, ub, dw, g1, s1, db, g2, s2)
    ids = jnp.broadcast_to(pair_group.astype(low)[:, None], (seq_count, LANES))
    hops = gather_rows(jnp.concatenate([units, ids], axis=1))
    sent = next(hops)
    parts = 2
    carried = None
    for part in range(parts):
        carried = ff_forward(
            part, parts, carried, seq_len, tie(nl, sent), hat, upstream, uw, ub, dw, g1, s1, db, g2, s2
        )
        sent = hops.send(carried[4])
    while not isinstance(sent, tuple):
        sent = hops.send(None)
    layer_output, act, slope, dbranch, final_sums, dr2_leads = carried
    loss_rows, fix, lead_sums = pair_loss(*sent, lead, lead_hat, lead_inv2, lead_inv, final_gain)

    *down_blocks, dbranch, down_sum = down_gradient(place, 4, act, dbranch, dr2_leads.reshape(-1, D), fix, seq_len)
    sent = down_blocks
    talls = [hidden // LANES] + [D // LANES] * 8
    down = all_sum(down_blocks)
    next(down)
    sent = (sent, down_blocks)
    down_kept = down_gradient(place, 0, act, tie(dbranch, sent))
    sent = down_kept
    sent = down.send(tie(down_kept, sent))
    dpre, up_sums, *up_blocks = hidden_gradient(place, tie(dbranch, sent), slope, dw, nl)
    sent = dpre
    sent = down.send(sent)
    up = all_sum(up_blocks[2:])
    next(up)
    sent = (sent, up_blocks[2:])
    stack, dctx, mixer = norm_one_backward(tie(dpre, sent), dbranch, hat, inv, uw, wo, g1)
    sent = dctx
    sent = down.send(sent)
    sent = up.send(tie(up_blocks[:2], sent))
    stack, qkv = attention_backward(seq_len, q, k, v, probs, tie(dctx, sent), stack)
    sent = stack
    value_blocks = square_gradient(place, [context, tokens], tie(stack, sent), (3, 2), None, "value_gradient")
    sent = value_blocks[2]
    sent = down.send(sent)
    value = all_sum(value_blocks[2:])
    next(value)
    sent = (sent, value_blocks[2:])
    sent = up.send(sent)
    final = jnp.sum(final_sums, axis=0)
    small = jnp.concatenate(
        [
            up_sums[0], mixer[2], mixer[0], mixer[1], final[2] + down_sum[0], final[0] + lead_sums[0],
            final[1] + lead_sums[1], qkv[0], qkv[2],
        ]
    ).reshape(-1, LANES)
    query_blocks = square_gradient(place, [tokens], tie(stack, sent), (0, 1), small, "query_gradient")
    sent = query_blocks[2]
    sent = value.send(tie(value_blocks[:2], sent))
    sent = up.send(sent)
    query = all_sum(query_blocks[2:])
    next(query)
    sent = (sent, query_blocks[2:])
    sent = down.send(sent)
    sent = query.send(tie(query_blocks[:2], sent))
    sent = value.send(sent)
    sent = up.send(sent)
    sent = down.send(sent)
    input_grad = input_gradient(tie(stack, sent), wq, wk, wv)
    sent = input_grad
    sent = value.send(sent)
    sent = query.send(sent)
    sent = up.send(sent)
    down_own = down.send(sent)
    sent = down_own
    sent = value.send(sent)
    down_out = spread(place, 0, tie(down_own, sent), [D], [], None, "down")
    sent = down_out
    sent = query.send(sent)
    sent = up.send(sent)
    sent = query.send(sent)
    sent = value.send(sent)
    sent = query.send(sent)
    down_out = spread(place, 4, down.send(sent), [D], [], down_out, "down")
    sent = down_out
    up_own = up.send(sent)
    sent = up_own
    sent = value.send(sent)
    up_out = spread(place, 0, tie(up_own, sent), [hidden], [], None, "up")
    sent = up_out
    sent = query.send(sent)
    up_out = spread(place, 4, up.send(sent), [hidden], [], up_out, "up")
    sent = up_out
    value_own = value.send(sent)
    sent = value_own
    value_out = spread(place, 0, tie(value_own, sent), [D] * 2, [], None, "value")
    sent = value_out
    value_out = spread(place, 4, value.send(sent), [D] * 2, [], value_out, "value")
    sent = value_out
    query_own = query.send(sent)
    sent = query_own
    query_out = spread(place, 0, tie(query_own, sent), [D] * 2, talls, None, "query")
    sent = query_out
    query_out = spread(place, 4, query.send(sent), [D] * 2, talls, query_out, "query")
    sent = query_out
    wq_grad, wk_grad, *smalls = query_out
    up_b, out_b, gain_one, shift_one, down_b, gain_two, shift_two, query_b, value_b = (each.reshape(-1) for each in smalls)
    return (
        layer_output[None], input_grad[None], loss_rows,
        wq_grad, query_b, wk_grad, value_out[1], value_b, value_out[0], out_b,
        gain_one, shift_one, up_out[0], up_b, down_out[0], down_b, gain_two, shift_two,
    )


def solution(mesh):
    split = P("stream", "dp", None)
    return jax.shard_map(
        shards,
        mesh=mesh,
        in_specs=(split, P("dp")) + (P(),) * 15 + (split,),
        out_specs=(split, split, P("stream", "dp")) + (P(),) * 15,
        check_vma=False,
    )
```

```python
import functools
import math

import jax
import jax.numpy as jnp
from jax import lax
from jax.experimental import pallas as pl
from jax.experimental.pallas import tpu as pltpu
from jax.sharding import PartitionSpec as P

D = 768
HEADS = 12
HD = 64
GROUPS = 109
LANES = 128

MARGIN = 0.3
LOGIT_SCALE = 30.0
NORM_EPS = 1e-12
UNIT_EPS = 1e-06
highest = lax.Precision.HIGHEST
low = jnp.bfloat16
full = jnp.float32


def dot(left, right):
    return lax.dot_general(left, right, (((1,), (0,)), ((), ())), preferred_element_type=full)


def dot_t(left, right):
    return lax.dot_general(left, right, (((1,), (1,)), ((), ())), preferred_element_type=full)


def t_dot(left, right):
    return lax.dot_general(left, right, (((0,), (0,)), ((), ())), preferred_element_type=full)


def mean_of(values):
    return jnp.sum(values, axis=-1, keepdims=True) * (1.0 / D)


def norm_stats(values):
    centred = values - mean_of(values)
    inv_std = lax.rsqrt(mean_of(centred * centred) + NORM_EPS)
    return centred * inv_std, inv_std


def norm_back(grad_hat, normed_hat, inv_std):
    return inv_std * (grad_hat - mean_of(grad_hat) - normed_hat * mean_of(grad_hat * normed_hat))


def normal_cdf(values):
    bell = jnp.exp(-0.5 * values * values)
    step = 1.0 / (1.0 + (0.3275911 / math.sqrt(2.0)) * jnp.abs(values))
    tail = 0.5 * 1.061405429
    for factor in (-1.453152027, 1.421413741, -0.284496736, 0.254829592):
        tail = tail * step + 0.5 * factor
    tail = tail * step * bell
    return jnp.where(values >= 0.0, 1.0 - tail, tail), bell


def gelu_and_slope(values):
    cdf, bell = normal_cdf(values)
    return values * cdf, cdf + values * bell * (1.0 / math.sqrt(2.0 * math.pi))


def columns_sum(values):
    return jnp.sum(values, axis=0, keepdims=True)


def line(ref, first=0):
    return jnp.concatenate([ref[pl.ds(first + k, 1), :] for k in range(D // LANES)], axis=1)


def fixed_spec(*shape):
    return pl.BlockSpec(shape, lambda *_: (0,) * len(shape))


def vector_spec(count=D):
    return fixed_spec(count // LANES, LANES)


def shape_of(*shape, dtype=low):
    return jax.ShapeDtypeStruct(shape, dtype)


def far(*shape, dtype=low):
    return pltpu.HBM(shape, dtype)


def near(*shape, dtype=low):
    return pltpu.VMEM(shape, dtype)


def params(grid_dims, mib=20):
    return pltpu.CompilerParams(dimension_semantics=("arbitrary",) * grid_dims, vmem_limit_bytes=mib << 20)


def cost(micros):
    return pl.CostEstimate(flops=int(micros * 0.02 * 1.15e9), bytes_accessed=1000, transcendentals=0)


def two_heads(block):
    lane = lax.broadcasted_iota(jnp.int32, block.shape, 1)
    zero = jnp.zeros_like(block)
    return jnp.concatenate([jnp.where(lane < HD, block, zero), jnp.where(lane < HD, zero, block)], axis=0)


def own_head(both):
    count = both.shape[0] // 2
    lane = lax.broadcasted_iota(jnp.int32, (count, both.shape[1]), 1)
    return jnp.where(lane < HD, both[:count], both[count:])


def cells_of(count, seq_len):
    return [
        (slice(start, start + seq_len), slice(first, first + 2 * HD))
        for first in range(0, D, 2 * HD)
        for start in range(0, count, seq_len)
    ]


def joined(pieces, count, seq_len):
    tall = count // seq_len
    columns = [jnp.concatenate(pieces[k : k + tall], axis=0) for k in range(0, len(pieces), tall)]
    return jnp.concatenate(columns, axis=1)


def attention_kernel(seq_len, x_ref, wq, wk, wv, wo, bq, bv, bo, gain, shift,
                     q_ref, k_ref, v_ref, p_ref, c_ref, nl_ref, hat_ref, inv_ref, nll_ref, hatl_ref):
    x = x_ref[...]
    count = x.shape[0]
    q = (dot(x, wq[...]) + line(bq)).astype(low)
    k = dot(x, wk[...]).astype(low)
    v = (dot(x, wv[...]) + line(bv)).astype(low)
    q_ref[...], k_ref[...], v_ref[...] = q, k, v
    cells = cells_of(count, seq_len)
    factor = 1.0 / math.sqrt(HD)
    scores = [dot_t(k[cell], two_heads(q[cell])) * factor for cell in cells]
    probs = []
    for cell, score in zip(cells, scores, strict=True):
        terms = jnp.exp(score - jnp.max(score, axis=0, keepdims=True))
        probs.append((terms * (1.0 / columns_sum(terms))).astype(low))
        p_ref[cell] = probs[-1]
    pieces = [own_head(t_dot(prob, v[cell])).astype(low) for cell, prob in zip(cells, probs, strict=True)]
    context = joined(pieces, count, seq_len)
    c_ref[...] = context
    hat, inv_std = norm_stats(x.astype(full) + dot(context, wo[...]) + line(bo))
    normed_low = (hat * line(gain) + line(shift)).astype(low)
    hat_ref[...] = hat
    inv_ref[...] = jnp.broadcast_to(inv_std, inv_ref.shape)
    nl_ref[...] = normed_low
    for s in range(count // seq_len):
        nll_ref[0, s : s + 1, :] = normed_low[s * seq_len : s * seq_len + 1, :].astype(full)
        hatl_ref[0, s : s + 1, :] = hat[s * seq_len : s * seq_len + 1, :]


def attention_forward(tokens, seq_len, wq, wk, wv, wo, *vectors):
    count = tokens.shape[0]
    rows = 256
    steps, leads = count // rows, rows // seq_len
    row, mat = pl.BlockSpec((rows, D), lambda i: (i, 0)), fixed_spec(D, D)
    lead = pl.BlockSpec((1, leads, D), lambda i: (i, 0, 0))
    return pl.pallas_call(
        functools.partial(attention_kernel, seq_len),
        grid=(steps,),
        in_specs=[row, mat, mat, mat, mat] + [vector_spec()] * 5,
        out_specs=[row] * 7 + [pl.BlockSpec((rows, LANES), lambda i: (i, 0)), lead, lead],
        out_shape=[far(count, D)] * 5
        + [far(count, D), far(count, D, dtype=full), far(count, LANES, dtype=full)]
        + [shape_of(steps, leads, D, dtype=full)] * 2,
        compiler_params=params(1, 20),
        name="attention_forward",
        cost_estimate=cost(10),
    )(tokens, wq, wk, wv, wo, *vectors)


def lead_kernel(nl_ref, hat_ref, uw, ub, dw, gain1, shift1, db, gain2, shift2,
                lead_ref, hat2_ref, inv2_ref, linv_ref, unit_ref, nl, acc):
    step = pl.program_id(0)

    @pl.when(step == 0)
    def _():
        hat = jnp.concatenate([hat_ref[k] for k in range(hat_ref.shape[0])], axis=0)
        nl[...] = jnp.concatenate([nl_ref[k] for k in range(nl_ref.shape[0])], axis=0).astype(low)
        acc[...] = hat * line(gain1) + line(shift1) + line(db)

    pre = dot(nl[...], uw[...]) + line(ub, step * (D // LANES))
    acc[...] += dot(gelu_and_slope(pre)[0].astype(low), dw[...])

    @pl.when(step == pl.num_programs(0) - 1)
    def _():
        hat, inv_std = norm_stats(acc[...])
        lead = hat * line(gain2) + line(shift2)
        lead_inv = lax.rsqrt(jnp.sum(lead * lead, axis=-1, keepdims=True) + UNIT_EPS)
        lead_ref[...] = lead
        hat2_ref[...] = hat
        inv2_ref[...] = jnp.broadcast_to(inv_std, inv2_ref.shape)
        linv_ref[...] = jnp.broadcast_to(lead_inv, linv_ref.shape)
        unit_ref[...] = (lead * lead_inv).astype(low)


def lead_forward(nl, hat, uw, ub, dw, *vectors):
    count = nl.shape[0] * nl.shape[1]
    hidden = uw.shape[1]
    row, lane = fixed_spec(count, D), fixed_spec(count, LANES)
    return pl.pallas_call(
        lead_kernel,
        grid=(hidden // D,),
        in_specs=[
            fixed_spec(*nl.shape), fixed_spec(*hat.shape),
            pl.BlockSpec((D, D), lambda j: (0, j)), vector_spec(hidden), pl.BlockSpec((D, D), lambda j: (j, 0)),
        ] + [vector_spec()] * 5,
        out_specs=[row, row, lane, lane, row],
        out_shape=[shape_of(count, D, dtype=full)] * 2
        + [shape_of(count, LANES, dtype=full)] * 2 + [shape_of(count, D)],
        scratch_shapes=[pltpu.VMEM((count, D), low), pltpu.VMEM((count, D), full)],
        compiler_params=params(1),
        name="lead_forward",
        cost_estimate=cost(3),
    )(nl, hat, uw, ub, dw, *vectors)


def ff_kernel(part, seq_len, nl_ref, uw, ub, dw, gain1, shift1, db, gain2, shift2, hat_far, up_far, *rest):
    out_ref, act_ref, slope_ref, low_ref, sums_ref, leads_ref, acc, hat_ref, up_ref, sems = rest[-10:]
    step = pl.program_id(0)
    rows = acc.shape[0]
    span = pl.ds(part * rows, rows)
    copies = [
        pltpu.make_async_copy(source.at[span, :], target, sems.at[k])
        for k, (source, target) in enumerate(((hat_far, hat_ref), (up_far, up_ref)))
    ]

    @pl.when(step == 0)
    def _():
        for copy in copies:
            copy.start()
        acc[...] = jnp.zeros_like(acc)

    value, slope = gelu_and_slope(dot(nl_ref[...], uw[...]) + line(ub, step * (D // LANES)))
    act = value.astype(low)
    slope_ref[...] = slope.astype(low)
    act_ref[...] = act
    acc[...] += dot(act, dw[...])

    @pl.when(step == pl.num_programs(0) - 1)
    def _():
        for copy in copies:
            copy.wait()
        normed = hat_ref[...] * line(gain1) + line(shift1)
        hat, inv_std = norm_stats(acc[...] + (normed + line(db)))
        gain = line(gain2)
        out_ref[...] = (hat * gain + line(shift2)).astype(low)
        grad = up_ref[...].astype(full)
        dr2 = norm_back(grad * gain, hat, inv_std)
        branch = dr2.astype(low)
        low_ref[...] = branch
        sums_ref[0, 0:1, :] = columns_sum(grad * hat)
        sums_ref[0, 1:2, :] = columns_sum(grad)
        sums_ref[0, 2:3, :] = columns_sum(branch.astype(full))
        for s in range(rows // seq_len):
            leads_ref[0, s : s + 1, :] = dr2[s * seq_len : s * seq_len + 1, :]


def ff_forward(part, parts, carried, seq_len, nl, hat, upstream, uw, ub, dw, *vectors):
    count = nl.shape[0]
    rows = count // parts
    hidden = uw.shape[1]
    row = pl.BlockSpec((rows, D), lambda j: (part, 0))
    wide = pl.BlockSpec((rows, D), lambda j: (part, j))
    anywhere = pl.BlockSpec(memory_space=pl.ANY)
    operands = [in_far(nl), uw, ub, dw, *vectors, in_far(hat), upstream]
    in_specs = [row, pl.BlockSpec((D, D), lambda j: (0, j)), vector_spec(hidden), pl.BlockSpec((D, D), lambda j: (j, 0))]
    in_specs += [vector_spec()] * 5 + [anywhere] * 2
    aliases = {}
    if carried is not None:
        aliases = {len(operands) + k: k for k in range(len(carried))}
        operands += list(carried)
        in_specs += [anywhere] * len(carried)
    sums = lambda tall: pl.BlockSpec((1, tall, D), lambda j: (part, 0, 0))
    return pl.pallas_call(
        functools.partial(ff_kernel, part, seq_len),
        grid=(hidden // D,),
        in_specs=in_specs,
        out_specs=[row, wide, wide, row, sums(8), sums(rows // seq_len)],
        scratch_shapes=[
            pltpu.VMEM((rows, D), full), pltpu.VMEM((rows, D), full), pltpu.VMEM((rows, D), low),
            pltpu.SemaphoreType.DMA((2,)),
        ],
        out_shape=[
            far(count, D), far(count, hidden), far(count, hidden),
            far(count, D), shape_of(parts, 8, D, dtype=full),
            shape_of(parts, rows // seq_len, D, dtype=full),
        ],
        input_output_aliases=aliases,
        compiler_params=params(1, 20),
        name=f"ff_forward_{part}",
        cost_estimate=cost(13),
    )(*operands)


def loss_kernel(seq_count, own_ref, other_ref, lead_ref, hat_ref, inv_ref, linv_ref, gain2, loss_ref, fix_ref, sums_ref):
    count = own_ref.shape[0]
    own, other = own_ref[:, :D], other_ref[:, :D]
    columns = own_ref[:, D : D + 1].astype(full)
    rows = dot_t(jnp.ones((8, LANES), low), own_ref[:, D:])[0:1] * (1.0 / LANES)
    same = columns == rows
    place = [lax.broadcasted_iota(jnp.int32, (count, count), axis) for axis in range(2)]
    diagonal = (place[0] == place[1]).astype(full)
    logits = LOGIT_SCALE * dot_t(own, other) - LOGIT_SCALE * MARGIN * diagonal
    masked = jnp.where(same, logits, -jnp.inf)
    col_top = jnp.max(masked, axis=0, keepdims=True)
    col_lse = col_top + jnp.log(columns_sum(jnp.exp(masked - col_top)))
    mine = masked[:seq_count]
    row_top = jnp.max(mine, axis=1, keepdims=True)
    row_lse = row_top + jnp.log(jnp.sum(jnp.exp(mine - row_top), axis=1, keepdims=True))
    mine_diag = diagonal[:seq_count]
    own_logit = jnp.sum(logits[:seq_count] * mine_diag, axis=1, keepdims=True)
    found = same.astype(full)
    row_weight = (count / GROUPS) / jnp.sum(found[:seq_count], axis=1, keepdims=True)
    col_weight = (count / GROUPS) / columns_sum(found)
    loss_ref[...] = jnp.broadcast_to(row_weight * (row_lse - own_logit), loss_ref.shape)
    dsims = row_weight * (jnp.exp(mine - row_lse) - mine_diag) + col_weight * (jnp.exp(mine - col_lse) - mine_diag)
    high = dsims.astype(low)
    rest = (dsims - high.astype(full)).astype(low)
    unit_grad = LOGIT_SCALE * (dot(high, other) + dot(rest, other))
    lead, lead_inv, hat = lead_ref[...], linv_ref[:, 0:1], hat_ref[...]
    cross = jnp.sum(lead * unit_grad, axis=-1, keepdims=True)
    lead_grad = lead_inv * unit_grad - lead_inv * lead_inv * lead_inv * cross * lead
    fix_ref[...] = norm_back(lead_grad * line(gain2), hat, inv_ref[:, 0:1])
    sums_ref[0:1, :] = columns_sum(lead_grad * hat)
    sums_ref[1:2, :] = columns_sum(lead_grad)


def pair_loss(own_side, other_side, lead, lead_hat, inv2, lead_inv, gain):
    seq_count = lead.shape[0]
    if own_side.shape[0] <= 512:
        loss, fix, sums = pl.pallas_call(
            functools.partial(loss_kernel, seq_count),
            out_shape=[
                shape_of(seq_count, LANES, dtype=full), shape_of(seq_count, D, dtype=full), shape_of(8, D, dtype=full)
            ],
            compiler_params=params(0),
            name="pair_loss",
            cost_estimate=cost(4),
        )(own_side, other_side, lead, lead_hat, inv2, lead_inv, in_far(gain.reshape(-1, LANES)))
        return loss[:, 0][None], fix, sums
    pairs_all = own_side.shape[0]
    groups = own_side[:, D].astype(full)
    same_group = groups[:, None] == groups[None, :]
    row_weight = pairs_all / GROUPS / jnp.sum(same_group.astype(full), axis=1)
    sim_scores = LOGIT_SCALE * jnp.einsum("id,jd->ij", own_side[:, :D], other_side[:, :D], preferred_element_type=full)
    place = jnp.arange(pairs_all, dtype=jnp.int32)
    diagonal = (place[:, None] == place[None, :]).astype(full)
    logits = sim_scores - LOGIT_SCALE * MARGIN * diagonal
    masked = jnp.where(same_group, logits, -jnp.inf)
    col_top = jnp.max(masked, axis=0, keepdims=True)
    col_lse = col_top + jnp.log(jnp.sum(jnp.exp(masked - col_top), axis=0, keepdims=True))
    own = masked[:seq_count]
    row_top = jnp.max(own, axis=1, keepdims=True)
    row_lse = row_top + jnp.log(jnp.sum(jnp.exp(own - row_top), axis=1, keepdims=True))
    own_diag = diagonal[:seq_count]
    own_logit = jnp.sum(logits[:seq_count] * own_diag, axis=1)
    loss_rows = (row_weight[:seq_count] * (row_lse[:, 0] - own_logit))[None]
    dsims = row_weight[:seq_count, None] * (jnp.exp(own - row_lse) - own_diag)
    dsims += row_weight[None, :] * (jnp.exp(own - col_lse) - own_diag)
    unit_grad = LOGIT_SCALE * jnp.dot(dsims, other_side[:, :D].astype(full), precision=highest)
    lead_inv = lead_inv[:, :1]
    cross = jnp.sum(lead * unit_grad, axis=-1, keepdims=True)
    lead_grad = lead_inv * unit_grad - lead_inv * lead_inv * lead_inv * cross * lead
    sums = jnp.stack([jnp.sum(lead_grad * lead_hat, axis=0), jnp.sum(lead_grad, axis=0)])
    return loss_rows, norm_back(lead_grad * gain[None], lead_hat, inv2[:, :1]), sums


def down_grad_kernel(seq_len, fresh, place, *refs):
    step = pl.program_id(0)
    if fresh:
        old_ref, leads_ref, fix_ref, act_ref, *outs, db_ref, sum_ref = refs

        @pl.when(step == 0)
        def _():
            db_ref[...] = old_ref[...]
            fixed = (leads_ref[...] + fix_ref[...]).astype(low)
            sum_ref[...] = columns_sum(fixed.astype(full) - leads_ref[...].astype(low).astype(full))
            for s in range(fix_ref.shape[0]):
                block = old_ref[s * seq_len : s * seq_len + 16, :]
                first = lax.broadcasted_iota(jnp.int32, block.shape, 0) == 0
                block = jnp.where(first, fixed[s : s + 1, :].astype(full), block.astype(full))
                db_ref[s * seq_len : s * seq_len + 16, :] = block.astype(low)
    else:
        db_ref, act_ref, *outs = refs
    grad = t_dot(act_ref[...], db_ref[...]).astype(low)
    tall = grad.shape[0]
    for rank in range(4):

        @pl.when(step == rank)
        def _(rank=rank):
            outs[rank // 2][rank % 2 * tall : (rank % 2 + 1) * tall, :] = grad


def down_gradient(place, first, act, dbranch, leads=None, fix=None, seq_len=None):
    count, hidden = act.shape
    tall = hidden // 8
    fresh = fix is not None
    operands = [dbranch] + ([leads, fix] if fresh else []) + [in_far(act)]
    moving = pl.BlockSpec((count, tall), lambda p, place: (0, place[first + p]))
    in_specs = [fixed_spec(*operand.shape) for operand in operands[:-1]] + [moving]
    out_specs = [fixed_spec(2 * tall, D)] * 2
    out_shape = [pltpu.VMEM((2 * tall, D), low)] * 2
    if fresh:
        out_specs += [fixed_spec(count, D), fixed_spec(1, D)]
        out_shape += [shape_of(count, D), shape_of(1, D, dtype=full)]
    return pl.pallas_call(
        functools.partial(down_grad_kernel, seq_len, fresh),
        grid_spec=pltpu.PrefetchScalarGridSpec(
            num_scalar_prefetch=1, grid=(4,), in_specs=in_specs, out_specs=out_specs
        ),
        out_shape=out_shape,
        compiler_params=params(1),
        name=f"down_grad_{first}",
        cost_estimate=cost(4),
    )(place, *operands)


def put_rows(place, grad_ref, outs, columns):
    tall = grad_ref.shape[0] // 8
    for rank in range(8):
        at = pl.multiple_of(place[rank] * tall, 16)
        outs[rank // 2][rank % 2 * tall : (rank % 2 + 1) * tall, columns] = grad_ref[pl.ds(at, tall), :]


def hidden_kernel(place, db_ref, slope_ref, dw, nl_ref, dpre_ref, sum_ref, *rest):
    *outs, scratch = rest
    dpre = (dot_t(db_ref[...], dw[...]) * slope_ref[...].astype(full)).astype(low)
    dpre_ref[...] = dpre
    sum_ref[0:1, :] = columns_sum(dpre.astype(full))
    scratch[...] = t_dot(nl_ref[...], dpre).astype(low)
    put_rows(place, scratch, outs, slice(None))


def hidden_gradient(place, dbranch, slope, dw, nl):
    count, hidden = slope.shape
    wide = pl.BlockSpec((count, D), lambda j, *_: (0, j))
    pair = D // 4
    return pl.pallas_call(
        hidden_kernel,
        grid_spec=pltpu.PrefetchScalarGridSpec(
            num_scalar_prefetch=1,
            grid=(hidden // D,),
            in_specs=[fixed_spec(count, D), wide, pl.BlockSpec((D, D), lambda j, *_: (j, 0)), fixed_spec(count, D)],
            out_specs=[wide] + [pl.BlockSpec((rows, D), lambda j, *_: (0, j)) for rows in (8, pair, pair, pair, pair)],
            scratch_shapes=[pltpu.VMEM((D, D), low)],
        ),
        out_shape=[far(count, hidden), shape_of(8, hidden, dtype=full)] + [shape_of(pair, hidden)] * 4,
        input_output_aliases={2: 0},
        compiler_params=params(1, 18),
        name="hidden_gradient",
        cost_estimate=cost(15),
    )(place, dbranch, in_far(slope), dw, in_far(nl))


def norm_one_kernel(dpre_ref, uw, gain1, wo_far, branch_far, hat_far, inv_far,
                    datt_ref, dctx_ref, sums_ref, acc, wo, branch_ref, hat_ref, inv_ref, sems):
    step = pl.program_id(0)
    copies = [
        pltpu.make_async_copy(source, target, sems.at[k])
        for k, (source, target) in enumerate(((wo_far, wo), (branch_far, branch_ref), (hat_far, hat_ref), (inv_far, inv_ref)))
    ]

    @pl.when(step == 0)
    def _():
        for copy in copies:
            copy.start()
        acc[...] = jnp.zeros_like(acc)

    acc[...] += dot_t(dpre_ref[...], uw[...])

    @pl.when(step == pl.num_programs(0) - 1)
    def _():
        for copy in copies:
            copy.wait()
        gain = line(gain1)
        totals = [jnp.zeros((1, D), full)] * 3
        for start in range(0, acc.shape[0], 256):
            rows = slice(start, start + 256)
            grad, hat = acc[rows, :] + branch_ref[rows, :].astype(full), hat_ref[rows, :]
            dr1 = norm_back(grad * gain, hat, inv_ref[rows, 0:1])
            datt = dr1.astype(low)
            datt_ref[0, rows, :] = datt
            dctx_ref[rows, :] = dot_t(datt, wo[...]).astype(low)
            totals = [
                total + columns_sum(part) for total, part in zip(totals, (grad * hat, grad, datt.astype(full)), strict=True)
            ]
        for rank, total in enumerate(totals):
            sums_ref[rank : rank + 1, :] = total


def norm_one_backward(dpre, dbranch, hat, inv, uw, wo, gain1):
    count, hidden = dpre.shape
    anywhere = pl.BlockSpec(memory_space=pl.ANY)
    return pl.pallas_call(
        norm_one_kernel,
        grid=(hidden // D,),
        in_specs=[
            pl.BlockSpec((count, D), lambda j: (0, j)), pl.BlockSpec((D, D), lambda j: (0, j)), vector_spec(), anywhere, anywhere, anywhere, anywhere,
        ],
        out_specs=[pl.BlockSpec((1, count, D), lambda j: (3, 0, 0)), fixed_spec(count, D), fixed_spec(8, D)],
        out_shape=[near(4, count, D), near(count, D), shape_of(8, D, dtype=full)],
        scratch_shapes=[
            pltpu.VMEM((count, D), full), pltpu.VMEM((D, D), low), pltpu.VMEM((count, D), low),
            pltpu.VMEM((count, D), full), pltpu.VMEM((count, LANES), full), pltpu.SemaphoreType.DMA((4,)),
        ],
        compiler_params=params(1, 24),
        name="norm_one_backward",
        cost_estimate=cost(13),
    )(in_far(dpre), uw, gain1, wo, dbranch, in_far(hat), in_far(inv))


def attention_back_kernel(seq_len, q_ref, k_ref, v_ref, p_ref, dc_ref, stack_ref, d_ref, sums):
    count = q_ref.shape[0]
    factor = 1.0 / math.sqrt(HD)

    @pl.when(pl.program_id(0) == 0)
    def _():
        sums[...] = jnp.zeros_like(sums)

    wide = 2 * 2 * HD

    @pl.loop(0, D // wide)
    def _(turn):
        lanes = pl.ds(pl.multiple_of(turn * wide, LANES), wide)
        q, k, v, probs, dctx = (ref[:, lanes] for ref in (q_ref, k_ref, v_ref, p_ref, dc_ref))
        cells = [
            (slice(start, start + seq_len), slice(first, first + 2 * HD))
            for first in range(0, wide, 2 * HD)
            for start in range(0, count, seq_len)
        ]
        spread_dctx = [two_heads(dctx[cell]) for cell in cells]
        dprobs = [dot_t(v[cell], both) for cell, both in zip(cells, spread_dctx, strict=True)]
        dvals = [dot(probs[cell], both).astype(low) for cell, both in zip(cells, spread_dctx, strict=True)]
        dscores = []
        for cell, dprob in zip(cells, dprobs, strict=True):
            prob = probs[cell].astype(full)
            dscores.append((prob * (dprob - columns_sum(prob * dprob))).astype(low))
        dkeys = [(dot(ds, two_heads(q[cell])) * factor).astype(low) for cell, ds in zip(cells, dscores, strict=True)]
        dqueries = [
            (own_head(t_dot(ds, k[cell])) * factor).astype(low) for cell, ds in zip(cells, dscores, strict=True)
        ]
        for rank, pieces in enumerate((dqueries, dkeys, dvals)):
            grad = joined(pieces, count, seq_len)
            d_ref[rank, :, lanes] = grad
            sums[rank : rank + 1, lanes] += columns_sum(grad.astype(full))


def attention_backward(seq_len, q, k, v, probs, dctx, stack):
    count = q.shape[0]
    rows = 256
    row = pl.BlockSpec((rows, D), lambda i: (i, 0))
    return pl.pallas_call(
        functools.partial(attention_back_kernel, seq_len),
        grid=(count // rows,),
        in_specs=[row] * 5 + [pl.BlockSpec(memory_space=pl.ANY)],
        out_specs=[pl.BlockSpec((3, rows, D), lambda i: (0, i, 0)), fixed_spec(8, D)],
        out_shape=[near(4, count, D), shape_of(8, D, dtype=full)],
        input_output_aliases={5: 0},
        compiler_params=params(1, 14),
        name="attention_backward",
        cost_estimate=cost(8),
    )(*map(in_near, (q, k, v, probs, dctx, stack)))


def square_grad_kernel(late, place, left_ref, d_ref, *rest):
    step = pl.program_id(0)
    if late:
        far_ref, *outs, scratch, late_ref, sem = rest
        copy = pltpu.make_async_copy(far_ref, late_ref, sem)

        @pl.when(step == 0)
        def _():
            copy.start()
            scratch[...] = t_dot(left_ref[...], d_ref[0]).astype(low)

        @pl.when(step == 1)
        def _():
            copy.wait()
            scratch[...] = t_dot(late_ref[...], d_ref[0]).astype(low)
    else:
        small_ref, *outs, scratch = rest
        scratch[...] = t_dot(left_ref[...], d_ref[0]).astype(low)

        @pl.when(step == 0)
        def _():
            tall = D // 8
            for rank in range(8):
                out_ref, first = outs[rank // 2], rank % 2 * tall
                out_ref[first : first + tall, 2 * D :] = jnp.zeros((tall, LANES), low)

                @pl.when(place[rank] == 0)
                def _(out_ref=out_ref, first=first):
                    out_ref[first : first + small_ref.shape[0], 2 * D :] = small_ref[...].astype(low)

    put_rows(place, scratch, outs, pl.ds(pl.multiple_of(step * D, LANES), D))


def square_gradient(place, lefts, stack, slots, small, name):
    count = lefts[0].shape[0]
    late = len(lefts) == 2
    pair, columns = D // 4, 2 * D + (0 if late else LANES)
    scratch = [pltpu.VMEM((D, D), low)]
    if late:
        scratch += [pltpu.VMEM((count, D), low), pltpu.SemaphoreType.DMA]
    return pl.pallas_call(
        functools.partial(square_grad_kernel, late),
        grid_spec=pltpu.PrefetchScalarGridSpec(
            num_scalar_prefetch=1,
            grid=(2,),
            in_specs=[
                fixed_spec(count, D),
                pl.BlockSpec((1, count, D), lambda j, *_: (slots[0] + j * (slots[1] - slots[0]), 0, 0)),
                pl.BlockSpec(memory_space=pl.ANY) if late else fixed_spec(*small.shape),
            ],
            out_specs=[fixed_spec(pair, columns)] * 4,
            scratch_shapes=scratch,
        ),
        out_shape=[shape_of(pair, columns)] * 4,
        compiler_params=params(1, 18),
        name=name,
        cost_estimate=cost(6),
    )(place, in_far(lefts[0]), in_near(stack), in_far(lefts[1]) if late else small)


def input_grad_kernel(d_ref, wq, wk, wv, out_ref):
    out_ref[...] = (
        d_ref[3].astype(full) + dot_t(d_ref[0], wq[...]) + dot_t(d_ref[1], wk[...]) + dot_t(d_ref[2], wv[...])
    )


def input_gradient(stack, wq, wk, wv):
    count = stack.shape[1]
    rows = 256
    mat = fixed_spec(D, D)
    return pl.pallas_call(
        input_grad_kernel,
        grid=(count // rows,),
        in_specs=[pl.BlockSpec((4, rows, D), lambda i: (0, i, 0))] + [mat] * 3,
        out_specs=pl.BlockSpec((rows, D), lambda i: (i, 0)),
        out_shape=far(count, D, dtype=full),
        compiler_params=params(1),
        name="input_gradient",
        cost_estimate=cost(6),
    )(in_near(stack), wq, wk, wv)


def spread_kernel(widths, talls, first, place, *refs):
    smalls = refs[len(refs) - len(talls) :]
    outs = refs[len(refs) - len(talls) - len(widths) : len(refs) - len(talls)]
    tall = outs[0].shape[0]
    held = refs[0].shape[0] // tall
    if first and talls:

        @pl.when(pl.program_id(0) == 0)
        def _():
            for ref, old in zip(smalls, refs[4 // held : 4 // held + len(talls)], strict=True):
                ref[...] = old[...]

    for rank in range(4):

        @pl.when(pl.program_id(0) == rank)
        def _(rank=rank):
            source, rows = refs[rank // held], rank % held * tall
            at = 0
            for ref, width in zip(outs, widths, strict=True):
                ref[...] = source[rows : rows + tall, at : at + width].astype(full)
                at += width
            if talls:

                @pl.when(place[first + rank] == 0)
                def _():
                    top = rows
                    for ref in smalls:
                        ref[...] = source[top : top + ref.shape[0], at:].astype(full)
                        top += ref.shape[0]


def spread(place, first, pairs, widths, talls, carried, name):
    tall = sum(pair.shape[0] for pair in pairs) // 4
    carried = list(carried or [])
    small = [fixed_spec(rows, LANES) for rows in talls]
    in_specs = [fixed_spec(*pair.shape) for pair in pairs]
    operands = list(pairs)
    if carried:
        operands += carried[len(widths) :] + carried[: len(widths)]
        in_specs += small + [pl.BlockSpec(memory_space=pl.ANY)] * len(widths)
    return pl.pallas_call(
        functools.partial(spread_kernel, widths, talls, first),
        grid_spec=pltpu.PrefetchScalarGridSpec(
            num_scalar_prefetch=1,
            grid=(4,),
            in_specs=in_specs,
            out_specs=[pl.BlockSpec((tall, width), lambda p, place: (place[first + p], 0)) for width in widths] + small,
        ),
        out_shape=[far(8 * tall, width, dtype=full) for width in widths]
        + [shape_of(rows, LANES, dtype=full) for rows in talls],
        input_output_aliases={1 + len(operands) - len(widths) + k: k for k in range(len(widths))} if carried else {},
        compiler_params=params(1),
        name=f"{name}_spread_{first}",
        cost_estimate=cost(3),
    )(place, *operands)


def places():
    half = lax.axis_index("stream")
    chip = lax.axis_index("dp")
    bits = (chip & 1, (chip >> 1) & 1)
    table = []
    for side in (half, 1 - half):
        first = jnp.where(side == 0, bits[0], bits[1])
        second = jnp.where(side == 0, bits[1], bits[0])
        table += [4 * side + 2 * (first ^ (k >> 1)) + (second ^ (k & 1)) for k in range(4)]
    return jnp.stack(table).astype(jnp.int32)


def chip_partner(bit_zero, bit_one):
    chips = lax.axis_size("dp")
    return [
        (half * chips + chip, half * chips + (chip ^ (bit_zero if half == 0 else bit_one)))
        for half in range(2)
        for chip in range(chips)
    ]


def core_partner():
    chips = lax.axis_size("dp")
    return [(half * chips + chip, (1 - half) * chips + chip) for half in range(2) for chip in range(chips)]


def swap(piece, pairs):
    return lax.ppermute(piece, ("stream", "dp"), pairs)


def add_low(left, right):
    return (left.astype(full) + right.astype(full)).astype(low)


def tie(value, after):
    return value if after is None else lax.optimization_barrier((value, after))[0]


def all_sum(sent):
    others = [swap(pair, core_partner()) for pair in sent]
    kept = yield sent
    pair = add_low(kept[1], others[1])
    other = swap(pair, chip_partner(1, 2))
    mine = add_low(kept[0], others[0])
    after = yield pair, mine
    tall = mine.shape[0] // 2
    mine = tie(mine, after)
    block = add_low(mine[tall:], other[tall:])
    mine = add_low(mine[:tall], other[:tall])
    other = swap(block, chip_partner(2, 1))
    after = yield block, mine
    bits = [1 << k for k in range(2, lax.axis_size("dp").bit_length() - 1)]
    for rank, pair in enumerate(zip(bits, bits[::-1], strict=True)):
        mine = add_low(tie(mine, after), other)
        other = swap(mine, chip_partner(*pair))
        after = (yield mine) if rank in (0, len(bits) - 1) else None
    mine = add_low(tie(mine, after), other)
    other = swap(mine, chip_partner(2, 1))
    after = yield mine
    pair = jnp.concatenate([tie(mine, after), other])
    other = swap(pair, chip_partner(1, 2))
    after = yield pair
    pairs = [tie(pair, after), other]
    others = [swap(each, core_partner()) for each in pairs]
    yield pairs
    yield others


def gather_rows(rows):
    chips = lax.axis_size("dp")
    bit = 1
    after = None
    while bit < chips:
        others = [swap(rows, chip_partner(k * bit, k * bit)) for k in range(1, 4) if k * bit < chips]
        after = yield rows
        rows = jnp.concatenate([tie(rows, after)] + others)
        bit *= 4
    other = swap(rows, core_partner())
    yield rows
    yield rows, other


def in_far(array):
    return pltpu.with_memory_space_constraint(array, pltpu.HBM)


def in_near(array):
    return pltpu.with_memory_space_constraint(array, pltpu.VMEM)


def shards(
    layer_input, pair_group, query_weight, query_bias, key_weight, value_weight, value_bias,
    out_weight, out_bias, mixer_gain, mixer_shift, up_weight, up_bias, down_weight, down_bias,
    final_gain, final_shift, upstream,
):
    count = layer_input.shape[1]
    seq_count = pair_group.shape[0]
    seq_len = count // seq_count
    hidden = up_bias.shape[0]
    tokens, upstream = in_far(layer_input[0]), in_far(upstream[0])
    wq, wk, wv, wo = map(in_far, (query_weight, key_weight, value_weight, out_weight))
    uw, dw = in_far(up_weight), in_far(down_weight)
    fold = lambda vector: in_far(vector.reshape(-1, LANES))
    bq, bv, bo, g1, s1 = map(fold, (query_bias, value_bias, out_bias, mixer_gain, mixer_shift))
    ub, db, g2, s2 = map(fold, (up_bias, down_bias, final_gain, final_shift))
    place = places()

    q, k, v, probs, context, nl, hat, inv, lead_nl, lead_hat = attention_forward(
        tokens, seq_len, wq, wk, wv, wo, bq, bv, bo, g1, s1
    )
    lead, lead_hat, lead_inv2, lead_inv, units = lead_forward(lead_nl, lead_hat, uw, ub, dw, g1, s1, db, g2, s2)
    ids = jnp.broadcast_to(pair_group.astype(low)[:, None], (seq_count, LANES))
    hops = gather_rows(jnp.concatenate([units, ids], axis=1))
    sent = next(hops)
    parts = 2
    carried = None
    for part in range(parts):
        carried = ff_forward(
            part, parts, carried, seq_len, tie(nl, sent), hat, upstream, uw, ub, dw, g1, s1, db, g2, s2
        )
        sent = hops.send(carried[4])
    while not isinstance(sent, tuple):
        sent = hops.send(None)
    layer_output, act, slope, dbranch, final_sums, dr2_leads = carried
    loss_rows, fix, lead_sums = pair_loss(*sent, lead, lead_hat, lead_inv2, lead_inv, final_gain)

    *down_blocks, dbranch, down_sum = down_gradient(place, 4, act, dbranch, dr2_leads.reshape(-1, D), fix, seq_len)
    sent = down_blocks
    talls = [hidden // LANES] + [D // LANES] * 8
    down = all_sum(down_blocks)
    next(down)
    sent = (sent, down_blocks)
    down_kept = down_gradient(place, 0, act, tie(dbranch, sent))
    sent = down_kept
    sent = down.send(tie(down_kept, sent))
    dpre, up_sums, *up_blocks = hidden_gradient(place, tie(dbranch, sent), slope, dw, nl)
    sent = dpre
    sent = down.send(sent)
    up = all_sum(up_blocks[2:])
    next(up)
    sent = (sent, up_blocks[2:])
    stack, dctx, mixer = norm_one_backward(tie(dpre, sent), dbranch, hat, inv, uw, wo, g1)
    sent = dctx
    sent = down.send(sent)
    sent = up.send(tie(up_blocks[:2], sent))
    stack, qkv = attention_backward(seq_len, q, k, v, probs, tie(dctx, sent), stack)
    sent = stack
    value_blocks = square_gradient(place, [context, tokens], tie(stack, sent), (3, 2), None, "value_gradient")
    sent = value_blocks[2]
    sent = down.send(sent)
    value = all_sum(value_blocks[2:])
    next(value)
    sent = (sent, value_blocks[2:])
    sent = up.send(sent)
    final = jnp.sum(final_sums, axis=0)
    small = jnp.concatenate(
        [
            up_sums[0], mixer[2], mixer[0], mixer[1], final[2] + down_sum[0], final[0] + lead_sums[0],
            final[1] + lead_sums[1], qkv[0], qkv[2],
        ]
    ).reshape(-1, LANES)
    query_blocks = square_gradient(place, [tokens], tie(stack, sent), (0, 1), small, "query_gradient")
    sent = query_blocks[2]
    sent = value.send(tie(value_blocks[:2], sent))
    sent = up.send(sent)
    query = all_sum(query_blocks[2:])
    next(query)
    sent = (sent, query_blocks[2:])
    sent = down.send(sent)
    sent = query.send(tie(query_blocks[:2], sent))
    sent = value.send(sent)
    sent = up.send(sent)
    sent = down.send(sent)
    input_grad = input_gradient(tie(stack, sent), wq, wk, wv)
    sent = input_grad
    sent = value.send(sent)
    sent = query.send(sent)
    sent = up.send(sent)
    down_own = down.send(sent)
    sent = down_own
    sent = value.send(sent)
    down_out = spread(place, 0, tie(down_own, sent), [D], [], None, "down")
    sent = down_out
    sent = query.send(sent)
    sent = up.send(sent)
    sent = query.send(sent)
    sent = value.send(sent)
    sent = query.send(sent)
    down_out = spread(place, 4, down.send(sent), [D], [], down_out, "down")
    sent = down_out
    up_own = up.send(sent)
    sent = up_own
    sent = value.send(sent)
    up_out = spread(place, 0, tie(up_own, sent), [hidden], [], None, "up")
    sent = up_out
    sent = query.send(sent)
    up_out = spread(place, 4, up.send(sent), [hidden], [], up_out, "up")
    sent = up_out
    value_own = value.send(sent)
    sent = value_own
    value_out = spread(place, 0, tie(value_own, sent), [D] * 2, [], None, "value")
    sent = value_out
    value_out = spread(place, 4, value.send(sent), [D] * 2, [], value_out, "value")
    sent = value_out
    query_own = query.send(sent)
    sent = query_own
    query_out = spread(place, 0, tie(query_own, sent), [D] * 2, talls, None, "query")
    sent = query_out
    query_out = spread(place, 4, query.send(sent), [D] * 2, talls, query_out, "query")
    sent = query_out
    wq_grad, wk_grad, *smalls = query_out
    up_b, out_b, gain_one, shift_one, down_b, gain_two, shift_two, query_b, value_b = (each.reshape(-1) for each in smalls)
    return (
        layer_output[None], input_grad[None], loss_rows,
        wq_grad, query_b, wk_grad, value_out[1], value_b, value_out[0], out_b,
        gain_one, shift_one, up_out[0], up_b, down_out[0], down_b, gain_two, shift_two,
    )


def solution(mesh):
    split = P("stream", "dp", None)
    return jax.shard_map(
        shards,
        mesh=mesh,
        in_specs=(split, P("dp")) + (P(),) * 15 + (split,),
        out_specs=(split, split, P("stream", "dp")) + (P(),) * 15,
        check_vma=False,
    )
```

```python
import functools
import math

import jax
import jax.numpy as jnp
from jax import lax
from jax.experimental import pallas as pl
from jax.experimental.pallas import tpu as pltpu
from jax.sharding import PartitionSpec as P

D = 768
HEADS = 12
HD = 64
GROUPS = 109
LANES = 128

MARGIN = 0.3
LOGIT_SCALE = 30.0
NORM_EPS = 1e-12
UNIT_EPS = 1e-06
highest = lax.Precision.HIGHEST
low = jnp.bfloat16
full = jnp.float32


def dot(left, right):
    return lax.dot_general(left, right, (((1,), (0,)), ((), ())), preferred_element_type=full)


def dot_t(left, right):
    return lax.dot_general(left, right, (((1,), (1,)), ((), ())), preferred_element_type=full)


def t_dot(left, right):
    return lax.dot_general(left, right, (((0,), (0,)), ((), ())), preferred_element_type=full)


def mean_of(values):
    return jnp.sum(values, axis=-1, keepdims=True) * (1.0 / D)


def norm_stats(values):
    centred = values - mean_of(values)
    inv_std = lax.rsqrt(mean_of(centred * centred) + NORM_EPS)
    return centred * inv_std, inv_std


def norm_back(grad_hat, normed_hat, inv_std):
    return inv_std * (grad_hat - mean_of(grad_hat) - normed_hat * mean_of(grad_hat * normed_hat))


def normal_cdf(values):
    bell = jnp.exp(-0.5 * values * values)
    step = 1.0 / (1.0 + (0.3275911 / math.sqrt(2.0)) * jnp.abs(values))
    tail = 0.5 * 1.061405429
    for factor in (-1.453152027, 1.421413741, -0.284496736, 0.254829592):
        tail = tail * step + 0.5 * factor
    tail = tail * step * bell
    return jnp.where(values >= 0.0, 1.0 - tail, tail), bell


def gelu_and_slope(values):
    cdf, bell = normal_cdf(values)
    return values * cdf, cdf + values * bell * (1.0 / math.sqrt(2.0 * math.pi))


def columns_sum(values):
    return jnp.sum(values, axis=0, keepdims=True)


def line(ref, first=0):
    return jnp.concatenate([ref[pl.ds(first + k, 1), :] for k in range(D // LANES)], axis=1)


def fixed_spec(*shape):
    return pl.BlockSpec(shape, lambda *_: (0,) * len(shape))


def vector_spec(count=D):
    return fixed_spec(count // LANES, LANES)


def shape_of(*shape, dtype=low):
    return jax.ShapeDtypeStruct(shape, dtype)


def far(*shape, dtype=low):
    return pltpu.HBM(shape, dtype)


def near(*shape, dtype=low):
    return pltpu.VMEM(shape, dtype)


def params(grid_dims, mib=20):
    return pltpu.CompilerParams(dimension_semantics=("arbitrary",) * grid_dims, vmem_limit_bytes=mib << 20)


def cost(micros):
    return pl.CostEstimate(flops=int(micros * 0.02 * 1.15e9), bytes_accessed=1000, transcendentals=0)


def two_heads(block):
    lane = lax.broadcasted_iota(jnp.int32, block.shape, 1)
    zero = jnp.zeros_like(block)
    return jnp.concatenate([jnp.where(lane < HD, block, zero), jnp.where(lane < HD, zero, block)], axis=0)


def own_head(both):
    count = both.shape[0] // 2
    lane = lax.broadcasted_iota(jnp.int32, (count, both.shape[1]), 1)
    return jnp.where(lane < HD, both[:count], both[count:])


def cells_of(count, seq_len):
    return [
        (slice(start, start + seq_len), slice(first, first + 2 * HD))
        for first in range(0, D, 2 * HD)
        for start in range(0, count, seq_len)
    ]


def joined(pieces, count, seq_len):
    tall = count // seq_len
    columns = [jnp.concatenate(pieces[k : k + tall], axis=0) for k in range(0, len(pieces), tall)]
    return jnp.concatenate(columns, axis=1)


def attention_kernel(seq_len, x_ref, wq, wk, wv, wo, bq, bv, bo, gain, shift,
                     q_ref, k_ref, v_ref, p_ref, c_ref, nl_ref, hat_ref, inv_ref, nll_ref, hatl_ref):
    x = x_ref[...]
    count = x.shape[0]
    q = (dot(x, wq[...]) + line(bq)).astype(low)
    k = dot(x, wk[...]).astype(low)
    v = (dot(x, wv[...]) + line(bv)).astype(low)
    q_ref[...], k_ref[...], v_ref[...] = q, k, v
    cells = cells_of(count, seq_len)
    factor = 1.0 / math.sqrt(HD)
    scores = [dot_t(k[cell], two_heads(q[cell])) * factor for cell in cells]
    probs = []
    for cell, score in zip(cells, scores, strict=True):
        terms = jnp.exp(score - jnp.max(score, axis=0, keepdims=True))
        probs.append((terms * (1.0 / columns_sum(terms))).astype(low))
        p_ref[cell] = probs[-1]
    pieces = [own_head(t_dot(prob, v[cell])).astype(low) for cell, prob in zip(cells, probs, strict=True)]
    context = joined(pieces, count, seq_len)
    c_ref[...] = context
    hat, inv_std = norm_stats(x.astype(full) + dot(context, wo[...]) + line(bo))
    normed_low = (hat * line(gain) + line(shift)).astype(low)
    hat_ref[...] = hat
    inv_ref[...] = jnp.broadcast_to(inv_std, inv_ref.shape)
    nl_ref[...] = normed_low
    for s in range(count // seq_len):
        nll_ref[0, s : s + 1, :] = normed_low[s * seq_len : s * seq_len + 1, :].astype(full)
        hatl_ref[0, s : s + 1, :] = hat[s * seq_len : s * seq_len + 1, :]


def attention_forward(tokens, seq_len, wq, wk, wv, wo, *vectors):
    count = tokens.shape[0]
    rows = 256
    steps, leads = count // rows, rows // seq_len
    row, mat = pl.BlockSpec((rows, D), lambda i: (i, 0)), fixed_spec(D, D)
    lead = pl.BlockSpec((1, leads, D), lambda i: (i, 0, 0))
    return pl.pallas_call(
        functools.partial(attention_kernel, seq_len),
        grid=(steps,),
        in_specs=[row, mat, mat, mat, mat] + [vector_spec()] * 5,
        out_specs=[row] * 7 + [pl.BlockSpec((rows, LANES), lambda i: (i, 0)), lead, lead],
        out_shape=[far(count, D)] * 5
        + [far(count, D), far(count, D, dtype=full), far(count, LANES, dtype=full)]
        + [shape_of(steps, leads, D, dtype=full)] * 2,
        compiler_params=params(1, 20),
        name="attention_forward",
        cost_estimate=cost(10),
    )(tokens, wq, wk, wv, wo, *vectors)


def lead_kernel(nl_ref, hat_ref, uw, ub, dw, gain1, shift1, db, gain2, shift2,
                lead_ref, hat2_ref, inv2_ref, linv_ref, unit_ref, nl, acc):
    step = pl.program_id(0)

    @pl.when(step == 0)
    def _():
        hat = jnp.concatenate([hat_ref[k] for k in range(hat_ref.shape[0])], axis=0)
        nl[...] = jnp.concatenate([nl_ref[k] for k in range(nl_ref.shape[0])], axis=0).astype(low)
        acc[...] = hat * line(gain1) + line(shift1) + line(db)

    pre = dot(nl[...], uw[...]) + line(ub, step * (D // LANES))
    acc[...] += dot(gelu_and_slope(pre)[0].astype(low), dw[...])

    @pl.when(step == pl.num_programs(0) - 1)
    def _():
        hat, inv_std = norm_stats(acc[...])
        lead = hat * line(gain2) + line(shift2)
        lead_inv = lax.rsqrt(jnp.sum(lead * lead, axis=-1, keepdims=True) + UNIT_EPS)
        lead_ref[...] = lead
        hat2_ref[...] = hat
        inv2_ref[...] = jnp.broadcast_to(inv_std, inv2_ref.shape)
        linv_ref[...] = jnp.broadcast_to(lead_inv, linv_ref.shape)
        unit_ref[...] = (lead * lead_inv).astype(low)


def lead_forward(nl, hat, uw, ub, dw, *vectors):
    count = nl.shape[0] * nl.shape[1]
    hidden = uw.shape[1]
    row, lane = fixed_spec(count, D), fixed_spec(count, LANES)
    return pl.pallas_call(
        lead_kernel,
        grid=(hidden // D,),
        in_specs=[
            fixed_spec(*nl.shape), fixed_spec(*hat.shape),
            pl.BlockSpec((D, D), lambda j: (0, j)), vector_spec(hidden), pl.BlockSpec((D, D), lambda j: (j, 0)),
        ] + [vector_spec()] * 5,
        out_specs=[row, row, lane, lane, row],
        out_shape=[shape_of(count, D, dtype=full)] * 2
        + [shape_of(count, LANES, dtype=full)] * 2 + [shape_of(count, D)],
        scratch_shapes=[pltpu.VMEM((count, D), low), pltpu.VMEM((count, D), full)],
        compiler_params=params(1),
        name="lead_forward",
        cost_estimate=cost(3),
    )(nl, hat, uw, ub, dw, *vectors)


def ff_kernel(part, seq_len, nl_ref, uw, ub, dw, gain1, shift1, db, gain2, shift2, hat_far, up_far, *rest):
    out_ref, act_ref, slope_ref, low_ref, sums_ref, leads_ref, acc, hat_ref, up_ref, sems = rest[-10:]
    step = pl.program_id(0)
    rows = acc.shape[0]
    span = pl.ds(part * rows, rows)
    copies = [
        pltpu.make_async_copy(source.at[span, :], target, sems.at[k])
        for k, (source, target) in enumerate(((hat_far, hat_ref), (up_far, up_ref)))
    ]

    @pl.when(step == 0)
    def _():
        for copy in copies:
            copy.start()
        acc[...] = jnp.zeros_like(acc)

    value, slope = gelu_and_slope(dot(nl_ref[...], uw[...]) + line(ub, step * (D // LANES)))
    act = value.astype(low)
    slope_ref[...] = slope.astype(low)
    act_ref[...] = act
    acc[...] += dot(act, dw[...])

    @pl.when(step == pl.num_programs(0) - 1)
    def _():
        for copy in copies:
            copy.wait()
        normed = hat_ref[...] * line(gain1) + line(shift1)
        hat, inv_std = norm_stats(acc[...] + (normed + line(db)))
        gain = line(gain2)
        out_ref[...] = (hat * gain + line(shift2)).astype(low)
        grad = up_ref[...].astype(full)
        dr2 = norm_back(grad * gain, hat, inv_std)
        branch = dr2.astype(low)
        low_ref[...] = branch
        sums_ref[0, 0:1, :] = columns_sum(grad * hat)
        sums_ref[0, 1:2, :] = columns_sum(grad)
        sums_ref[0, 2:3, :] = columns_sum(branch.astype(full))
        for s in range(rows // seq_len):
            leads_ref[0, s : s + 1, :] = dr2[s * seq_len : s * seq_len + 1, :]


def ff_forward(part, parts, carried, seq_len, nl, hat, upstream, uw, ub, dw, *vectors):
    count = nl.shape[0]
    rows = count // parts
    hidden = uw.shape[1]
    row = pl.BlockSpec((rows, D), lambda j: (part, 0))
    wide = pl.BlockSpec((rows, D), lambda j: (part, j))
    anywhere = pl.BlockSpec(memory_space=pl.ANY)
    operands = [in_far(nl), uw, ub, dw, *vectors, in_far(hat), upstream]
    in_specs = [row, pl.BlockSpec((D, D), lambda j: (0, j)), vector_spec(hidden), pl.BlockSpec((D, D), lambda j: (j, 0))]
    in_specs += [vector_spec()] * 5 + [anywhere] * 2
    aliases = {}
    if carried is not None:
        aliases = {len(operands) + k: k for k in range(len(carried))}
        operands += list(carried)
        in_specs += [anywhere] * len(carried)
    sums = lambda tall: pl.BlockSpec((1, tall, D), lambda j: (part, 0, 0))
    return pl.pallas_call(
        functools.partial(ff_kernel, part, seq_len),
        grid=(hidden // D,),
        in_specs=in_specs,
        out_specs=[row, wide, wide, row, sums(8), sums(rows // seq_len)],
        scratch_shapes=[
            pltpu.VMEM((rows, D), full), pltpu.VMEM((rows, D), full), pltpu.VMEM((rows, D), low),
            pltpu.SemaphoreType.DMA((2,)),
        ],
        out_shape=[
            far(count, D), far(count, hidden), far(count, hidden),
            far(count, D), shape_of(parts, 8, D, dtype=full),
            shape_of(parts, rows // seq_len, D, dtype=full),
        ],
        input_output_aliases=aliases,
        compiler_params=params(1, 20),
        name=f"ff_forward_{part}",
        cost_estimate=cost(13),
    )(*operands)


def loss_kernel(seq_count, own_ref, other_ref, lead_ref, hat_ref, inv_ref, linv_ref, gain2, loss_ref, fix_ref, sums_ref):
    count = own_ref.shape[0]
    own, other = own_ref[:, :D], other_ref[:, :D]
    columns = own_ref[:, D : D + 1].astype(full)
    rows = dot_t(jnp.ones((8, LANES), low), own_ref[:, D:])[0:1] * (1.0 / LANES)
    same = columns == rows
    place = [lax.broadcasted_iota(jnp.int32, (count, count), axis) for axis in range(2)]
    diagonal = (place[0] == place[1]).astype(full)
    logits = LOGIT_SCALE * dot_t(own, other) - LOGIT_SCALE * MARGIN * diagonal
    masked = jnp.where(same, logits, -jnp.inf)
    col_top = jnp.max(masked, axis=0, keepdims=True)
    col_lse = col_top + jnp.log(columns_sum(jnp.exp(masked - col_top)))
    mine = masked[:seq_count]
    row_top = jnp.max(mine, axis=1, keepdims=True)
    row_lse = row_top + jnp.log(jnp.sum(jnp.exp(mine - row_top), axis=1, keepdims=True))
    mine_diag = diagonal[:seq_count]
    own_logit = jnp.sum(logits[:seq_count] * mine_diag, axis=1, keepdims=True)
    found = same.astype(full)
    row_weight = (count / GROUPS) / jnp.sum(found[:seq_count], axis=1, keepdims=True)
    col_weight = (count / GROUPS) / columns_sum(found)
    loss_ref[...] = jnp.broadcast_to(row_weight * (row_lse - own_logit), loss_ref.shape)
    dsims = row_weight * (jnp.exp(mine - row_lse) - mine_diag) + col_weight * (jnp.exp(mine - col_lse) - mine_diag)
    high = dsims.astype(low)
    rest = (dsims - high.astype(full)).astype(low)
    unit_grad = LOGIT_SCALE * (dot(high, other) + dot(rest, other))
    lead, lead_inv, hat = lead_ref[...], linv_ref[:, 0:1], hat_ref[...]
    cross = jnp.sum(lead * unit_grad, axis=-1, keepdims=True)
    lead_grad = lead_inv * unit_grad - lead_inv * lead_inv * lead_inv * cross * lead
    fix_ref[...] = norm_back(lead_grad * line(gain2), hat, inv_ref[:, 0:1])
    sums_ref[0:1, :] = columns_sum(lead_grad * hat)
    sums_ref[1:2, :] = columns_sum(lead_grad)


def pair_loss(own_side, other_side, lead, lead_hat, inv2, lead_inv, gain):
    seq_count = lead.shape[0]
    if own_side.shape[0] <= 512:
        loss, fix, sums = pl.pallas_call(
            functools.partial(loss_kernel, seq_count),
            out_shape=[
                shape_of(seq_count, LANES, dtype=full), shape_of(seq_count, D, dtype=full), shape_of(8, D, dtype=full)
            ],
            compiler_params=params(0),
            name="pair_loss",
            cost_estimate=cost(4),
        )(own_side, other_side, lead, lead_hat, inv2, lead_inv, in_far(gain.reshape(-1, LANES)))
        return loss[:, 0][None], fix, sums
    pairs_all = own_side.shape[0]
    groups = own_side[:, D].astype(full)
    same_group = groups[:, None] == groups[None, :]
    row_weight = pairs_all / GROUPS / jnp.sum(same_group.astype(full), axis=1)
    sim_scores = LOGIT_SCALE * jnp.einsum("id,jd->ij", own_side[:, :D], other_side[:, :D], preferred_element_type=full)
    place = jnp.arange(pairs_all, dtype=jnp.int32)
    diagonal = (place[:, None] == place[None, :]).astype(full)
    logits = sim_scores - LOGIT_SCALE * MARGIN * diagonal
    masked = jnp.where(same_group, logits, -jnp.inf)
    col_top = jnp.max(masked, axis=0, keepdims=True)
    col_lse = col_top + jnp.log(jnp.sum(jnp.exp(masked - col_top), axis=0, keepdims=True))
    own = masked[:seq_count]
    row_top = jnp.max(own, axis=1, keepdims=True)
    row_lse = row_top + jnp.log(jnp.sum(jnp.exp(own - row_top), axis=1, keepdims=True))
    own_diag = diagonal[:seq_count]
    own_logit = jnp.sum(logits[:seq_count] * own_diag, axis=1)
    loss_rows = (row_weight[:seq_count] * (row_lse[:, 0] - own_logit))[None]
    dsims = row_weight[:seq_count, None] * (jnp.exp(own - row_lse) - own_diag)
    dsims += row_weight[None, :] * (jnp.exp(own - col_lse) - own_diag)
    unit_grad = LOGIT_SCALE * jnp.dot(dsims, other_side[:, :D].astype(full), precision=highest)
    lead_inv = lead_inv[:, :1]
    cross = jnp.sum(lead * unit_grad, axis=-1, keepdims=True)
    lead_grad = lead_inv * unit_grad - lead_inv * lead_inv * lead_inv * cross * lead
    sums = jnp.stack([jnp.sum(lead_grad * lead_hat, axis=0), jnp.sum(lead_grad, axis=0)])
    return loss_rows, norm_back(lead_grad * gain[None], lead_hat, inv2[:, :1]), sums


def down_grad_kernel(seq_len, fresh, place, *refs):
    step = pl.program_id(0)
    if fresh:
        old_ref, leads_ref, fix_ref, act_ref, *outs, db_ref, sum_ref = refs

        @pl.when(step == 0)
        def _():
            db_ref[...] = old_ref[...]
            fixed = (leads_ref[...] + fix_ref[...]).astype(low)
            sum_ref[...] = columns_sum(fixed.astype(full) - leads_ref[...].astype(low).astype(full))
            for s in range(fix_ref.shape[0]):
                block = old_ref[s * seq_len : s * seq_len + 16, :]
                first = lax.broadcasted_iota(jnp.int32, block.shape, 0) == 0
                block = jnp.where(first, fixed[s : s + 1, :].astype(full), block.astype(full))
                db_ref[s * seq_len : s * seq_len + 16, :] = block.astype(low)
    else:
        db_ref, act_ref, *outs = refs
    grad = t_dot(act_ref[...], db_ref[...]).astype(low)
    tall = grad.shape[0]
    for rank in range(4):

        @pl.when(step == rank)
        def _(rank=rank):
            outs[rank // 2][rank % 2 * tall : (rank % 2 + 1) * tall, :] = grad


def down_gradient(place, first, act, dbranch, leads=None, fix=None, seq_len=None):
    count, hidden = act.shape
    tall = hidden // 8
    fresh = fix is not None
    operands = [dbranch] + ([leads, fix] if fresh else []) + [in_far(act)]
    moving = pl.BlockSpec((count, tall), lambda p, place: (0, place[first + p]))
    in_specs = [fixed_spec(*operand.shape) for operand in operands[:-1]] + [moving]
    out_specs = [fixed_spec(2 * tall, D)] * 2
    out_shape = [pltpu.VMEM((2 * tall, D), low)] * 2
    if fresh:
        out_specs += [fixed_spec(count, D), fixed_spec(1, D)]
        out_shape += [shape_of(count, D), shape_of(1, D, dtype=full)]
    return pl.pallas_call(
        functools.partial(down_grad_kernel, seq_len, fresh),
        grid_spec=pltpu.PrefetchScalarGridSpec(
            num_scalar_prefetch=1, grid=(4,), in_specs=in_specs, out_specs=out_specs
        ),
        out_shape=out_shape,
        compiler_params=params(1),
        name=f"down_grad_{first}",
        cost_estimate=cost(4),
    )(place, *operands)


def put_rows(place, grad_ref, outs, columns):
    tall = grad_ref.shape[0] // 8
    for rank in range(8):
        at = pl.multiple_of(place[rank] * tall, 16)
        outs[rank // 2][rank % 2 * tall : (rank % 2 + 1) * tall, columns] = grad_ref[pl.ds(at, tall), :]


def hidden_kernel(place, db_ref, slope_ref, dw, nl_ref, dpre_ref, sum_ref, *rest):
    *outs, scratch = rest
    dpre = (dot_t(db_ref[...], dw[...]) * slope_ref[...].astype(full)).astype(low)
    dpre_ref[...] = dpre
    sum_ref[0:1, :] = columns_sum(dpre.astype(full))
    scratch[...] = t_dot(nl_ref[...], dpre).astype(low)
    put_rows(place, scratch, outs, slice(None))


def hidden_gradient(place, dbranch, slope, dw, nl):
    count, hidden = slope.shape
    wide = pl.BlockSpec((count, D), lambda j, *_: (0, j))
    pair = D // 4
    return pl.pallas_call(
        hidden_kernel,
        grid_spec=pltpu.PrefetchScalarGridSpec(
            num_scalar_prefetch=1,
            grid=(hidden // D,),
            in_specs=[fixed_spec(count, D), wide, pl.BlockSpec((D, D), lambda j, *_: (j, 0)), fixed_spec(count, D)],
            out_specs=[wide] + [pl.BlockSpec((rows, D), lambda j, *_: (0, j)) for rows in (8, pair, pair, pair, pair)],
            scratch_shapes=[pltpu.VMEM((D, D), low)],
        ),
        out_shape=[far(count, hidden), shape_of(8, hidden, dtype=full)] + [shape_of(pair, hidden)] * 4,
        input_output_aliases={2: 0},
        compiler_params=params(1, 18),
        name="hidden_gradient",
        cost_estimate=cost(15),
    )(place, dbranch, in_far(slope), dw, in_far(nl))


def norm_one_kernel(dpre_ref, uw, gain1, wo_far, branch_far, hat_far, inv_far,
                    datt_ref, dctx_ref, sums_ref, acc, wo, branch_ref, hat_ref, inv_ref, sems):
    step = pl.program_id(0)
    copies = [
        pltpu.make_async_copy(source, target, sems.at[k])
        for k, (source, target) in enumerate(((wo_far, wo), (branch_far, branch_ref), (hat_far, hat_ref), (inv_far, inv_ref)))
    ]

    @pl.when(step == 0)
    def _():
        for copy in copies:
            copy.start()
        acc[...] = jnp.zeros_like(acc)

    acc[...] += dot_t(dpre_ref[...], uw[...])

    @pl.when(step == pl.num_programs(0) - 1)
    def _():
        for copy in copies:
            copy.wait()
        gain = line(gain1)
        totals = [jnp.zeros((1, D), full)] * 3
        for start in range(0, acc.shape[0], 256):
            rows = slice(start, start + 256)
            grad, hat = acc[rows, :] + branch_ref[rows, :].astype(full), hat_ref[rows, :]
            dr1 = norm_back(grad * gain, hat, inv_ref[rows, 0:1])
            datt = dr1.astype(low)
            datt_ref[0, rows, :] = datt
            dctx_ref[rows, :] = dot_t(datt, wo[...]).astype(low)
            totals = [
                total + columns_sum(part) for total, part in zip(totals, (grad * hat, grad, datt.astype(full)), strict=True)
            ]
        for rank, total in enumerate(totals):
            sums_ref[rank : rank + 1, :] = total


def norm_one_backward(dpre, dbranch, hat, inv, uw, wo, gain1):
    count, hidden = dpre.shape
    anywhere = pl.BlockSpec(memory_space=pl.ANY)
    return pl.pallas_call(
        norm_one_kernel,
        grid=(hidden // D,),
        in_specs=[
            pl.BlockSpec((count, D), lambda j: (0, j)), pl.BlockSpec((D, D), lambda j: (0, j)), vector_spec(), anywhere, anywhere, anywhere, anywhere,
        ],
        out_specs=[pl.BlockSpec((1, count, D), lambda j: (3, 0, 0)), fixed_spec(count, D), fixed_spec(8, D)],
        out_shape=[near(4, count, D), near(count, D), shape_of(8, D, dtype=full)],
        scratch_shapes=[
            pltpu.VMEM((count, D), full), pltpu.VMEM((D, D), low), pltpu.VMEM((count, D), low),
            pltpu.VMEM((count, D), full), pltpu.VMEM((count, LANES), full), pltpu.SemaphoreType.DMA((4,)),
        ],
        compiler_params=params(1, 24),
        name="norm_one_backward",
        cost_estimate=cost(13),
    )(in_far(dpre), uw, gain1, wo, dbranch, in_far(hat), in_far(inv))


def attention_back_kernel(seq_len, q_ref, k_ref, v_ref, p_ref, dc_ref, stack_ref, d_ref, sums):
    count = q_ref.shape[0]
    factor = 1.0 / math.sqrt(HD)

    @pl.when(pl.program_id(0) == 0)
    def _():
        sums[...] = jnp.zeros_like(sums)

    wide = 2 * 2 * HD

    @pl.loop(0, D // wide)
    def _(turn):
        lanes = pl.ds(pl.multiple_of(turn * wide, LANES), wide)
        q, k, v, probs, dctx = (ref[:, lanes] for ref in (q_ref, k_ref, v_ref, p_ref, dc_ref))
        cells = [
            (slice(start, start + seq_len), slice(first, first + 2 * HD))
            for first in range(0, wide, 2 * HD)
            for start in range(0, count, seq_len)
        ]
        spread_dctx = [two_heads(dctx[cell]) for cell in cells]
        dprobs = [dot_t(v[cell], both) for cell, both in zip(cells, spread_dctx, strict=True)]
        dvals = [dot(probs[cell], both).astype(low) for cell, both in zip(cells, spread_dctx, strict=True)]
        dscores = []
        for cell, dprob in zip(cells, dprobs, strict=True):
            prob = probs[cell].astype(full)
            dscores.append((prob * (dprob - columns_sum(prob * dprob))).astype(low))
        dkeys = [(dot(ds, two_heads(q[cell])) * factor).astype(low) for cell, ds in zip(cells, dscores, strict=True)]
        dqueries = [
            (own_head(t_dot(ds, k[cell])) * factor).astype(low) for cell, ds in zip(cells, dscores, strict=True)
        ]
        for rank, pieces in enumerate((dqueries, dkeys, dvals)):
            grad = joined(pieces, count, seq_len)
            d_ref[rank, :, lanes] = grad
            sums[rank : rank + 1, lanes] += columns_sum(grad.astype(full))


def attention_backward(seq_len, q, k, v, probs, dctx, stack):
    count = q.shape[0]
    rows = 256
    row = pl.BlockSpec((rows, D), lambda i: (i, 0))
    return pl.pallas_call(
        functools.partial(attention_back_kernel, seq_len),
        grid=(count // rows,),
        in_specs=[row] * 5 + [pl.BlockSpec(memory_space=pl.ANY)],
        out_specs=[pl.BlockSpec((3, rows, D), lambda i: (0, i, 0)), fixed_spec(8, D)],
        out_shape=[near(4, count, D), shape_of(8, D, dtype=full)],
        input_output_aliases={5: 0},
        compiler_params=params(1, 14),
        name="attention_backward",
        cost_estimate=cost(8),
    )(*map(in_near, (q, k, v, probs, dctx, stack)))


def square_grad_kernel(late, place, left_ref, d_ref, *rest):
    step = pl.program_id(0)
    if late:
        far_ref, *outs, scratch, late_ref, sem = rest
        copy = pltpu.make_async_copy(far_ref, late_ref, sem)

        @pl.when(step == 0)
        def _():
            copy.start()
            scratch[...] = t_dot(left_ref[...], d_ref[0]).astype(low)

        @pl.when(step == 1)
        def _():
            copy.wait()
            scratch[...] = t_dot(late_ref[...], d_ref[0]).astype(low)
    else:
        small_ref, *outs, scratch = rest
        scratch[...] = t_dot(left_ref[...], d_ref[0]).astype(low)

        @pl.when(step == 0)
        def _():
            tall = D // 8
            for rank in range(8):
                out_ref, first = outs[rank // 2], rank % 2 * tall
                out_ref[first : first + tall, 2 * D :] = jnp.zeros((tall, LANES), low)

                @pl.when(place[rank] == 0)
                def _(out_ref=out_ref, first=first):
                    out_ref[first : first + small_ref.shape[0], 2 * D :] = small_ref[...].astype(low)

    put_rows(place, scratch, outs, pl.ds(pl.multiple_of(step * D, LANES), D))


def square_gradient(place, lefts, stack, slots, small, name):
    count = lefts[0].shape[0]
    late = len(lefts) == 2
    pair, columns = D // 4, 2 * D + (0 if late else LANES)
    scratch = [pltpu.VMEM((D, D), low)]
    if late:
        scratch += [pltpu.VMEM((count, D), low), pltpu.SemaphoreType.DMA]
    return pl.pallas_call(
        functools.partial(square_grad_kernel, late),
        grid_spec=pltpu.PrefetchScalarGridSpec(
            num_scalar_prefetch=1,
            grid=(2,),
            in_specs=[
                fixed_spec(count, D),
                pl.BlockSpec((1, count, D), lambda j, *_: (slots[0] + j * (slots[1] - slots[0]), 0, 0)),
                pl.BlockSpec(memory_space=pl.ANY) if late else fixed_spec(*small.shape),
            ],
            out_specs=[fixed_spec(pair, columns)] * 4,
            scratch_shapes=scratch,
        ),
        out_shape=[shape_of(pair, columns)] * 4,
        compiler_params=params(1, 18),
        name=name,
        cost_estimate=cost(6),
    )(place, in_far(lefts[0]), in_near(stack), in_far(lefts[1]) if late else small)


def input_grad_kernel(d_ref, wq, wk, wv, out_ref):
    out_ref[...] = (
        d_ref[3].astype(full) + dot_t(d_ref[0], wq[...]) + dot_t(d_ref[1], wk[...]) + dot_t(d_ref[2], wv[...])
    )


def input_gradient(stack, wq, wk, wv):
    count = stack.shape[1]
    rows = 256
    mat = fixed_spec(D, D)
    return pl.pallas_call(
        input_grad_kernel,
        grid=(count // rows,),
        in_specs=[pl.BlockSpec((4, rows, D), lambda i: (0, i, 0))] + [mat] * 3,
        out_specs=pl.BlockSpec((rows, D), lambda i: (i, 0)),
        out_shape=far(count, D, dtype=full),
        compiler_params=params(1),
        name="input_gradient",
        cost_estimate=cost(6),
    )(in_near(stack), wq, wk, wv)


def spread_kernel(widths, talls, first, place, *refs):
    smalls = refs[len(refs) - len(talls) :]
    outs = refs[len(refs) - len(talls) - len(widths) : len(refs) - len(talls)]
    tall = outs[0].shape[0]
    held = refs[0].shape[0] // tall
    if first and talls:

        @pl.when(pl.program_id(0) == 0)
        def _():
            for ref, old in zip(smalls, refs[4 // held : 4 // held + len(talls)], strict=True):
                ref[...] = old[...]

    for rank in range(4):

        @pl.when(pl.program_id(0) == rank)
        def _(rank=rank):
            source, rows = refs[rank // held], rank % held * tall
            at = 0
            for ref, width in zip(outs, widths, strict=True):
                ref[...] = source[rows : rows + tall, at : at + width].astype(full)
                at += width
            if talls:

                @pl.when(place[first + rank] == 0)
                def _():
                    top = rows
                    for ref in smalls:
                        ref[...] = source[top : top + ref.shape[0], at:].astype(full)
                        top += ref.shape[0]


def spread(place, first, pairs, widths, talls, carried, name):
    tall = sum(pair.shape[0] for pair in pairs) // 4
    carried = list(carried or [])
    small = [fixed_spec(rows, LANES) for rows in talls]
    in_specs = [fixed_spec(*pair.shape) for pair in pairs]
    operands = list(pairs)
    if carried:
        operands += carried[len(widths) :] + carried[: len(widths)]
        in_specs += small + [pl.BlockSpec(memory_space=pl.ANY)] * len(widths)
    return pl.pallas_call(
        functools.partial(spread_kernel, widths, talls, first),
        grid_spec=pltpu.PrefetchScalarGridSpec(
            num_scalar_prefetch=1,
            grid=(4,),
            in_specs=in_specs,
            out_specs=[pl.BlockSpec((tall, width), lambda p, place: (place[first + p], 0)) for width in widths] + small,
        ),
        out_shape=[far(8 * tall, width, dtype=full) for width in widths]
        + [shape_of(rows, LANES, dtype=full) for rows in talls],
        input_output_aliases={1 + len(operands) - len(widths) + k: k for k in range(len(widths))} if carried else {},
        compiler_params=params(1),
        name=f"{name}_spread_{first}",
        cost_estimate=cost(3),
    )(place, *operands)


def places():
    half = lax.axis_index("stream")
    chip = lax.axis_index("dp")
    bits = (chip & 1, (chip >> 1) & 1)
    table = []
    for side in (half, 1 - half):
        first = jnp.where(side == 0, bits[0], bits[1])
        second = jnp.where(side == 0, bits[1], bits[0])
        table += [4 * side + 2 * (first ^ (k >> 1)) + (second ^ (k & 1)) for k in range(4)]
    return jnp.stack(table).astype(jnp.int32)


def chip_partner(bit_zero, bit_one):
    chips = lax.axis_size("dp")
    return [
        (half * chips + chip, half * chips + (chip ^ (bit_zero if half == 0 else bit_one)))
        for half in range(2)
        for chip in range(chips)
    ]


def core_partner():
    chips = lax.axis_size("dp")
    return [(half * chips + chip, (1 - half) * chips + chip) for half in range(2) for chip in range(chips)]


def swap(piece, pairs):
    return lax.ppermute(piece, ("stream", "dp"), pairs)


def add_low(left, right):
    return (left.astype(full) + right.astype(full)).astype(low)


def tie(value, after):
    return value if after is None else lax.optimization_barrier((value, after))[0]


def all_sum(sent):
    others = [swap(pair, core_partner()) for pair in sent]
    kept = yield sent
    pair = add_low(kept[1], others[1])
    other = swap(pair, chip_partner(1, 2))
    mine = add_low(kept[0], others[0])
    after = yield pair, mine
    tall = mine.shape[0] // 2
    mine = tie(mine, after)
    block = add_low(mine[tall:], other[tall:])
    mine = add_low(mine[:tall], other[:tall])
    other = swap(block, chip_partner(2, 1))
    after = yield block, mine
    bits = [1 << k for k in range(2, lax.axis_size("dp").bit_length() - 1)]
    for rank, pair in enumerate(zip(bits, bits[::-1], strict=True)):
        mine = add_low(tie(mine, after), other)
        other = swap(mine, chip_partner(*pair))
        after = (yield mine) if rank in (0, len(bits) - 1) else None
    mine = add_low(tie(mine, after), other)
    other = swap(mine, chip_partner(2, 1))
    after = yield mine
    pair = jnp.concatenate([tie(mine, after), other])
    other = swap(pair, chip_partner(1, 2))
    after = yield pair
    pairs = [tie(pair, after), other]
    others = [swap(each, core_partner()) for each in pairs]
    yield pairs
    yield others


def gather_rows(rows):
    chips = lax.axis_size("dp")
    bit = 1
    after = None
    while bit < chips:
        others = [swap(rows, chip_partner(k * bit, k * bit)) for k in range(1, 4) if k * bit < chips]
        after = yield rows
        rows = jnp.concatenate([tie(rows, after)] + others)
        bit *= 4
    other = swap(rows, core_partner())
    yield rows
    yield rows, other


def in_far(array):
    return pltpu.with_memory_space_constraint(array, pltpu.HBM)


def in_near(array):
    return pltpu.with_memory_space_constraint(array, pltpu.VMEM)


def shards(
    layer_input, pair_group, query_weight, query_bias, key_weight, value_weight, value_bias,
    out_weight, out_bias, mixer_gain, mixer_shift, up_weight, up_bias, down_weight, down_bias,
    final_gain, final_shift, upstream,
):
    count = layer_input.shape[1]
    seq_count = pair_group.shape[0]
    seq_len = count // seq_count
    hidden = up_bias.shape[0]
    tokens, upstream = in_far(layer_input[0]), in_far(upstream[0])
    wq, wk, wv, wo = map(in_far, (query_weight, key_weight, value_weight, out_weight))
    uw, dw = in_far(up_weight), in_far(down_weight)
    fold = lambda vector: in_far(vector.reshape(-1, LANES))
    bq, bv, bo, g1, s1 = map(fold, (query_bias, value_bias, out_bias, mixer_gain, mixer_shift))
    ub, db, g2, s2 = map(fold, (up_bias, down_bias, final_gain, final_shift))
    place = places()

    q, k, v, probs, context, nl, hat, inv, lead_nl, lead_hat = attention_forward(
        tokens, seq_len, wq, wk, wv, wo, bq, bv, bo, g1, s1
    )
    lead, lead_hat, lead_inv2, lead_inv, units = lead_forward(lead_nl, lead_hat, uw, ub, dw, g1, s1, db, g2, s2)
    ids = jnp.broadcast_to(pair_group.astype(low)[:, None], (seq_count, LANES))
    hops = gather_rows(jnp.concatenate([units, ids], axis=1))
    sent = next(hops)
    parts = 2
    carried = None
    for part in range(parts):
        carried = ff_forward(
            part, parts, carried, seq_len, tie(nl, sent), hat, upstream, uw, ub, dw, g1, s1, db, g2, s2
        )
        sent = hops.send(carried[4])
    while not isinstance(sent, tuple):
        sent = hops.send(None)
    layer_output, act, slope, dbranch, final_sums, dr2_leads = carried
    loss_rows, fix, lead_sums = pair_loss(*sent, lead, lead_hat, lead_inv2, lead_inv, final_gain)

    *down_blocks, dbranch, down_sum = down_gradient(place, 4, act, dbranch, dr2_leads.reshape(-1, D), fix, seq_len)
    sent = down_blocks
    talls = [hidden // LANES] + [D // LANES] * 8
    down = all_sum(down_blocks)
    next(down)
    sent = (sent, down_blocks)
    down_kept = down_gradient(place, 0, act, tie(dbranch, sent))
    sent = down_kept
    sent = down.send(tie(down_kept, sent))
    dpre, up_sums, *up_blocks = hidden_gradient(place, tie(dbranch, sent), slope, dw, nl)
    sent = dpre
    sent = down.send(sent)
    up = all_sum(up_blocks[2:])
    next(up)
    sent = (sent, up_blocks[2:])
    stack, dctx, mixer = norm_one_backward(tie(dpre, sent), dbranch, hat, inv, uw, wo, g1)
    sent = dctx
    sent = down.send(sent)
    sent = up.send(tie(up_blocks[:2], sent))
    stack, qkv = attention_backward(seq_len, q, k, v, probs, tie(dctx, sent), stack)
    sent = stack
    value_blocks = square_gradient(place, [context, tokens], tie(stack, sent), (3, 2), None, "value_gradient")
    sent = value_blocks[2]
    sent = down.send(sent)
    value = all_sum(value_blocks[2:])
    next(value)
    sent = (sent, value_blocks[2:])
    sent = up.send(sent)
    final = jnp.sum(final_sums, axis=0)
    small = jnp.concatenate(
        [
            up_sums[0], mixer[2], mixer[0], mixer[1], final[2] + down_sum[0], final[0] + lead_sums[0],
            final[1] + lead_sums[1], qkv[0], qkv[2],
        ]
    ).reshape(-1, LANES)
    query_blocks = square_gradient(place, [tokens], tie(stack, sent), (0, 1), small, "query_gradient")
    sent = query_blocks[2]
    sent = value.send(tie(value_blocks[:2], sent))
    sent = up.send(sent)
    query = all_sum(query_blocks[2:])
    next(query)
    sent = (sent, query_blocks[2:])
    sent = down.send(sent)
    sent = query.send(tie(query_blocks[:2], sent))
    sent = value.send(sent)
    sent = up.send(sent)
    sent = down.send(sent)
    input_grad = input_gradient(tie(stack, sent), wq, wk, wv)
    sent = input_grad
    sent = value.send(sent)
    sent = query.send(sent)
    sent = up.send(sent)
    down_own = down.send(sent)
    sent = down_own
    sent = value.send(sent)
    sent = query.send(sent)
    sent = up.send(sent)
    down_out = spread(place, 0, tie(down_own, sent), [D], [], None, "down")
    sent = down_out
    sent = query.send(sent)
    sent = value.send(sent)
    sent = query.send(sent)
    down_out = spread(place, 4, down.send(sent), [D], [], down_out, "down")
    sent = down_out
    up_own = up.send(sent)
    sent = up_own
    sent = value.send(sent)
    up_out = spread(place, 0, tie(up_own, sent), [hidden], [], None, "up")
    sent = up_out
    sent = query.send(sent)
    up_out = spread(place, 4, up.send(sent), [hidden], [], up_out, "up")
    sent = up_out
    value_own = value.send(sent)
    sent = value_own
    value_out = spread(place, 0, tie(value_own, sent), [D] * 2, [], None, "value")
    sent = value_out
    value_out = spread(place, 4, value.send(sent), [D] * 2, [], value_out, "value")
    sent = value_out
    query_own = query.send(sent)
    sent = query_own
    query_out = spread(place, 0, tie(query_own, sent), [D] * 2, talls, None, "query")
    sent = query_out
    query_out = spread(place, 4, query.send(sent), [D] * 2, talls, query_out, "query")
    sent = query_out
    wq_grad, wk_grad, *smalls = query_out
    up_b, out_b, gain_one, shift_one, down_b, gain_two, shift_two, query_b, value_b = (each.reshape(-1) for each in smalls)
    return (
        layer_output[None], input_grad[None], loss_rows,
        wq_grad, query_b, wk_grad, value_out[1], value_b, value_out[0], out_b,
        gain_one, shift_one, up_out[0], up_b, down_out[0], down_b, gain_two, shift_two,
    )


def solution(mesh):
    split = P("stream", "dp", None)
    return jax.shard_map(
        shards,
        mesh=mesh,
        in_specs=(split, P("dp")) + (P(),) * 15 + (split,),
        out_specs=(split, split, P("stream", "dp")) + (P(),) * 15,
        check_vma=False,
    )
```

```python
import functools
import math

import jax
import jax.numpy as jnp
from jax import lax
from jax.experimental import pallas as pl
from jax.experimental.pallas import tpu as pltpu
from jax.sharding import PartitionSpec as P

D = 768
HEADS = 12
HD = 64
GROUPS = 109
LANES = 128

MARGIN = 0.3
LOGIT_SCALE = 30.0
NORM_EPS = 1e-12
UNIT_EPS = 1e-06
highest = lax.Precision.HIGHEST
low = jnp.bfloat16
full = jnp.float32


def dot(left, right):
    return lax.dot_general(left, right, (((1,), (0,)), ((), ())), preferred_element_type=full)


def dot_t(left, right):
    return lax.dot_general(left, right, (((1,), (1,)), ((), ())), preferred_element_type=full)


def t_dot(left, right):
    return lax.dot_general(left, right, (((0,), (0,)), ((), ())), preferred_element_type=full)


def mean_of(values):
    return jnp.sum(values, axis=-1, keepdims=True) * (1.0 / D)


def norm_stats(values):
    centred = values - mean_of(values)
    inv_std = lax.rsqrt(mean_of(centred * centred) + NORM_EPS)
    return centred * inv_std, inv_std


def norm_back(grad_hat, normed_hat, inv_std):
    return inv_std * (grad_hat - mean_of(grad_hat) - normed_hat * mean_of(grad_hat * normed_hat))


def normal_cdf(values):
    bell = jnp.exp(-0.5 * values * values)
    step = 1.0 / (1.0 + (0.3275911 / math.sqrt(2.0)) * jnp.abs(values))
    tail = 0.5 * 1.061405429
    for factor in (-1.453152027, 1.421413741, -0.284496736, 0.254829592):
        tail = tail * step + 0.5 * factor
    tail = tail * step * bell
    return jnp.where(values >= 0.0, 1.0 - tail, tail), bell


def gelu_and_slope(values):
    cdf, bell = normal_cdf(values)
    return values * cdf, cdf + values * bell * (1.0 / math.sqrt(2.0 * math.pi))


def columns_sum(values):
    return jnp.sum(values, axis=0, keepdims=True)


def line(ref, first=0):
    return jnp.concatenate([ref[pl.ds(first + k, 1), :] for k in range(D // LANES)], axis=1)


def fixed_spec(*shape):
    return pl.BlockSpec(shape, lambda *_: (0,) * len(shape))


def vector_spec(count=D):
    return fixed_spec(count // LANES, LANES)


def shape_of(*shape, dtype=low):
    return jax.ShapeDtypeStruct(shape, dtype)


def far(*shape, dtype=low):
    return pltpu.HBM(shape, dtype)


def near(*shape, dtype=low):
    return pltpu.VMEM(shape, dtype)


def params(grid_dims, mib=20):
    return pltpu.CompilerParams(dimension_semantics=("arbitrary",) * grid_dims, vmem_limit_bytes=mib << 20)


def cost(micros):
    return pl.CostEstimate(flops=int(micros * 0.02 * 1.15e9), bytes_accessed=1000, transcendentals=0)


def two_heads(block):
    lane = lax.broadcasted_iota(jnp.int32, block.shape, 1)
    zero = jnp.zeros_like(block)
    return jnp.concatenate([jnp.where(lane < HD, block, zero), jnp.where(lane < HD, zero, block)], axis=0)


def own_head(both):
    count = both.shape[0] // 2
    lane = lax.broadcasted_iota(jnp.int32, (count, both.shape[1]), 1)
    return jnp.where(lane < HD, both[:count], both[count:])


def cells_of(count, seq_len):
    return [
        (slice(start, start + seq_len), slice(first, first + 2 * HD))
        for first in range(0, D, 2 * HD)
        for start in range(0, count, seq_len)
    ]


def joined(pieces, count, seq_len):
    tall = count // seq_len
    columns = [jnp.concatenate(pieces[k : k + tall], axis=0) for k in range(0, len(pieces), tall)]
    return jnp.concatenate(columns, axis=1)


def attention_kernel(seq_len, x_ref, wq, wk, wv, wo, bq, bv, bo, gain, shift,
                     q_ref, k_ref, v_ref, p_ref, c_ref, nl_ref, hat_ref, inv_ref, nll_ref, hatl_ref):
    x = x_ref[...]
    count = x.shape[0]
    q = (dot(x, wq[...]) + line(bq)).astype(low)
    k = dot(x, wk[...]).astype(low)
    v = (dot(x, wv[...]) + line(bv)).astype(low)
    q_ref[...], k_ref[...], v_ref[...] = q, k, v
    cells = cells_of(count, seq_len)
    factor = 1.0 / math.sqrt(HD)
    scores = [dot_t(k[cell], two_heads(q[cell])) * factor for cell in cells]
    probs = []
    for cell, score in zip(cells, scores, strict=True):
        terms = jnp.exp(score - jnp.max(score, axis=0, keepdims=True))
        probs.append((terms * (1.0 / columns_sum(terms))).astype(low))
        p_ref[cell] = probs[-1]
    pieces = [own_head(t_dot(prob, v[cell])).astype(low) for cell, prob in zip(cells, probs, strict=True)]
    context = joined(pieces, count, seq_len)
    c_ref[...] = context
    hat, inv_std = norm_stats(x.astype(full) + dot(context, wo[...]) + line(bo))
    normed_low = (hat * line(gain) + line(shift)).astype(low)
    hat_ref[...] = hat
    inv_ref[...] = jnp.broadcast_to(inv_std, inv_ref.shape)
    nl_ref[...] = normed_low
    for s in range(count // seq_len):
        nll_ref[0, s : s + 1, :] = normed_low[s * seq_len : s * seq_len + 1, :].astype(full)
        hatl_ref[0, s : s + 1, :] = hat[s * seq_len : s * seq_len + 1, :]


def attention_forward(tokens, seq_len, wq, wk, wv, wo, *vectors):
    count = tokens.shape[0]
    rows = 256
    steps, leads = count // rows, rows // seq_len
    row, mat = pl.BlockSpec((rows, D), lambda i: (i, 0)), fixed_spec(D, D)
    lead = pl.BlockSpec((1, leads, D), lambda i: (i, 0, 0))
    return pl.pallas_call(
        functools.partial(attention_kernel, seq_len),
        grid=(steps,),
        in_specs=[row, mat, mat, mat, mat] + [vector_spec()] * 5,
        out_specs=[row] * 7 + [pl.BlockSpec((rows, LANES), lambda i: (i, 0)), lead, lead],
        out_shape=[far(count, D)] * 5
        + [far(count, D), far(count, D, dtype=full), far(count, LANES, dtype=full)]
        + [shape_of(steps, leads, D, dtype=full)] * 2,
        compiler_params=params(1, 20),
        name="attention_forward",
        cost_estimate=cost(10),
    )(tokens, wq, wk, wv, wo, *vectors)


def lead_kernel(nl_ref, hat_ref, uw, ub, dw, gain1, shift1, db, gain2, shift2,
                lead_ref, hat2_ref, inv2_ref, linv_ref, unit_ref, nl, acc):
    step = pl.program_id(0)

    @pl.when(step == 0)
    def _():
        hat = jnp.concatenate([hat_ref[k] for k in range(hat_ref.shape[0])], axis=0)
        nl[...] = jnp.concatenate([nl_ref[k] for k in range(nl_ref.shape[0])], axis=0).astype(low)
        acc[...] = hat * line(gain1) + line(shift1) + line(db)

    pre = dot(nl[...], uw[...]) + line(ub, step * (D // LANES))
    acc[...] += dot(gelu_and_slope(pre)[0].astype(low), dw[...])

    @pl.when(step == pl.num_programs(0) - 1)
    def _():
        hat, inv_std = norm_stats(acc[...])
        lead = hat * line(gain2) + line(shift2)
        lead_inv = lax.rsqrt(jnp.sum(lead * lead, axis=-1, keepdims=True) + UNIT_EPS)
        lead_ref[...] = lead
        hat2_ref[...] = hat
        inv2_ref[...] = jnp.broadcast_to(inv_std, inv2_ref.shape)
        linv_ref[...] = jnp.broadcast_to(lead_inv, linv_ref.shape)
        unit_ref[...] = (lead * lead_inv).astype(low)


def lead_forward(nl, hat, uw, ub, dw, *vectors):
    count = nl.shape[0] * nl.shape[1]
    hidden = uw.shape[1]
    row, lane = fixed_spec(count, D), fixed_spec(count, LANES)
    return pl.pallas_call(
        lead_kernel,
        grid=(hidden // D,),
        in_specs=[
            fixed_spec(*nl.shape), fixed_spec(*hat.shape),
            pl.BlockSpec((D, D), lambda j: (0, j)), vector_spec(hidden), pl.BlockSpec((D, D), lambda j: (j, 0)),
        ] + [vector_spec()] * 5,
        out_specs=[row, row, lane, lane, row],
        out_shape=[shape_of(count, D, dtype=full)] * 2
        + [shape_of(count, LANES, dtype=full)] * 2 + [shape_of(count, D)],
        scratch_shapes=[pltpu.VMEM((count, D), low), pltpu.VMEM((count, D), full)],
        compiler_params=params(1),
        name="lead_forward",
        cost_estimate=cost(3),
    )(nl, hat, uw, ub, dw, *vectors)


def ff_kernel(part, seq_len, nl_ref, uw, ub, dw, gain1, shift1, db, gain2, shift2, hat_far, up_far, *rest):
    out_ref, act_ref, slope_ref, low_ref, sums_ref, leads_ref, acc, hat_ref, up_ref, sems = rest[-10:]
    step = pl.program_id(0)
    rows = acc.shape[0]
    span = pl.ds(part * rows, rows)
    copies = [
        pltpu.make_async_copy(source.at[span, :], target, sems.at[k])
        for k, (source, target) in enumerate(((hat_far, hat_ref), (up_far, up_ref)))
    ]

    @pl.when(step == 0)
    def _():
        for copy in copies:
            copy.start()
        acc[...] = jnp.zeros_like(acc)

    value, slope = gelu_and_slope(dot(nl_ref[...], uw[...]) + line(ub, step * (D // LANES)))
    act = value.astype(low)
    slope_ref[...] = slope.astype(low)
    act_ref[...] = act
    acc[...] += dot(act, dw[...])

    @pl.when(step == pl.num_programs(0) - 1)
    def _():
        for copy in copies:
            copy.wait()
        normed = hat_ref[...] * line(gain1) + line(shift1)
        hat, inv_std = norm_stats(acc[...] + (normed + line(db)))
        gain = line(gain2)
        out_ref[...] = (hat * gain + line(shift2)).astype(low)
        grad = up_ref[...].astype(full)
        dr2 = norm_back(grad * gain, hat, inv_std)
        branch = dr2.astype(low)
        low_ref[...] = branch
        sums_ref[0, 0:1, :] = columns_sum(grad * hat)
        sums_ref[0, 1:2, :] = columns_sum(grad)
        sums_ref[0, 2:3, :] = columns_sum(branch.astype(full))
        for s in range(rows // seq_len):
            leads_ref[0, s : s + 1, :] = dr2[s * seq_len : s * seq_len + 1, :]


def ff_forward(part, parts, carried, seq_len, nl, hat, upstream, uw, ub, dw, *vectors):
    count = nl.shape[0]
    rows = count // parts
    hidden = uw.shape[1]
    row = pl.BlockSpec((rows, D), lambda j: (part, 0))
    wide = pl.BlockSpec((rows, D), lambda j: (part, j))
    anywhere = pl.BlockSpec(memory_space=pl.ANY)
    operands = [in_far(nl), uw, ub, dw, *vectors, in_far(hat), upstream]
    in_specs = [row, pl.BlockSpec((D, D), lambda j: (0, j)), vector_spec(hidden), pl.BlockSpec((D, D), lambda j: (j, 0))]
    in_specs += [vector_spec()] * 5 + [anywhere] * 2
    aliases = {}
    if carried is not None:
        aliases = {len(operands) + k: k for k in range(len(carried))}
        operands += list(carried)
        in_specs += [anywhere] * len(carried)
    sums = lambda tall: pl.BlockSpec((1, tall, D), lambda j: (part, 0, 0))
    return pl.pallas_call(
        functools.partial(ff_kernel, part, seq_len),
        grid=(hidden // D,),
        in_specs=in_specs,
        out_specs=[row, wide, wide, row, sums(8), sums(rows // seq_len)],
        scratch_shapes=[
            pltpu.VMEM((rows, D), full), pltpu.VMEM((rows, D), full), pltpu.VMEM((rows, D), low),
            pltpu.SemaphoreType.DMA((2,)),
        ],
        out_shape=[
            far(count, D), far(count, hidden), far(count, hidden),
            far(count, D), shape_of(parts, 8, D, dtype=full),
            shape_of(parts, rows // seq_len, D, dtype=full),
        ],
        input_output_aliases=aliases,
        compiler_params=params(1, 20),
        name=f"ff_forward_{part}",
        cost_estimate=cost(13),
    )(*operands)


def loss_kernel(seq_count, own_ref, other_ref, lead_ref, hat_ref, inv_ref, linv_ref, gain2, loss_ref, fix_ref, sums_ref):
    count = own_ref.shape[0]
    own, other = own_ref[:, :D], other_ref[:, :D]
    columns = own_ref[:, D : D + 1].astype(full)
    rows = dot_t(jnp.ones((8, LANES), low), own_ref[:, D:])[0:1] * (1.0 / LANES)
    same = columns == rows
    place = [lax.broadcasted_iota(jnp.int32, (count, count), axis) for axis in range(2)]
    diagonal = (place[0] == place[1]).astype(full)
    logits = LOGIT_SCALE * dot_t(own, other) - LOGIT_SCALE * MARGIN * diagonal
    masked = jnp.where(same, logits, -jnp.inf)
    col_top = jnp.max(masked, axis=0, keepdims=True)
    col_lse = col_top + jnp.log(columns_sum(jnp.exp(masked - col_top)))
    mine = masked[:seq_count]
    row_top = jnp.max(mine, axis=1, keepdims=True)
    row_lse = row_top + jnp.log(jnp.sum(jnp.exp(mine - row_top), axis=1, keepdims=True))
    mine_diag = diagonal[:seq_count]
    own_logit = jnp.sum(logits[:seq_count] * mine_diag, axis=1, keepdims=True)
    found = same.astype(full)
    row_weight = (count / GROUPS) / jnp.sum(found[:seq_count], axis=1, keepdims=True)
    col_weight = (count / GROUPS) / columns_sum(found)
    loss_ref[...] = jnp.broadcast_to(row_weight * (row_lse - own_logit), loss_ref.shape)
    dsims = row_weight * (jnp.exp(mine - row_lse) - mine_diag) + col_weight * (jnp.exp(mine - col_lse) - mine_diag)
    high = dsims.astype(low)
    rest = (dsims - high.astype(full)).astype(low)
    unit_grad = LOGIT_SCALE * (dot(high, other) + dot(rest, other))
    lead, lead_inv, hat = lead_ref[...], linv_ref[:, 0:1], hat_ref[...]
    cross = jnp.sum(lead * unit_grad, axis=-1, keepdims=True)
    lead_grad = lead_inv * unit_grad - lead_inv * lead_inv * lead_inv * cross * lead
    fix_ref[...] = norm_back(lead_grad * line(gain2), hat, inv_ref[:, 0:1])
    sums_ref[0:1, :] = columns_sum(lead_grad * hat)
    sums_ref[1:2, :] = columns_sum(lead_grad)


def pair_loss(own_side, other_side, lead, lead_hat, inv2, lead_inv, gain):
    seq_count = lead.shape[0]
    if own_side.shape[0] <= 512:
        loss, fix, sums = pl.pallas_call(
            functools.partial(loss_kernel, seq_count),
            out_shape=[
                shape_of(seq_count, LANES, dtype=full), shape_of(seq_count, D, dtype=full), shape_of(8, D, dtype=full)
            ],
            compiler_params=params(0),
            name="pair_loss",
            cost_estimate=cost(4),
        )(own_side, other_side, lead, lead_hat, inv2, lead_inv, in_far(gain.reshape(-1, LANES)))
        return loss[:, 0][None], fix, sums
    pairs_all = own_side.shape[0]
    groups = own_side[:, D].astype(full)
    same_group = groups[:, None] == groups[None, :]
    row_weight = pairs_all / GROUPS / jnp.sum(same_group.astype(full), axis=1)
    sim_scores = LOGIT_SCALE * jnp.einsum("id,jd->ij", own_side[:, :D], other_side[:, :D], preferred_element_type=full)
    place = jnp.arange(pairs_all, dtype=jnp.int32)
    diagonal = (place[:, None] == place[None, :]).astype(full)
    logits = sim_scores - LOGIT_SCALE * MARGIN * diagonal
    masked = jnp.where(same_group, logits, -jnp.inf)
    col_top = jnp.max(masked, axis=0, keepdims=True)
    col_lse = col_top + jnp.log(jnp.sum(jnp.exp(masked - col_top), axis=0, keepdims=True))
    own = masked[:seq_count]
    row_top = jnp.max(own, axis=1, keepdims=True)
    row_lse = row_top + jnp.log(jnp.sum(jnp.exp(own - row_top), axis=1, keepdims=True))
    own_diag = diagonal[:seq_count]
    own_logit = jnp.sum(logits[:seq_count] * own_diag, axis=1)
    loss_rows = (row_weight[:seq_count] * (row_lse[:, 0] - own_logit))[None]
    dsims = row_weight[:seq_count, None] * (jnp.exp(own - row_lse) - own_diag)
    dsims += row_weight[None, :] * (jnp.exp(own - col_lse) - own_diag)
    unit_grad = LOGIT_SCALE * jnp.dot(dsims, other_side[:, :D].astype(full), precision=highest)
    lead_inv = lead_inv[:, :1]
    cross = jnp.sum(lead * unit_grad, axis=-1, keepdims=True)
    lead_grad = lead_inv * unit_grad - lead_inv * lead_inv * lead_inv * cross * lead
    sums = jnp.stack([jnp.sum(lead_grad * lead_hat, axis=0), jnp.sum(lead_grad, axis=0)])
    return loss_rows, norm_back(lead_grad * gain[None], lead_hat, inv2[:, :1]), sums


def down_grad_kernel(seq_len, fresh, place, *refs):
    step = pl.program_id(0)
    if fresh:
        old_ref, leads_ref, fix_ref, act_ref, *outs, db_ref, sum_ref = refs

        @pl.when(step == 0)
        def _():
            db_ref[...] = old_ref[...]
            fixed = (leads_ref[...] + fix_ref[...]).astype(low)
            sum_ref[...] = columns_sum(fixed.astype(full) - leads_ref[...].astype(low).astype(full))
            for s in range(fix_ref.shape[0]):
                block = old_ref[s * seq_len : s * seq_len + 16, :]
                first = lax.broadcasted_iota(jnp.int32, block.shape, 0) == 0
                block = jnp.where(first, fixed[s : s + 1, :].astype(full), block.astype(full))
                db_ref[s * seq_len : s * seq_len + 16, :] = block.astype(low)
    else:
        db_ref, act_ref, *outs = refs
    grad = t_dot(act_ref[...], db_ref[...]).astype(low)
    tall = grad.shape[0]
    for rank in range(4):

        @pl.when(step == rank)
        def _(rank=rank):
            outs[rank // 2][rank % 2 * tall : (rank % 2 + 1) * tall, :] = grad


def down_gradient(place, first, act, dbranch, leads=None, fix=None, seq_len=None):
    count, hidden = act.shape
    tall = hidden // 8
    fresh = fix is not None
    operands = [dbranch] + ([leads, fix] if fresh else []) + [in_far(act)]
    moving = pl.BlockSpec((count, tall), lambda p, place: (0, place[first + p]))
    in_specs = [fixed_spec(*operand.shape) for operand in operands[:-1]] + [moving]
    out_specs = [fixed_spec(2 * tall, D)] * 2
    out_shape = [pltpu.VMEM((2 * tall, D), low)] * 2
    if fresh:
        out_specs += [fixed_spec(count, D), fixed_spec(1, D)]
        out_shape += [shape_of(count, D), shape_of(1, D, dtype=full)]
    return pl.pallas_call(
        functools.partial(down_grad_kernel, seq_len, fresh),
        grid_spec=pltpu.PrefetchScalarGridSpec(
            num_scalar_prefetch=1, grid=(4,), in_specs=in_specs, out_specs=out_specs
        ),
        out_shape=out_shape,
        compiler_params=params(1),
        name=f"down_grad_{first}",
        cost_estimate=cost(4),
    )(place, *operands)


def put_rows(place, grad_ref, outs, columns):
    tall = grad_ref.shape[0] // 8
    for rank in range(8):
        at = pl.multiple_of(place[rank] * tall, 16)
        outs[rank // 2][rank % 2 * tall : (rank % 2 + 1) * tall, columns] = grad_ref[pl.ds(at, tall), :]


def hidden_kernel(place, db_ref, slope_ref, dw, nl_ref, dpre_ref, sum_ref, *rest):
    *outs, scratch = rest
    dpre = (dot_t(db_ref[...], dw[...]) * slope_ref[...].astype(full)).astype(low)
    dpre_ref[...] = dpre
    sum_ref[0:1, :] = columns_sum(dpre.astype(full))
    scratch[...] = t_dot(nl_ref[...], dpre).astype(low)
    put_rows(place, scratch, outs, slice(None))


def hidden_gradient(place, dbranch, slope, dw, nl):
    count, hidden = slope.shape
    wide = pl.BlockSpec((count, D), lambda j, *_: (0, j))
    pair = D // 4
    return pl.pallas_call(
        hidden_kernel,
        grid_spec=pltpu.PrefetchScalarGridSpec(
            num_scalar_prefetch=1,
            grid=(hidden // D,),
            in_specs=[fixed_spec(count, D), wide, pl.BlockSpec((D, D), lambda j, *_: (j, 0)), fixed_spec(count, D)],
            out_specs=[wide] + [pl.BlockSpec((rows, D), lambda j, *_: (0, j)) for rows in (8, pair, pair, pair, pair)],
            scratch_shapes=[pltpu.VMEM((D, D), low)],
        ),
        out_shape=[far(count, hidden), shape_of(8, hidden, dtype=full)] + [shape_of(pair, hidden)] * 4,
        input_output_aliases={2: 0},
        compiler_params=params(1, 18),
        name="hidden_gradient",
        cost_estimate=cost(15),
    )(place, dbranch, in_far(slope), dw, in_far(nl))


def norm_one_kernel(dpre_ref, uw, gain1, wo_far, branch_far, hat_far, inv_far,
                    datt_ref, dctx_ref, sums_ref, acc, wo, branch_ref, hat_ref, inv_ref, sems):
    step = pl.program_id(0)
    copies = [
        pltpu.make_async_copy(source, target, sems.at[k])
        for k, (source, target) in enumerate(((wo_far, wo), (branch_far, branch_ref), (hat_far, hat_ref), (inv_far, inv_ref)))
    ]

    @pl.when(step == 0)
    def _():
        for copy in copies:
            copy.start()
        acc[...] = jnp.zeros_like(acc)

    acc[...] += dot_t(dpre_ref[...], uw[...])

    @pl.when(step == pl.num_programs(0) - 1)
    def _():
        for copy in copies:
            copy.wait()
        gain = line(gain1)
        totals = [jnp.zeros((1, D), full)] * 3
        for start in range(0, acc.shape[0], 256):
            rows = slice(start, start + 256)
            grad, hat = acc[rows, :] + branch_ref[rows, :].astype(full), hat_ref[rows, :]
            dr1 = norm_back(grad * gain, hat, inv_ref[rows, 0:1])
            datt = dr1.astype(low)
            datt_ref[0, rows, :] = datt
            dctx_ref[rows, :] = dot_t(datt, wo[...]).astype(low)
            totals = [
                total + columns_sum(part) for total, part in zip(totals, (grad * hat, grad, datt.astype(full)), strict=True)
            ]
        for rank, total in enumerate(totals):
            sums_ref[rank : rank + 1, :] = total


def norm_one_backward(dpre, dbranch, hat, inv, uw, wo, gain1):
    count, hidden = dpre.shape
    anywhere = pl.BlockSpec(memory_space=pl.ANY)
    return pl.pallas_call(
        norm_one_kernel,
        grid=(hidden // D,),
        in_specs=[
            pl.BlockSpec((count, D), lambda j: (0, j)), pl.BlockSpec((D, D), lambda j: (0, j)), vector_spec(), anywhere, anywhere, anywhere, anywhere,
        ],
        out_specs=[pl.BlockSpec((1, count, D), lambda j: (3, 0, 0)), fixed_spec(count, D), fixed_spec(8, D)],
        out_shape=[near(4, count, D), near(count, D), shape_of(8, D, dtype=full)],
        scratch_shapes=[
            pltpu.VMEM((count, D), full), pltpu.VMEM((D, D), low), pltpu.VMEM((count, D), low),
            pltpu.VMEM((count, D), full), pltpu.VMEM((count, LANES), full), pltpu.SemaphoreType.DMA((4,)),
        ],
        compiler_params=params(1, 24),
        name="norm_one_backward",
        cost_estimate=cost(13),
    )(in_far(dpre), uw, gain1, wo, dbranch, in_far(hat), in_far(inv))


def attention_back_kernel(seq_len, q_ref, k_ref, v_ref, p_ref, dc_ref, stack_ref, d_ref, sums):
    count = q_ref.shape[0]
    factor = 1.0 / math.sqrt(HD)

    @pl.when(pl.program_id(0) == 0)
    def _():
        sums[...] = jnp.zeros_like(sums)

    wide = 2 * 2 * HD

    @pl.loop(0, D // wide)
    def _(turn):
        lanes = pl.ds(pl.multiple_of(turn * wide, LANES), wide)
        q, k, v, probs, dctx = (ref[:, lanes] for ref in (q_ref, k_ref, v_ref, p_ref, dc_ref))
        cells = [
            (slice(start, start + seq_len), slice(first, first + 2 * HD))
            for first in range(0, wide, 2 * HD)
            for start in range(0, count, seq_len)
        ]
        spread_dctx = [two_heads(dctx[cell]) for cell in cells]
        dprobs = [dot_t(v[cell], both) for cell, both in zip(cells, spread_dctx, strict=True)]
        dvals = [dot(probs[cell], both).astype(low) for cell, both in zip(cells, spread_dctx, strict=True)]
        dscores = []
        for cell, dprob in zip(cells, dprobs, strict=True):
            prob = probs[cell].astype(full)
            dscores.append((prob * (dprob - columns_sum(prob * dprob))).astype(low))
        dkeys = [(dot(ds, two_heads(q[cell])) * factor).astype(low) for cell, ds in zip(cells, dscores, strict=True)]
        dqueries = [
            (own_head(t_dot(ds, k[cell])) * factor).astype(low) for cell, ds in zip(cells, dscores, strict=True)
        ]
        for rank, pieces in enumerate((dqueries, dkeys, dvals)):
            grad = joined(pieces, count, seq_len)
            d_ref[rank, :, lanes] = grad
            sums[rank : rank + 1, lanes] += columns_sum(grad.astype(full))


def attention_backward(seq_len, q, k, v, probs, dctx, stack):
    count = q.shape[0]
    rows = 256
    row = pl.BlockSpec((rows, D), lambda i: (i, 0))
    return pl.pallas_call(
        functools.partial(attention_back_kernel, seq_len),
        grid=(count // rows,),
        in_specs=[row] * 5 + [pl.BlockSpec(memory_space=pl.ANY)],
        out_specs=[pl.BlockSpec((3, rows, D), lambda i: (0, i, 0)), fixed_spec(8, D)],
        out_shape=[near(4, count, D), shape_of(8, D, dtype=full)],
        input_output_aliases={5: 0},
        compiler_params=params(1, 14),
        name="attention_backward",
        cost_estimate=cost(8),
    )(*map(in_near, (q, k, v, probs, dctx, stack)))


def square_grad_kernel(late, place, left_ref, d_ref, *rest):
    step = pl.program_id(0)
    if late:
        far_ref, *outs, scratch, late_ref, sem = rest
        copy = pltpu.make_async_copy(far_ref, late_ref, sem)

        @pl.when(step == 0)
        def _():
            copy.start()
            scratch[...] = t_dot(left_ref[...], d_ref[0]).astype(low)

        @pl.when(step == 1)
        def _():
            copy.wait()
            scratch[...] = t_dot(late_ref[...], d_ref[0]).astype(low)
    else:
        small_ref, *outs, scratch = rest
        scratch[...] = t_dot(left_ref[...], d_ref[0]).astype(low)

        @pl.when(step == 0)
        def _():
            tall = D // 8
            for rank in range(8):
                out_ref, first = outs[rank // 2], rank % 2 * tall
                out_ref[first : first + tall, 2 * D :] = jnp.zeros((tall, LANES), low)

                @pl.when(place[rank] == 0)
                def _(out_ref=out_ref, first=first):
                    out_ref[first : first + small_ref.shape[0], 2 * D :] = small_ref[...].astype(low)

    put_rows(place, scratch, outs, pl.ds(pl.multiple_of(step * D, LANES), D))


def square_gradient(place, lefts, stack, slots, small, name):
    count = lefts[0].shape[0]
    late = len(lefts) == 2
    pair, columns = D // 4, 2 * D + (0 if late else LANES)
    scratch = [pltpu.VMEM((D, D), low)]
    if late:
        scratch += [pltpu.VMEM((count, D), low), pltpu.SemaphoreType.DMA]
    return pl.pallas_call(
        functools.partial(square_grad_kernel, late),
        grid_spec=pltpu.PrefetchScalarGridSpec(
            num_scalar_prefetch=1,
            grid=(2,),
            in_specs=[
                fixed_spec(count, D),
                pl.BlockSpec((1, count, D), lambda j, *_: (slots[0] + j * (slots[1] - slots[0]), 0, 0)),
                pl.BlockSpec(memory_space=pl.ANY) if late else fixed_spec(*small.shape),
            ],
            out_specs=[fixed_spec(pair, columns)] * 4,
            scratch_shapes=scratch,
        ),
        out_shape=[shape_of(pair, columns)] * 4,
        compiler_params=params(1, 18),
        name=name,
        cost_estimate=cost(6),
    )(place, in_far(lefts[0]), in_near(stack), in_far(lefts[1]) if late else small)


def input_grad_kernel(d_ref, wq, wk, wv, out_ref):
    out_ref[...] = (
        d_ref[3].astype(full) + dot_t(d_ref[0], wq[...]) + dot_t(d_ref[1], wk[...]) + dot_t(d_ref[2], wv[...])
    )


def input_gradient(stack, wq, wk, wv):
    count = stack.shape[1]
    rows = 256
    mat = fixed_spec(D, D)
    return pl.pallas_call(
        input_grad_kernel,
        grid=(count // rows,),
        in_specs=[pl.BlockSpec((4, rows, D), lambda i: (0, i, 0))] + [mat] * 3,
        out_specs=pl.BlockSpec((rows, D), lambda i: (i, 0)),
        out_shape=far(count, D, dtype=full),
        compiler_params=params(1),
        name="input_gradient",
        cost_estimate=cost(6),
    )(in_near(stack), wq, wk, wv)


def spread_kernel(widths, talls, first, place, *refs):
    smalls = refs[len(refs) - len(talls) :]
    outs = refs[len(refs) - len(talls) - len(widths) : len(refs) - len(talls)]
    tall = outs[0].shape[0]
    held = refs[0].shape[0] // tall
    if first and talls:

        @pl.when(pl.program_id(0) == 0)
        def _():
            for ref, old in zip(smalls, refs[4 // held : 4 // held + len(talls)], strict=True):
                ref[...] = old[...]

    for rank in range(4):

        @pl.when(pl.program_id(0) == rank)
        def _(rank=rank):
            source, rows = refs[rank // held], rank % held * tall
            at = 0
            for ref, width in zip(outs, widths, strict=True):
                ref[...] = source[rows : rows + tall, at : at + width].astype(full)
                at += width
            if talls:

                @pl.when(place[first + rank] == 0)
                def _():
                    top = rows
                    for ref in smalls:
                        ref[...] = source[top : top + ref.shape[0], at:].astype(full)
                        top += ref.shape[0]


def spread(place, first, pairs, widths, talls, carried, name):
    tall = sum(pair.shape[0] for pair in pairs) // 4
    carried = list(carried or [])
    small = [fixed_spec(rows, LANES) for rows in talls]
    in_specs = [fixed_spec(*pair.shape) for pair in pairs]
    operands = list(pairs)
    if carried:
        operands += carried[len(widths) :] + carried[: len(widths)]
        in_specs += small + [pl.BlockSpec(memory_space=pl.ANY)] * len(widths)
    return pl.pallas_call(
        functools.partial(spread_kernel, widths, talls, first),
        grid_spec=pltpu.PrefetchScalarGridSpec(
            num_scalar_prefetch=1,
            grid=(4,),
            in_specs=in_specs,
            out_specs=[pl.BlockSpec((tall, width), lambda p, place: (place[first + p], 0)) for width in widths] + small,
        ),
        out_shape=[far(8 * tall, width, dtype=full) for width in widths]
        + [shape_of(rows, LANES, dtype=full) for rows in talls],
        input_output_aliases={1 + len(operands) - len(widths) + k: k for k in range(len(widths))} if carried else {},
        compiler_params=params(1),
        name=f"{name}_spread_{first}",
        cost_estimate=cost(3),
    )(place, *operands)


def places():
    half = lax.axis_index("stream")
    chip = lax.axis_index("dp")
    bits = (chip & 1, (chip >> 1) & 1)
    table = []
    for side in (half, 1 - half):
        first = jnp.where(side == 0, bits[0], bits[1])
        second = jnp.where(side == 0, bits[1], bits[0])
        table += [4 * side + 2 * (first ^ (k >> 1)) + (second ^ (k & 1)) for k in range(4)]
    return jnp.stack(table).astype(jnp.int32)


def chip_partner(bit_zero, bit_one):
    chips = lax.axis_size("dp")
    return [
        (half * chips + chip, half * chips + (chip ^ (bit_zero if half == 0 else bit_one)))
        for half in range(2)
        for chip in range(chips)
    ]


def core_partner():
    chips = lax.axis_size("dp")
    return [(half * chips + chip, (1 - half) * chips + chip) for half in range(2) for chip in range(chips)]


def swap(piece, pairs):
    return lax.ppermute(piece, ("stream", "dp"), pairs)


def add_low(left, right):
    return (left.astype(full) + right.astype(full)).astype(low)


def tie(value, after):
    return value if after is None else lax.optimization_barrier((value, after))[0]


def all_sum(sent):
    others = [swap(pair, core_partner()) for pair in sent]
    kept = yield sent
    pair = add_low(kept[1], others[1])
    other = swap(pair, chip_partner(1, 2))
    mine = add_low(kept[0], others[0])
    after = yield pair, mine
    tall = mine.shape[0] // 2
    mine = tie(mine, after)
    block = add_low(mine[tall:], other[tall:])
    mine = add_low(mine[:tall], other[:tall])
    other = swap(block, chip_partner(2, 1))
    after = yield block, mine
    bits = [1 << k for k in range(2, lax.axis_size("dp").bit_length() - 1)]
    for rank, pair in enumerate(zip(bits, bits[::-1], strict=True)):
        mine = add_low(tie(mine, after), other)
        other = swap(mine, chip_partner(*pair))
        after = (yield mine) if rank in (0, len(bits) - 1) else None
    mine = add_low(tie(mine, after), other)
    other = swap(mine, chip_partner(2, 1))
    after = yield mine
    pair = jnp.concatenate([tie(mine, after), other])
    other = swap(pair, chip_partner(1, 2))
    after = yield pair
    pairs = [tie(pair, after), other]
    others = [swap(each, core_partner()) for each in pairs]
    yield pairs
    yield others


def gather_rows(rows):
    chips = lax.axis_size("dp")
    bit = 1
    after = None
    while bit < chips:
        others = [swap(rows, chip_partner(k * bit, k * bit)) for k in range(1, 4) if k * bit < chips]
        after = yield rows
        rows = jnp.concatenate([tie(rows, after)] + others)
        bit *= 4
    other = swap(rows, core_partner())
    yield rows
    yield rows, other


def in_far(array):
    return pltpu.with_memory_space_constraint(array, pltpu.HBM)


def in_near(array):
    return pltpu.with_memory_space_constraint(array, pltpu.VMEM)


def shards(
    layer_input, pair_group, query_weight, query_bias, key_weight, value_weight, value_bias,
    out_weight, out_bias, mixer_gain, mixer_shift, up_weight, up_bias, down_weight, down_bias,
    final_gain, final_shift, upstream,
):
    count = layer_input.shape[1]
    seq_count = pair_group.shape[0]
    seq_len = count // seq_count
    hidden = up_bias.shape[0]
    tokens, upstream = in_far(layer_input[0]), in_far(upstream[0])
    wq, wk, wv, wo = map(in_far, (query_weight, key_weight, value_weight, out_weight))
    uw, dw = in_near(up_weight), in_near(down_weight)
    fold = lambda vector: in_far(vector.reshape(-1, LANES))
    bq, bv, bo, g1, s1 = map(fold, (query_bias, value_bias, out_bias, mixer_gain, mixer_shift))
    ub, db, g2, s2 = map(fold, (up_bias, down_bias, final_gain, final_shift))
    place = places()

    q, k, v, probs, context, nl, hat, inv, lead_nl, lead_hat = attention_forward(
        tokens, seq_len, wq, wk, wv, wo, bq, bv, bo, g1, s1
    )
    lead, lead_hat, lead_inv2, lead_inv, units = lead_forward(lead_nl, lead_hat, uw, ub, dw, g1, s1, db, g2, s2)
    ids = jnp.broadcast_to(pair_group.astype(low)[:, None], (seq_count, LANES))
    hops = gather_rows(jnp.concatenate([units, ids], axis=1))
    sent = next(hops)
    parts = 2
    carried = None
    for part in range(parts):
        carried = ff_forward(
            part, parts, carried, seq_len, tie(nl, sent), hat, upstream, uw, ub, dw, g1, s1, db, g2, s2
        )
        sent = hops.send(carried[4])
    while not isinstance(sent, tuple):
        sent = hops.send(None)
    layer_output, act, slope, dbranch, final_sums, dr2_leads = carried
    loss_rows, fix, lead_sums = pair_loss(*sent, lead, lead_hat, lead_inv2, lead_inv, final_gain)

    *down_blocks, dbranch, down_sum = down_gradient(place, 4, act, dbranch, dr2_leads.reshape(-1, D), fix, seq_len)
    sent = down_blocks
    talls = [hidden // LANES] + [D // LANES] * 8
    down = all_sum(down_blocks)
    next(down)
    sent = (sent, down_blocks)
    down_kept = down_gradient(place, 0, act, tie(dbranch, sent))
    sent = down_kept
    sent = down.send(tie(down_kept, sent))
    dpre, up_sums, *up_blocks = hidden_gradient(place, tie(dbranch, sent), slope, in_far(down_weight), nl)
    sent = dpre
    sent = down.send(sent)
    up = all_sum(up_blocks[2:])
    next(up)
    sent = (sent, up_blocks[2:])
    stack, dctx, mixer = norm_one_backward(tie(dpre, sent), dbranch, hat, inv, in_far(up_weight), wo, g1)
    sent = dctx
    sent = down.send(sent)
    sent = up.send(tie(up_blocks[:2], sent))
    stack, qkv = attention_backward(seq_len, q, k, v, probs, tie(dctx, sent), stack)
    sent = stack
    value_blocks = square_gradient(place, [context, tokens], tie(stack, sent), (3, 2), None, "value_gradient")
    sent = value_blocks[2]
    sent = down.send(sent)
    value = all_sum(value_blocks[2:])
    next(value)
    sent = (sent, value_blocks[2:])
    sent = up.send(sent)
    final = jnp.sum(final_sums, axis=0)
    small = jnp.concatenate(
        [
            up_sums[0], mixer[2], mixer[0], mixer[1], final[2] + down_sum[0], final[0] + lead_sums[0],
            final[1] + lead_sums[1], qkv[0], qkv[2],
        ]
    ).reshape(-1, LANES)
    query_blocks = square_gradient(place, [tokens], tie(stack, sent), (0, 1), small, "query_gradient")
    sent = query_blocks[2]
    sent = value.send(tie(value_blocks[:2], sent))
    sent = up.send(sent)
    query = all_sum(query_blocks[2:])
    next(query)
    sent = (sent, query_blocks[2:])
    sent = down.send(sent)
    sent = query.send(tie(query_blocks[:2], sent))
    sent = value.send(sent)
    sent = up.send(sent)
    sent = down.send(sent)
    input_grad = input_gradient(tie(stack, sent), wq, wk, wv)
    sent = input_grad
    sent = value.send(sent)
    sent = query.send(sent)
    sent = up.send(sent)
    down_own = down.send(sent)
    sent = down_own
    sent = value.send(sent)
    sent = query.send(sent)
    sent = up.send(sent)
    down_out = spread(place, 0, tie(down_own, sent), [D], [], None, "down")
    sent = down_out
    sent = query.send(sent)
    sent = value.send(sent)
    sent = query.send(sent)
    down_out = spread(place, 4, down.send(sent), [D], [], down_out, "down")
    sent = down_out
    up_own = up.send(sent)
    sent = up_own
    sent = value.send(sent)
    up_out = spread(place, 0, tie(up_own, sent), [hidden], [], None, "up")
    sent = up_out
    sent = query.send(sent)
    up_out = spread(place, 4, up.send(sent), [hidden], [], up_out, "up")
    sent = up_out
    value_own = value.send(sent)
    sent = value_own
    value_out = spread(place, 0, tie(value_own, sent), [D] * 2, [], None, "value")
    sent = value_out
    value_out = spread(place, 4, value.send(sent), [D] * 2, [], value_out, "value")
    sent = value_out
    query_own = query.send(sent)
    sent = query_own
    query_out = spread(place, 0, tie(query_own, sent), [D] * 2, talls, None, "query")
    sent = query_out
    query_out = spread(place, 4, query.send(sent), [D] * 2, talls, query_out, "query")
    sent = query_out
    wq_grad, wk_grad, *smalls = query_out
    up_b, out_b, gain_one, shift_one, down_b, gain_two, shift_two, query_b, value_b = (each.reshape(-1) for each in smalls)
    return (
        layer_output[None], input_grad[None], loss_rows,
        wq_grad, query_b, wk_grad, value_out[1], value_b, value_out[0], out_b,
        gain_one, shift_one, up_out[0], up_b, down_out[0], down_b, gain_two, shift_two,
    )


def solution(mesh):
    split = P("stream", "dp", None)
    return jax.shard_map(
        shards,
        mesh=mesh,
        in_specs=(split, P("dp")) + (P(),) * 15 + (split,),
        out_specs=(split, split, P("stream", "dp")) + (P(),) * 15,
        check_vma=False,
    )
```
